128 devices in a mesh: basin: 32 (over z, x, core), tm: 4 (over y).
Axes of the slice: x: 4, y: 4, z: 4, core: 2. Of those that a mesh axis runs over, the one named last changes fastest.
Arguments:
- incidence: int32 [1024, 16, 128], P('basin'), may hold values 0 or 1
- row_gauge: int32 [16384], P('basin'), may hold values from 0 to 8191, as said below
- gauge_kernel: int32 [8192], P('basin'), may hold values from 0 to 31
- kernels: float32 [32, 128], replicated, may hold values from 0 to 0.0156
- observed: float32 [8192, 512], P('basin', 'tm'), may hold values from -8 to 8
- first_guess: float32 [131072, 512], P('basin', 'tm'), may hold values from -4 to 4
Outputs:
- inflows: float32 [131072, 512], P('basin', 'tm')
The draws below stay inside these ranges and needn't reach their ends.
Inputs may be any that keep to these rules, and one draw needn't show every extreme that they name: `row_gauge`: the 512 slots of one index of basin name gauges of any one owner (gauges o * 256 to o * 256 + 255 belong to owner o) at most 32 times; in every draw one owner is named exactly 32 times by the slots of every index of basin.
All inputs are finite; a program needn't handle non-finite values. No bound on the sum of `incidence` on one device may be relied on, other than what follows from the above.
Results may differ from the reference program's by a relative error of at most 0.0001.
Values sent between devices are 32-bit elements; how exact they have to be, the bound alone decides.
A program may use at most 128 MiB of HBM per device.

```python
import jax
import jax.numpy as jnp
from jax import lax

BLK = 128
BSLOT = 16
RB = 32
G_DEV = 256
TAPS = 128
NK = 32
ITERS = 3
BLOCKS = 1024
REACHES = 131072
GAUGES = 8192
HOURS = 512
CAP = 32
N_BASIN = 32


def draw_row_gauge(key, part):
    rows = RB * BSLOT
    key_busy, key_shift, key_perm, key_local = jax.random.split(jax.random.fold_in(key, 11), 4)
    busy = jax.random.randint(key_busy, (), 0, N_BASIN)
    index = jnp.arange(rows, dtype=jnp.int32)[None, :]
    offset = jax.random.randint(key_shift, (N_BASIN, 1), 0, N_BASIN - 1)
    other = (index - CAP + offset) % (N_BASIN - 1)
    other = other + (other >= busy).astype(jnp.int32)
    owner = jnp.where(index < CAP, busy, other).astype(jnp.int32)
    orders = jax.vmap(lambda sub: jax.random.permutation(sub, rows))(jax.random.split(key_perm, N_BASIN))
    owner = jnp.take_along_axis(owner, orders.astype(jnp.int32), axis=1).reshape(-1)
    local = jax.random.randint(key_local, (N_BASIN * rows,), 0, G_DEV)
    lowest = jnp.argmin(owner)
    highest = jnp.argmax(owner)
    local = local.at[lowest].set(0)
    local = local.at[highest].set(G_DEV - 1)
    return (owner * G_DEV + local).astype(jnp.int32)


def draw_observed(key, part):
    key_base, key_hour = jax.random.split(jax.random.fold_in(key, 23), 2)
    rows = jnp.arange(GAUGES, dtype=jnp.float32)[:, None] / GAUGES
    ramp = jnp.exp(2.302585 * rows)
    hour_scale = jnp.exp(2.302585 * jax.random.uniform(key_hour, (1, HOURS), jnp.float32))
    base = jnp.clip(jax.random.normal(key_base, (GAUGES, HOURS), jnp.float32), -4.0, 4.0)
    return (0.02 * base * ramp * hour_scale).astype(jnp.float32)


def plant(drawn, stream_key, low, top_value):
    longest = drawn.shape.index(max(drawn.shape))
    spots = []
    for shift in (0, 1):
        where = [jax.random.randint(jax.random.fold_in(stream_key, axis), (), 0, length) for axis, length in enumerate(drawn.shape)]
        where[longest] = (where[longest] + shift) % drawn.shape[longest]
        spots.append(tuple(where))
    return drawn.at[spots[0]].set(low).at[spots[1]].set(top_value)


def block_levels(own_key, extent, shards, smallest, high):
    gain, own = 1.0, jax.random.fold_in(own_key, 6)
    for position, blocks in shards:
        steps = jnp.exp(jax.random.uniform(jax.random.fold_in(own, position), (blocks,), jnp.float32, smallest / len(shards), high / len(shards)))
        gain = gain * jnp.repeat(steps, extent[position] // blocks).reshape([-1 if axis == position else 1 for axis in range(len(extent))])
    return gain


def gaussian(stream_key, shape, scale, limit, shards=(), kind=jnp.bfloat16):
    result = jax.random.normal(stream_key, shape, jnp.float32) * scale
    if len(shards) > 0:
        result = block_levels(stream_key, shape, shards, -0.22, 0.18) * result
    return jnp.clip(result, min=-limit, max=limit).astype(kind)


def setup_inputs(seed: int = 0) -> dict:
    key_list = jax.random.split(jax.random.key(seed), 7)
    return {
        "incidence": plant((jax.random.randint(key_list[0], (BLOCKS, BSLOT, BLK), 0, 2) < 1).astype(jnp.int32), jax.random.fold_in(key_list[0], 1), 0, 1),
        "row_gauge": draw_row_gauge(jax.random.fold_in(key_list[6], 71), 0),
        "gauge_kernel": plant(jax.random.randint(key_list[2], (GAUGES,), 0, NK), jax.random.fold_in(key_list[2], 1), 0, NK - 1).astype(jnp.int32),
        "kernels": jnp.clip(jax.random.uniform(key_list[3], (NK, TAPS), jnp.float32, 0.0, 0.0156), 0.0, 0.0156),
        "observed": draw_observed(jax.random.fold_in(key_list[6], 71), 0),
        "first_guess": gaussian(key_list[5], (REACHES, HOURS), 0.3, 4.0, ((0, 32), (1, 4)), jnp.float32),
    }


HIGH = lax.Precision.HIGHEST

def subtree(field, incidence):
    blocks = incidence.shape[0]
    weights = incidence.astype(jnp.float32)
    shaped = field.reshape(blocks, BLK, HOURS)
    return jnp.einsum('bjr,brt->bjt', weights, shaped, precision=HIGH).reshape(blocks * BSLOT, HOURS)

def spread_rows(rows, incidence):
    blocks = incidence.shape[0]
    weights = incidence.astype(jnp.float32)
    shaped = rows.reshape(blocks, BSLOT, HOURS)
    return jnp.einsum('bjr,bjt->brt', weights, shaped, precision=HIGH).reshape(blocks * BLK, HOURS)

def delay(series, taps_of):
    padded = jnp.pad(series, ((0, 0), (TAPS - 1, 0)))

    def step(tau, total):
        piece = lax.dynamic_slice_in_dim(padded, TAPS - 1 - tau, HOURS, 1)
        weight = lax.dynamic_slice_in_dim(taps_of, tau, 1, 1)
        return total + weight * piece
    return lax.fori_loop(0, TAPS, step, jnp.zeros(series.shape, jnp.float32))

def advance(series, taps_of):
    padded = jnp.pad(series, ((0, 0), (0, TAPS - 1)))

    def step(tau, total):
        piece = lax.dynamic_slice_in_dim(padded, tau, HOURS, 1)
        weight = lax.dynamic_slice_in_dim(taps_of, tau, 1, 1)
        return total + weight * piece
    return lax.fori_loop(0, TAPS, step, jnp.zeros(series.shape, jnp.float32))

def norm_of(values):
    return jnp.sqrt(jnp.sum(values * values))

def reference(incidence, row_gauge, gauge_kernel, kernels, observed, first_guess):
    taps_of = kernels[gauge_kernel]

    def forward(field):
        partial_value = subtree(field, incidence)
        sums = jnp.zeros((GAUGES, HOURS), jnp.float32).at[row_gauge].add(partial_value)
        return delay(sums, taps_of)

    def backward(series):
        upstream = advance(series, taps_of)
        return spread_rows(upstream[row_gauge], incidence)
    start = observed - forward(first_guess)
    beta = norm_of(start)
    u = start / beta
    pulled = backward(u)
    alpha = norm_of(pulled)
    v = pulled / alpha
    w = v
    correction = jnp.zeros(first_guess.shape, jnp.float32)
    phibar = beta
    rhobar = alpha
    for step in range(ITERS):
        p = forward(v) - alpha * u
        beta = norm_of(p)
        u = p / beta
        rho = jnp.sqrt(rhobar * rhobar + beta * beta)
        cosine = rhobar / rho
        sine = beta / rho
        phi = cosine * phibar
        phibar = sine * phibar
        correction = correction + phi / rho * w
        if step < ITERS - 1:
            pulled = backward(u) - beta * v
            alpha = norm_of(pulled)
            v = pulled / alpha
            theta = sine * alpha
            rhobar = -cosine * alpha
            w = v - theta / rho * w
    return first_guess + correction
```

```python
import functools

import jax
import jax.numpy as jnp
from jax import lax
from jax.experimental import pallas as pl
from jax.experimental.pallas import tpu as pltpu
from jax.sharding import PartitionSpec as P

ITERS = 3
CAP = 32
LANES = 128

HIGH = lax.Precision.HIGHEST
MESH = pl.DeviceIdType.MESH


def from_behind(x, axis, by):
    devices = lax.axis_size(axis)
    pairs = [(i, i + by) for i in range(devices) if 0 <= i + by < devices]
    return lax.ppermute(x, axis, pairs)


def lag_table(kernels, lag):
    classes, taps = kernels.shape
    rows, hours = lag.shape
    onehot = (lag[None, :, :] == jnp.arange(taps)[:, None, None]).astype(jnp.float32)
    picked = jnp.dot(kernels, onehot.reshape(taps, rows * hours), precision=HIGH)
    picked = picked.reshape(classes, rows, hours)
    return jnp.transpose(picked, (1, 0, 2)).reshape(rows, classes * hours)


def class_mix(extended, table, selector):
    gauges = extended.shape[0]
    classes = selector.shape[1]
    spread = jnp.dot(extended, table, precision=HIGH).reshape(gauges, classes, -1)
    return jnp.sum(spread * selector[:, :, None], axis=1)


def squared(values):
    return jnp.sum(values * values)


def _allreduce_body(x_ref, o_ref, buf, own_sem, send_sem, recv_sem, *, nb, nt, rounds):
    me = lax.axis_index("basin") * nt + lax.axis_index("tm")

    def peer(r):
        step = 1 << r
        bit = (me // step) % 2
        other = me + step - 2 * step * bit
        return (other // nt, other % nt)

    barrier = pltpu.get_barrier_semaphore()
    for r in range(rounds):
        pl.semaphore_signal(barrier, inc=1, device_id=peer(r), device_id_type=MESH)
    pl.semaphore_wait(barrier, rounds)

    own = pltpu.make_async_copy(x_ref, buf.at[pl.ds(me, 1)], own_sem)
    own.start()
    own.wait()
    for r in range(rounds):
        step = 1 << r
        base = (me // step) * step
        copy = pltpu.make_async_remote_copy(
            src_ref=buf.at[pl.ds(base, step)],
            dst_ref=buf.at[pl.ds(base, step)],
            send_sem=send_sem.at[r],
            recv_sem=recv_sem.at[r],
            device_id=peer(r),
            device_id_type=MESH,
        )
        copy.start()
        copy.wait()
    o_ref[...] = jnp.sum(buf[...], axis=0, keepdims=True)


def global_total(value):
    nb = lax.axis_size("basin")
    nt = lax.axis_size("tm")
    n = nb * nt
    rounds = n.bit_length() - 1
    if n != (1 << rounds) or n < 2:
        return lax.psum(value, ("basin", "tm"))
    x = jnp.broadcast_to(value.astype(jnp.float32), (1, LANES))
    out = pl.pallas_call(
        functools.partial(_allreduce_body, nb=nb, nt=nt, rounds=rounds),
        out_shape=jax.ShapeDtypeStruct((1, LANES), jnp.float32),
        in_specs=[pl.BlockSpec(memory_space=pltpu.VMEM)],
        out_specs=pl.BlockSpec(memory_space=pltpu.VMEM),
        scratch_shapes=[
            pltpu.VMEM((n, LANES), jnp.float32),
            pltpu.SemaphoreType.DMA(()),
            pltpu.SemaphoreType.DMA((rounds,)),
            pltpu.SemaphoreType.DMA((rounds,)),
        ],
        compiler_params=pltpu.CompilerParams(collective_id=0, has_side_effects=True),
    )(x)
    return out[0, 0]


def shards(incidence, row_gauge, gauge_kernel, kernels, observed, first_guess):
    weights = incidence.astype(jnp.float32)
    blocks, slots, width = weights.shape
    gauges_here, hours = observed.shape
    owners = lax.axis_size("basin")
    classes = kernels.shape[0]
    partials = blocks * slots
    outer = jnp.arange(2 * hours)[:, None]
    inner = jnp.arange(hours)[None, :]
    table_fwd = lag_table(kernels, inner + hours - outer)
    table_bwd = lag_table(kernels, outer - inner)
    selector = (gauge_kernel[:, None] == jnp.arange(classes)[None, :]).astype(jnp.float32)

    owner = row_gauge // gauges_here
    local = row_gauge % gauges_here
    hit = owner[:, None] == jnp.arange(owners)[None, :]
    rank = jnp.cumsum(hit.astype(jnp.int32), axis=0) - 1
    dest = owner * CAP + jnp.sum(jnp.where(hit, rank, 0), axis=1)
    entries = owners * CAP
    place = (jnp.arange(entries)[:, None] == dest[None, :]).astype(jnp.float32)
    sent_ids = jnp.full((entries,), -1, jnp.int32).at[dest].set(local)
    got_ids = lax.all_to_all(sent_ids, "basin", 0, 0, tiled=True)
    gather = (jnp.arange(gauges_here)[:, None] == got_ids[None, :]).astype(jnp.float32)

    def to_gauges(partial_value):
        outgoing = jnp.dot(place, partial_value, precision=HIGH)
        incoming = lax.all_to_all(outgoing, "basin", 0, 0, tiled=True)
        return jnp.dot(gather, incoming, precision=HIGH)

    def from_gauges(upstream):
        outgoing = jnp.dot(gather.T, upstream, precision=HIGH)
        incoming = lax.all_to_all(outgoing, "basin", 0, 0, tiled=True)
        return jnp.dot(place.T, incoming, precision=HIGH)

    def forward(field):
        partial_value = jnp.einsum(
            "bjr,brt->bjt", weights, field.reshape(blocks, width, hours), precision=HIGH
        )
        sums = to_gauges(partial_value.reshape(partials, hours))
        earlier = from_behind(sums, "tm", 1)
        return class_mix(jnp.concatenate([earlier, sums], axis=1), table_fwd, selector)

    def backward(series):
        later = from_behind(series, "tm", -1)
        upstream = class_mix(jnp.concatenate([series, later], axis=1), table_bwd, selector)
        rows = from_gauges(upstream)
        spread = jnp.einsum(
            "bjr,bjt->brt", weights, rows.reshape(blocks, slots, hours), precision=HIGH
        )
        return spread.reshape(blocks * width, hours)

    start = observed - forward(first_guess)
    beta = jnp.sqrt(global_total(squared(start)))
    u = start / beta
    pulled = backward(u)
    alpha = jnp.sqrt(global_total(squared(pulled)))
    v = pulled / alpha
    w = v
    correction = jnp.zeros(first_guess.shape, jnp.float32)
    phibar = beta
    rhobar = alpha
    for step in range(ITERS):
        final = step == ITERS - 1
        p = forward(v) - alpha * u
        beta = jnp.sqrt(global_total(squared(p)))
        if not final:
            pulled = backward(p / beta) - beta * v
            alpha_next = jnp.sqrt(global_total(squared(pulled)))
            v_next = pulled / alpha_next
        u = p / beta
        rho = jnp.sqrt(rhobar * rhobar + beta * beta)
        cosine = rhobar / rho
        sine = beta / rho
        phi = cosine * phibar
        phibar = sine * phibar
        correction = correction + phi / rho * w
        if not final:
            theta = sine * alpha_next
            rhobar = -cosine * alpha_next
            w = v_next - theta / rho * w
            v = v_next
            alpha = alpha_next
    return first_guess + correction


def solution(mesh):
    in_specs = (
        P("basin", None, None),
        P("basin"),
        P("basin"),
        P(),
        P("basin", "tm"),
        P("basin", "tm"),
    )
    out_specs = P("basin", "tm")
    return jax.shard_map(shards, mesh=mesh, in_specs=in_specs, out_specs=out_specs, check_vma=False)
```

```python
import functools

import jax
import jax.numpy as jnp
from jax import lax
from jax.experimental import pallas as pl
from jax.experimental.pallas import tpu as pltpu
from jax.sharding import PartitionSpec as P

ITERS = 3
CAP = 32
LANES = 128

HIGH = lax.Precision.HIGHEST
MESH = pl.DeviceIdType.MESH


def from_behind(x, axis, by):
    devices = lax.axis_size(axis)
    pairs = [(i, i + by) for i in range(devices) if 0 <= i + by < devices]
    return lax.ppermute(x, axis, pairs)


def lag_table(kernels, lag):
    classes, taps = kernels.shape
    rows, hours = lag.shape
    onehot = (lag[None, :, :] == jnp.arange(taps)[:, None, None]).astype(jnp.float32)
    picked = jnp.dot(kernels, onehot.reshape(taps, rows * hours), precision=HIGH)
    picked = picked.reshape(classes, rows, hours)
    return jnp.transpose(picked, (1, 0, 2)).reshape(rows, classes * hours)


def class_mix(extended, table, selector):
    gauges = extended.shape[0]
    classes = selector.shape[1]
    spread = jnp.dot(extended, table, precision=HIGH).reshape(gauges, classes, -1)
    return jnp.sum(spread * selector[:, :, None], axis=1)


def squared(values):
    return jnp.sum(values * values)


def _allreduce_body(x_ref, o_ref, buf, own_sem, send_sem, recv_sem, *, nb, nt, rounds):
    me = lax.axis_index("basin") * nt + lax.axis_index("tm")

    def peer(r):
        step = 1 << r
        bit = (me // step) % 2
        other = me + step - 2 * step * bit
        return (other // nt, other % nt)

    barrier = pltpu.get_barrier_semaphore()
    for r in range(rounds):
        pl.semaphore_signal(barrier, inc=1, device_id=peer(r), device_id_type=MESH)
    pl.semaphore_wait(barrier, rounds)

    own = pltpu.make_async_copy(x_ref, buf.at[pl.ds(me, 1)], own_sem)
    own.start()
    own.wait()
    for r in range(rounds):
        step = 1 << r
        base = (me // step) * step
        copy = pltpu.make_async_remote_copy(
            src_ref=buf.at[pl.ds(base, step)],
            dst_ref=buf.at[pl.ds(base, step)],
            send_sem=send_sem.at[r],
            recv_sem=recv_sem.at[r],
            device_id=peer(r),
            device_id_type=MESH,
        )
        copy.start()
        copy.wait()
    o_ref[...] = jnp.sum(buf[...], axis=0, keepdims=True)


def global_total(value):
    nb = lax.axis_size("basin")
    nt = lax.axis_size("tm")
    n = nb * nt
    rounds = n.bit_length() - 1
    if n != (1 << rounds) or n < 2:
        return lax.psum(value, ("basin", "tm"))
    x = jnp.broadcast_to(value.astype(jnp.float32), (1, LANES))
    out = pl.pallas_call(
        functools.partial(_allreduce_body, nb=nb, nt=nt, rounds=rounds),
        out_shape=jax.ShapeDtypeStruct((1, LANES), jnp.float32),
        in_specs=[pl.BlockSpec(memory_space=pltpu.VMEM)],
        out_specs=pl.BlockSpec(memory_space=pltpu.VMEM),
        scratch_shapes=[
            pltpu.VMEM((n, LANES), jnp.float32),
            pltpu.SemaphoreType.DMA(()),
            pltpu.SemaphoreType.DMA((rounds,)),
            pltpu.SemaphoreType.DMA((rounds,)),
        ],
        compiler_params=pltpu.CompilerParams(collective_id=0, has_side_effects=True),
    )(x)
    return out[0, 0]


def _exchange_body(x_ref, o_ref, landed, own_sem, send_sem, recv_sem, *, nb):
    me = lax.axis_index("basin")
    hour_block = lax.axis_index("tm")
    barrier = pltpu.get_barrier_semaphore()
    for k in range(1, nb):
        pl.semaphore_signal(
            barrier, inc=1, device_id=(lax.rem(me + k, nb), hour_block), device_id_type=MESH
        )
    pl.semaphore_wait(barrier, nb - 1)
    own = pltpu.make_async_copy(x_ref.at[me], landed.at[me], own_sem)
    own.start()
    copies = []
    for k in range(1, nb):
        peer = lax.rem(me + k, nb)
        copy = pltpu.make_async_remote_copy(
            src_ref=x_ref.at[peer],
            dst_ref=landed.at[me],
            send_sem=send_sem.at[k],
            recv_sem=recv_sem.at[k],
            device_id=(peer, hour_block),
            device_id_type=MESH,
        )
        copy.start()
        copies.append(copy)
    own.wait()
    for k in range(1, nb):
        copies[k - 1].wait_send()
        source = lax.rem(me + nb - k, nb)
        pltpu.make_async_remote_copy(
            src_ref=x_ref.at[source],
            dst_ref=landed.at[source],
            send_sem=send_sem.at[k],
            recv_sem=recv_sem.at[k],
            device_id=(source, hour_block),
            device_id_type=MESH,
        ).wait_recv()
    o_ref[...] = landed[...]


def basin_exchange(x):
    nb = lax.axis_size("basin")
    total, hours = x.shape
    shaped = x.reshape(nb, total // nb, hours)
    out = pl.pallas_call(
        functools.partial(_exchange_body, nb=nb),
        out_shape=jax.ShapeDtypeStruct(shaped.shape, jnp.float32),
        in_specs=[pl.BlockSpec(memory_space=pltpu.VMEM)],
        out_specs=pl.BlockSpec(memory_space=pltpu.VMEM),
        scratch_shapes=[
            pltpu.VMEM(shaped.shape, jnp.float32),
            pltpu.SemaphoreType.DMA(()),
            pltpu.SemaphoreType.DMA((nb,)),
            pltpu.SemaphoreType.DMA((nb,)),
        ],
        compiler_params=pltpu.CompilerParams(collective_id=1, has_side_effects=True),
    )(shaped)
    return out.reshape(total, hours)


def shards(incidence, row_gauge, gauge_kernel, kernels, observed, first_guess):
    weights = incidence.astype(jnp.float32)
    blocks, slots, width = weights.shape
    gauges_here, hours = observed.shape
    owners = lax.axis_size("basin")
    classes = kernels.shape[0]
    partials = blocks * slots
    outer = jnp.arange(2 * hours)[:, None]
    inner = jnp.arange(hours)[None, :]
    table_fwd = lag_table(kernels, inner + hours - outer)
    table_bwd = lag_table(kernels, outer - inner)
    selector = (gauge_kernel[:, None] == jnp.arange(classes)[None, :]).astype(jnp.float32)

    owner = row_gauge // gauges_here
    local = row_gauge % gauges_here
    hit = owner[:, None] == jnp.arange(owners)[None, :]
    rank = jnp.cumsum(hit.astype(jnp.int32), axis=0) - 1
    dest = owner * CAP + jnp.sum(jnp.where(hit, rank, 0), axis=1)
    entries = owners * CAP
    place = (jnp.arange(entries)[:, None] == dest[None, :]).astype(jnp.float32)
    sent_ids = jnp.full((entries,), -1, jnp.int32).at[dest].set(local)
    got_ids = lax.all_to_all(sent_ids, "basin", 0, 0, tiled=True)
    gather = (jnp.arange(gauges_here)[:, None] == got_ids[None, :]).astype(jnp.float32)

    def to_gauges(partial_value):
        outgoing = jnp.dot(place, partial_value, precision=HIGH)
        incoming = basin_exchange(outgoing)
        return jnp.dot(gather, incoming, precision=HIGH)

    def from_gauges(upstream):
        outgoing = jnp.dot(gather.T, upstream, precision=HIGH)
        incoming = basin_exchange(outgoing)
        return jnp.dot(place.T, incoming, precision=HIGH)

    def forward(field):
        partial_value = jnp.einsum(
            "bjr,brt->bjt", weights, field.reshape(blocks, width, hours), precision=HIGH
        )
        sums = to_gauges(partial_value.reshape(partials, hours))
        earlier = from_behind(sums, "tm", 1)
        return class_mix(jnp.concatenate([earlier, sums], axis=1), table_fwd, selector)

    def backward(series):
        later = from_behind(series, "tm", -1)
        upstream = class_mix(jnp.concatenate([series, later], axis=1), table_bwd, selector)
        rows = from_gauges(upstream)
        spread = jnp.einsum(
            "bjr,bjt->brt", weights, rows.reshape(blocks, slots, hours), precision=HIGH
        )
        return spread.reshape(blocks * width, hours)

    start = observed - forward(first_guess)
    beta = jnp.sqrt(global_total(squared(start)))
    u = start / beta
    pulled = backward(u)
    alpha = jnp.sqrt(global_total(squared(pulled)))
    v = pulled / alpha
    w = v
    correction = jnp.zeros(first_guess.shape, jnp.float32)
    phibar = beta
    rhobar = alpha
    for step in range(ITERS):
        final = step == ITERS - 1
        p = forward(v) - alpha * u
        beta = jnp.sqrt(global_total(squared(p)))
        if not final:
            pulled = backward(p / beta) - beta * v
            alpha_next = jnp.sqrt(global_total(squared(pulled)))
            v_next = pulled / alpha_next
        u = p / beta
        rho = jnp.sqrt(rhobar * rhobar + beta * beta)
        cosine = rhobar / rho
        sine = beta / rho
        phi = cosine * phibar
        phibar = sine * phibar
        correction = correction + phi / rho * w
        if not final:
            theta = sine * alpha_next
            rhobar = -cosine * alpha_next
            w = v_next - theta / rho * w
            v = v_next
            alpha = alpha_next
    return first_guess + correction


def solution(mesh):
    in_specs = (
        P("basin", None, None),
        P("basin"),
        P("basin"),
        P(),
        P("basin", "tm"),
        P("basin", "tm"),
    )
    out_specs = P("basin", "tm")
    return jax.shard_map(shards, mesh=mesh, in_specs=in_specs, out_specs=out_specs, check_vma=False)
```

```python
import functools

import jax
import jax.numpy as jnp
from jax import lax
from jax.experimental import pallas as pl
from jax.experimental.pallas import tpu as pltpu
from jax.sharding import PartitionSpec as P

ITERS = 3
CAP = 32
LANES = 128

HIGH = lax.Precision.HIGHEST
MESH = pl.DeviceIdType.MESH


def from_behind(x, axis, by):
    devices = lax.axis_size(axis)
    pairs = [(i, i + by) for i in range(devices) if 0 <= i + by < devices]
    return lax.ppermute(x, axis, pairs)


def lag_table(kernels, lag):
    classes, taps = kernels.shape
    rows, hours = lag.shape
    onehot = (lag[None, :, :] == jnp.arange(taps)[:, None, None]).astype(jnp.float32)
    picked = jnp.dot(kernels, onehot.reshape(taps, rows * hours), precision=HIGH)
    picked = picked.reshape(classes, rows, hours)
    return jnp.transpose(picked, (1, 0, 2)).reshape(rows, classes * hours)


def class_mix(extended, table, selector):
    gauges = extended.shape[0]
    classes = selector.shape[1]
    spread = jnp.dot(extended, table, precision=HIGH).reshape(gauges, classes, -1)
    return jnp.sum(spread * selector[:, :, None], axis=1)


def squared(values):
    return jnp.sum(values * values)


def _allreduce_body(x_ref, o_ref, buf, own_sem, send_sem, recv_sem, *, nb, nt, rounds):
    me = lax.axis_index("basin") * nt + lax.axis_index("tm")

    def peer(r):
        step = 1 << r
        bit = (me // step) % 2
        other = me + step - 2 * step * bit
        return (other // nt, other % nt)

    barrier = pltpu.get_barrier_semaphore()
    for r in range(rounds):
        pl.semaphore_signal(barrier, inc=1, device_id=peer(r), device_id_type=MESH)
    pl.semaphore_wait(barrier, rounds)

    own = pltpu.make_async_copy(x_ref, buf.at[pl.ds(me, 1)], own_sem)
    own.start()
    own.wait()
    for r in range(rounds):
        step = 1 << r
        base = (me // step) * step
        copy = pltpu.make_async_remote_copy(
            src_ref=buf.at[pl.ds(base, step)],
            dst_ref=buf.at[pl.ds(base, step)],
            send_sem=send_sem.at[r],
            recv_sem=recv_sem.at[r],
            device_id=peer(r),
            device_id_type=MESH,
        )
        copy.start()
        copy.wait()
    o_ref[...] = jnp.sum(buf[...], axis=0, keepdims=True)


def global_total(value):
    nb = lax.axis_size("basin")
    nt = lax.axis_size("tm")
    n = nb * nt
    rounds = n.bit_length() - 1
    if n != (1 << rounds) or n < 2:
        return lax.psum(value, ("basin", "tm"))
    x = jnp.broadcast_to(value.astype(jnp.float32), (1, LANES))
    out = pl.pallas_call(
        functools.partial(_allreduce_body, nb=nb, nt=nt, rounds=rounds),
        out_shape=jax.ShapeDtypeStruct((1, LANES), jnp.float32),
        in_specs=[pl.BlockSpec(memory_space=pltpu.VMEM)],
        out_specs=pl.BlockSpec(memory_space=pltpu.VMEM),
        scratch_shapes=[
            pltpu.VMEM((n, LANES), jnp.float32),
            pltpu.SemaphoreType.DMA(()),
            pltpu.SemaphoreType.DMA((rounds,)),
            pltpu.SemaphoreType.DMA((rounds,)),
        ],
        compiler_params=pltpu.CompilerParams(collective_id=0, has_side_effects=True),
    )(x)
    return out[0, 0]


def _exchange_body(x_ref, o_ref, landed, own_sem, send_sem, recv_sem, *, nb):
    me = lax.axis_index("basin")
    hour_block = lax.axis_index("tm")
    barrier = pltpu.get_barrier_semaphore()
    for k in range(1, nb):
        pl.semaphore_signal(
            barrier, inc=1, device_id=(lax.rem(me + k, nb), hour_block), device_id_type=MESH
        )
    pl.semaphore_wait(barrier, nb - 1)
    own = pltpu.make_async_copy(x_ref.at[me], landed.at[me], own_sem)
    own.start()
    copies = []
    for k in range(1, nb):
        peer = lax.rem(me + k, nb)
        copy = pltpu.make_async_remote_copy(
            src_ref=x_ref.at[peer],
            dst_ref=landed.at[me],
            send_sem=send_sem.at[k],
            recv_sem=recv_sem.at[k],
            device_id=(peer, hour_block),
            device_id_type=MESH,
        )
        copy.start()
        copies.append(copy)
    own.wait()
    for k in range(1, nb):
        copies[k - 1].wait_send()
        source = lax.rem(me + nb - k, nb)
        pltpu.make_async_remote_copy(
            src_ref=x_ref.at[source],
            dst_ref=landed.at[source],
            send_sem=send_sem.at[k],
            recv_sem=recv_sem.at[k],
            device_id=(source, hour_block),
            device_id_type=MESH,
        ).wait_recv()
    o_ref[...] = landed[...]


def basin_exchange(x, carry):
    nb = lax.axis_size("basin")
    total, hours = x.shape
    rows = total // nb
    extra = jnp.broadcast_to(carry.astype(jnp.float32), (nb, 8, hours))
    packed = jnp.concatenate([x.reshape(nb, rows, hours), extra], axis=1)
    out = pl.pallas_call(
        functools.partial(_exchange_body, nb=nb),
        out_shape=jax.ShapeDtypeStruct(packed.shape, jnp.float32),
        in_specs=[pl.BlockSpec(memory_space=pltpu.VMEM)],
        out_specs=pl.BlockSpec(memory_space=pltpu.VMEM),
        scratch_shapes=[
            pltpu.VMEM(packed.shape, jnp.float32),
            pltpu.SemaphoreType.DMA(()),
            pltpu.SemaphoreType.DMA((nb,)),
            pltpu.SemaphoreType.DMA((nb,)),
        ],
        compiler_params=pltpu.CompilerParams(collective_id=1, has_side_effects=True),
    )(packed)
    return out[:, :rows, :].reshape(total, hours), jnp.sum(out[:, rows, 0])


def _shift_body(x_ref, c_ref, o_ref, t_ref, held, carried, own_sem, dsend, drecv, csend, crecv, *, nt, by):
    basin = lax.axis_index("basin")
    me = lax.axis_index("tm")
    barrier = pltpu.get_barrier_semaphore()
    for k in range(1, nt):
        pl.semaphore_signal(
            barrier, inc=1, device_id=(basin, lax.rem(me + k, nt)), device_id_type=MESH
        )
    pl.semaphore_wait(barrier, nt - 1)

    target = me + by
    source = me - by
    has_target = jnp.logical_and(target >= 0, target < nt)
    has_source = jnp.logical_and(source >= 0, source < nt)
    data = pltpu.make_async_remote_copy(
        src_ref=x_ref,
        dst_ref=held,
        send_sem=dsend,
        recv_sem=drecv,
        device_id=(basin, lax.rem(target + nt, nt)),
        device_id_type=MESH,
    )

    @pl.when(has_target)
    def _():
        data.start()

    own = pltpu.make_async_copy(c_ref, carried.at[pl.ds(me, 1)], own_sem)
    own.start()
    copies = []
    for k in range(1, nt):
        copy = pltpu.make_async_remote_copy(
            src_ref=c_ref,
            dst_ref=carried.at[pl.ds(me, 1)],
            send_sem=csend.at[k],
            recv_sem=crecv.at[k],
            device_id=(basin, lax.rem(me + k, nt)),
            device_id_type=MESH,
        )
        copy.start()
        copies.append(copy)
    own.wait()
    for k in range(1, nt):
        copies[k - 1].wait_send()
        origin = lax.rem(me + nt - k, nt)
        pltpu.make_async_remote_copy(
            src_ref=c_ref,
            dst_ref=carried.at[pl.ds(origin, 1)],
            send_sem=csend.at[k],
            recv_sem=crecv.at[k],
            device_id=(basin, origin),
            device_id_type=MESH,
        ).wait_recv()
    t_ref[...] = jnp.sum(carried[...], axis=0, keepdims=True)

    @pl.when(has_target)
    def _():
        data.wait_send()

    @pl.when(has_source)
    def _():
        data.wait_recv()
        o_ref[...] = held[...]

    @pl.when(jnp.logical_not(has_source))
    def _():
        o_ref[...] = jnp.zeros(o_ref.shape, o_ref.dtype)


def tm_shift(x, carry, by, ident):
    nt = lax.axis_size("tm")
    c = jnp.broadcast_to(carry.astype(jnp.float32), (1, LANES))
    out, summed = pl.pallas_call(
        functools.partial(_shift_body, nt=nt, by=by),
        out_shape=(
            jax.ShapeDtypeStruct(x.shape, jnp.float32),
            jax.ShapeDtypeStruct((1, LANES), jnp.float32),
        ),
        in_specs=[pl.BlockSpec(memory_space=pltpu.VMEM)] * 2,
        out_specs=(pl.BlockSpec(memory_space=pltpu.VMEM),) * 2,
        scratch_shapes=[
            pltpu.VMEM(x.shape, jnp.float32),
            pltpu.VMEM((nt, LANES), jnp.float32),
            pltpu.SemaphoreType.DMA(()),
            pltpu.SemaphoreType.DMA(()),
            pltpu.SemaphoreType.DMA(()),
            pltpu.SemaphoreType.DMA((nt,)),
            pltpu.SemaphoreType.DMA((nt,)),
        ],
        compiler_params=pltpu.CompilerParams(collective_id=ident, has_side_effects=True),
    )(x, c)
    return out, summed[0, 0]


def shards(incidence, row_gauge, gauge_kernel, kernels, observed, first_guess):
    weights = incidence.astype(jnp.float32)
    blocks, slots, width = weights.shape
    gauges_here, hours = observed.shape
    owners = lax.axis_size("basin")
    classes = kernels.shape[0]
    partials = blocks * slots
    outer = jnp.arange(2 * hours)[:, None]
    inner = jnp.arange(hours)[None, :]
    table_fwd = lag_table(kernels, inner + hours - outer)
    table_bwd = lag_table(kernels, outer - inner)
    selector = (gauge_kernel[:, None] == jnp.arange(classes)[None, :]).astype(jnp.float32)

    owner = row_gauge // gauges_here
    local = row_gauge % gauges_here
    hit = owner[:, None] == jnp.arange(owners)[None, :]
    rank = jnp.cumsum(hit.astype(jnp.int32), axis=0) - 1
    dest = owner * CAP + jnp.sum(jnp.where(hit, rank, 0), axis=1)
    entries = owners * CAP
    place = (jnp.arange(entries)[:, None] == dest[None, :]).astype(jnp.float32)
    sent_ids = jnp.full((entries,), -1, jnp.int32).at[dest].set(local)
    got_ids = lax.all_to_all(sent_ids, "basin", 0, 0, tiled=True)
    gather = (jnp.arange(gauges_here)[:, None] == got_ids[None, :]).astype(jnp.float32)

    def forward(field):
        partial_value = jnp.einsum(
            "bjr,brt->bjt", weights, field.reshape(blocks, width, hours), precision=HIGH
        )
        outgoing = jnp.dot(place, partial_value.reshape(partials, hours), precision=HIGH)
        incoming, basin_sq = basin_exchange(outgoing, squared(field))
        sums = jnp.dot(gather, incoming, precision=HIGH)
        earlier, total_sq = tm_shift(sums, basin_sq, 1, 2)
        return class_mix(jnp.concatenate([earlier, sums], axis=1), table_fwd, selector), total_sq

    def backward(series):
        later, tm_sq = tm_shift(series, squared(series), -1, 3)
        upstream = class_mix(jnp.concatenate([series, later], axis=1), table_bwd, selector)
        outgoing = jnp.dot(gather.T, upstream, precision=HIGH)
        incoming, total_sq = basin_exchange(outgoing, tm_sq)
        rows = jnp.dot(place.T, incoming, precision=HIGH)
        spread = jnp.einsum(
            "bjr,bjt->brt", weights, rows.reshape(blocks, slots, hours), precision=HIGH
        )
        return spread.reshape(blocks * width, hours), total_sq

    start = observed - forward(first_guess)[0]
    pulled_start, beta_sq = backward(start)
    beta = jnp.sqrt(beta_sq)
    u = start / beta
    pulled = pulled_start / beta
    forward_pulled, alpha_sq = forward(pulled)
    alpha = jnp.sqrt(alpha_sq)
    v = pulled / alpha
    w = v
    correction = jnp.zeros(first_guess.shape, jnp.float32)
    phibar = beta
    rhobar = alpha
    for step in range(ITERS):
        final = step == ITERS - 1
        p = forward_pulled / alpha - alpha * u
        if final:
            beta = jnp.sqrt(global_total(squared(p)))
        else:
            pulled_p, beta_sq = backward(p)
            beta = jnp.sqrt(beta_sq)
            pulled = pulled_p / beta - beta * v
            forward_pulled, alpha_next = forward(pulled)
            alpha_next = jnp.sqrt(alpha_next)
            v_next = pulled / alpha_next
        u = p / beta
        rho = jnp.sqrt(rhobar * rhobar + beta * beta)
        cosine = rhobar / rho
        sine = beta / rho
        phi = cosine * phibar
        phibar = sine * phibar
        correction = correction + phi / rho * w
        if not final:
            theta = sine * alpha_next
            rhobar = -cosine * alpha_next
            w = v_next - theta / rho * w
            v = v_next
            alpha = alpha_next
    return first_guess + correction


def solution(mesh):
    in_specs = (
        P("basin", None, None),
        P("basin"),
        P("basin"),
        P(),
        P("basin", "tm"),
        P("basin", "tm"),
    )
    out_specs = P("basin", "tm")
    return jax.shard_map(shards, mesh=mesh, in_specs=in_specs, out_specs=out_specs, check_vma=False)
```

```python
import functools

import jax
import jax.numpy as jnp
from jax import lax
from jax.experimental import pallas as pl
from jax.experimental.pallas import tpu as pltpu
from jax.sharding import PartitionSpec as P

ITERS = 3
CAP = 32
LANES = 128

HIGH = lax.Precision.HIGHEST
MESH = pl.DeviceIdType.MESH


def from_behind(x, axis, by):
    devices = lax.axis_size(axis)
    pairs = [(i, i + by) for i in range(devices) if 0 <= i + by < devices]
    return lax.ppermute(x, axis, pairs)


def lag_table(kernels, lag):
    classes, taps = kernels.shape
    rows, hours = lag.shape
    onehot = (lag[None, :, :] == jnp.arange(taps)[:, None, None]).astype(jnp.float32)
    picked = jnp.dot(kernels, onehot.reshape(taps, rows * hours), precision=HIGH)
    picked = picked.reshape(classes, rows, hours)
    return jnp.transpose(picked, (1, 0, 2)).reshape(rows, classes * hours)


def class_mix(extended, table, selector):
    gauges = extended.shape[0]
    classes = selector.shape[1]
    spread = jnp.dot(extended, table, precision=lax.Precision.HIGH).reshape(gauges, classes, -1)
    return jnp.sum(spread * selector[:, :, None], axis=1)


def squared(values):
    return jnp.sum(values * values)


def _total_body(x_ref, o_ref, landed, own_sem, send_sem, recv_sem, *, nb, nt):
    n = nb * nt
    me = lax.axis_index("basin") * nt + lax.axis_index("tm")

    def device(index):
        return (index // nt, index % nt)

    barrier = pltpu.get_barrier_semaphore()
    for k in range(1, n):
        pl.semaphore_signal(barrier, inc=1, device_id=device(lax.rem(me + k, n)), device_id_type=MESH)
    pl.semaphore_wait(barrier, n - 1)

    own = pltpu.make_async_copy(x_ref, landed.at[pl.ds(me, 1)], own_sem)
    own.start()
    copies = []
    for k in range(1, n):
        copy = pltpu.make_async_remote_copy(
            src_ref=x_ref,
            dst_ref=landed.at[pl.ds(me, 1)],
            send_sem=send_sem.at[k],
            recv_sem=recv_sem.at[k],
            device_id=device(lax.rem(me + k, n)),
            device_id_type=MESH,
        )
        copy.start()
        copies.append(copy)
    own.wait()
    for k in range(1, n):
        copies[k - 1].wait_send()
        origin = lax.rem(me + n - k, n)
        pltpu.make_async_remote_copy(
            src_ref=x_ref,
            dst_ref=landed.at[pl.ds(origin, 1)],
            send_sem=send_sem.at[k],
            recv_sem=recv_sem.at[k],
            device_id=device(origin),
            device_id_type=MESH,
        ).wait_recv()
    o_ref[...] = jnp.sum(landed[...], axis=0, keepdims=True)


def global_total(value):
    nb = lax.axis_size("basin")
    nt = lax.axis_size("tm")
    n = nb * nt
    x = jnp.broadcast_to(value.astype(jnp.float32), (1, LANES))
    out = pl.pallas_call(
        functools.partial(_total_body, nb=nb, nt=nt),
        out_shape=jax.ShapeDtypeStruct((1, LANES), jnp.float32),
        in_specs=[pl.BlockSpec(memory_space=pltpu.VMEM)],
        out_specs=pl.BlockSpec(memory_space=pltpu.VMEM),
        scratch_shapes=[
            pltpu.VMEM((n, LANES), jnp.float32),
            pltpu.SemaphoreType.DMA(()),
            pltpu.SemaphoreType.DMA((n,)),
            pltpu.SemaphoreType.DMA((n,)),
        ],
        compiler_params=pltpu.CompilerParams(collective_id=0, has_side_effects=True),
    )(x)
    return out[0, 0]


def _exchange_body(x_ref, o_ref, landed, own_sem, send_sem, recv_sem, *, nb):
    me = lax.axis_index("basin")
    hour_block = lax.axis_index("tm")
    barrier = pltpu.get_barrier_semaphore()
    for k in range(1, nb):
        pl.semaphore_signal(
            barrier, inc=1, device_id=(lax.rem(me + k, nb), hour_block), device_id_type=MESH
        )
    pl.semaphore_wait(barrier, nb - 1)
    own = pltpu.make_async_copy(x_ref.at[me], landed.at[me], own_sem)
    own.start()
    copies = []
    for k in range(1, nb):
        peer = lax.rem(me + k, nb)
        copy = pltpu.make_async_remote_copy(
            src_ref=x_ref.at[peer],
            dst_ref=landed.at[me],
            send_sem=send_sem.at[k],
            recv_sem=recv_sem.at[k],
            device_id=(peer, hour_block),
            device_id_type=MESH,
        )
        copy.start()
        copies.append(copy)
    own.wait()
    for k in range(1, nb):
        copies[k - 1].wait_send()
        source = lax.rem(me + nb - k, nb)
        pltpu.make_async_remote_copy(
            src_ref=x_ref.at[source],
            dst_ref=landed.at[source],
            send_sem=send_sem.at[k],
            recv_sem=recv_sem.at[k],
            device_id=(source, hour_block),
            device_id_type=MESH,
        ).wait_recv()
    o_ref[...] = landed[...]


def basin_exchange(x, carry):
    nb = lax.axis_size("basin")
    total, hours = x.shape
    rows = total // nb
    extra = jnp.broadcast_to(carry.astype(jnp.float32), (nb, 8, hours))
    packed = jnp.concatenate([x.reshape(nb, rows, hours), extra], axis=1)
    out = pl.pallas_call(
        functools.partial(_exchange_body, nb=nb),
        out_shape=jax.ShapeDtypeStruct(packed.shape, jnp.float32),
        in_specs=[pl.BlockSpec(memory_space=pltpu.VMEM)],
        out_specs=pl.BlockSpec(memory_space=pltpu.VMEM),
        scratch_shapes=[
            pltpu.VMEM(packed.shape, jnp.float32),
            pltpu.SemaphoreType.DMA(()),
            pltpu.SemaphoreType.DMA((nb,)),
            pltpu.SemaphoreType.DMA((nb,)),
        ],
        compiler_params=pltpu.CompilerParams(collective_id=1, has_side_effects=True),
    )(packed)
    return out[:, :rows, :].reshape(total, hours), jnp.sum(out[:, rows, 0])


def _shift_body(x_ref, c_ref, o_ref, t_ref, held, carried, own_sem, dsend, drecv, csend, crecv, *, nt, by):
    basin = lax.axis_index("basin")
    me = lax.axis_index("tm")
    barrier = pltpu.get_barrier_semaphore()
    for k in range(1, nt):
        pl.semaphore_signal(
            barrier, inc=1, device_id=(basin, lax.rem(me + k, nt)), device_id_type=MESH
        )
    pl.semaphore_wait(barrier, nt - 1)

    target = me + by
    source = me - by
    has_target = jnp.logical_and(target >= 0, target < nt)
    has_source = jnp.logical_and(source >= 0, source < nt)
    data = pltpu.make_async_remote_copy(
        src_ref=x_ref,
        dst_ref=held,
        send_sem=dsend,
        recv_sem=drecv,
        device_id=(basin, lax.rem(target + nt, nt)),
        device_id_type=MESH,
    )

    @pl.when(has_target)
    def _():
        data.start()

    own = pltpu.make_async_copy(c_ref, carried.at[pl.ds(me, 1)], own_sem)
    own.start()
    copies = []
    for k in range(1, nt):
        copy = pltpu.make_async_remote_copy(
            src_ref=c_ref,
            dst_ref=carried.at[pl.ds(me, 1)],
            send_sem=csend.at[k],
            recv_sem=crecv.at[k],
            device_id=(basin, lax.rem(me + k, nt)),
            device_id_type=MESH,
        )
        copy.start()
        copies.append(copy)
    own.wait()
    for k in range(1, nt):
        copies[k - 1].wait_send()
        origin = lax.rem(me + nt - k, nt)
        pltpu.make_async_remote_copy(
            src_ref=c_ref,
            dst_ref=carried.at[pl.ds(origin, 1)],
            send_sem=csend.at[k],
            recv_sem=crecv.at[k],
            device_id=(basin, origin),
            device_id_type=MESH,
        ).wait_recv()
    t_ref[...] = jnp.sum(carried[...], axis=0, keepdims=True)

    @pl.when(has_target)
    def _():
        data.wait_send()

    @pl.when(has_source)
    def _():
        data.wait_recv()
        o_ref[...] = held[...]

    @pl.when(jnp.logical_not(has_source))
    def _():
        o_ref[...] = jnp.zeros(o_ref.shape, o_ref.dtype)


def tm_shift(x, carry, by, ident):
    nt = lax.axis_size("tm")
    c = jnp.broadcast_to(carry.astype(jnp.float32), (1, LANES))
    out, summed = pl.pallas_call(
        functools.partial(_shift_body, nt=nt, by=by),
        out_shape=(
            jax.ShapeDtypeStruct(x.shape, jnp.float32),
            jax.ShapeDtypeStruct((1, LANES), jnp.float32),
        ),
        in_specs=[pl.BlockSpec(memory_space=pltpu.VMEM)] * 2,
        out_specs=(pl.BlockSpec(memory_space=pltpu.VMEM),) * 2,
        scratch_shapes=[
            pltpu.VMEM(x.shape, jnp.float32),
            pltpu.VMEM((nt, LANES), jnp.float32),
            pltpu.SemaphoreType.DMA(()),
            pltpu.SemaphoreType.DMA(()),
            pltpu.SemaphoreType.DMA(()),
            pltpu.SemaphoreType.DMA((nt,)),
            pltpu.SemaphoreType.DMA((nt,)),
        ],
        compiler_params=pltpu.CompilerParams(collective_id=ident, has_side_effects=True),
    )(x, c)
    return out, summed[0, 0]


def shards(incidence, row_gauge, gauge_kernel, kernels, observed, first_guess):
    weights = incidence.astype(jnp.float32)
    blocks, slots, width = weights.shape
    gauges_here, hours = observed.shape
    owners = lax.axis_size("basin")
    classes = kernels.shape[0]
    partials = blocks * slots
    outer = jnp.arange(2 * hours)[:, None]
    inner = jnp.arange(hours)[None, :]
    table_fwd = lag_table(kernels, inner + hours - outer)
    table_bwd = lag_table(kernels, outer - inner)
    selector = (gauge_kernel[:, None] == jnp.arange(classes)[None, :]).astype(jnp.float32)

    owner = row_gauge // gauges_here
    local = row_gauge % gauges_here
    hit = owner[:, None] == jnp.arange(owners)[None, :]
    rank = jnp.cumsum(hit.astype(jnp.int32), axis=0) - 1
    dest = owner * CAP + jnp.sum(jnp.where(hit, rank, 0), axis=1)
    entries = owners * CAP
    place = (jnp.arange(entries)[:, None] == dest[None, :]).astype(jnp.float32)
    sent_ids = jnp.full((entries,), -1, jnp.int32).at[dest].set(local)
    got_ids = lax.all_to_all(sent_ids, "basin", 0, 0, tiled=True)
    gather = (jnp.arange(gauges_here)[:, None] == got_ids[None, :]).astype(jnp.float32)

    def forward(field):
        partial_value = jnp.einsum(
            "bjr,brt->bjt", weights, field.reshape(blocks, width, hours), precision=HIGH
        )
        outgoing = jnp.dot(place, partial_value.reshape(partials, hours), precision=HIGH)
        incoming, basin_sq = basin_exchange(outgoing, squared(field))
        sums = jnp.dot(gather, incoming, precision=HIGH)
        earlier, total_sq = tm_shift(sums, basin_sq, 1, 2)
        return class_mix(jnp.concatenate([earlier, sums], axis=1), table_fwd, selector), total_sq

    def backward(series):
        later, tm_sq = tm_shift(series, squared(series), -1, 3)
        upstream = class_mix(jnp.concatenate([series, later], axis=1), table_bwd, selector)
        outgoing = jnp.dot(gather.T, upstream, precision=HIGH)
        incoming, total_sq = basin_exchange(outgoing, tm_sq)
        rows = jnp.dot(place.T, incoming, precision=HIGH)
        spread = jnp.einsum(
            "bjr,bjt->brt", weights, rows.reshape(blocks, slots, hours), precision=HIGH
        )
        return spread.reshape(blocks * width, hours), total_sq

    start = observed - forward(first_guess)[0]
    pulled_start, beta_sq = backward(start)
    beta = jnp.sqrt(beta_sq)
    u = start / beta
    pulled = pulled_start / beta
    forward_pulled, alpha_sq = forward(pulled)
    alpha = jnp.sqrt(alpha_sq)
    v = pulled / alpha
    w = v
    correction = jnp.zeros(first_guess.shape, jnp.float32)
    phibar = beta
    rhobar = alpha
    for step in range(ITERS):
        final = step == ITERS - 1
        p = forward_pulled / alpha - alpha * u
        if final:
            beta = jnp.sqrt(global_total(squared(p)))
        else:
            pulled_p, beta_sq = backward(p)
            beta = jnp.sqrt(beta_sq)
            pulled = pulled_p / beta - beta * v
            forward_pulled, alpha_next = forward(pulled)
            alpha_next = jnp.sqrt(alpha_next)
            v_next = pulled / alpha_next
        u = p / beta
        rho = jnp.sqrt(rhobar * rhobar + beta * beta)
        cosine = rhobar / rho
        sine = beta / rho
        phi = cosine * phibar
        phibar = sine * phibar
        correction = correction + phi / rho * w
        if not final:
            theta = sine * alpha_next
            rhobar = -cosine * alpha_next
            w = v_next - theta / rho * w
            v = v_next
            alpha = alpha_next
    return first_guess + correction


def solution(mesh):
    in_specs = (
        P("basin", None, None),
        P("basin"),
        P("basin"),
        P(),
        P("basin", "tm"),
        P("basin", "tm"),
    )
    out_specs = P("basin", "tm")
    return jax.shard_map(shards, mesh=mesh, in_specs=in_specs, out_specs=out_specs, check_vma=False)
```

```python
import functools

import jax
import jax.numpy as jnp
from jax import lax
from jax.experimental import pallas as pl
from jax.experimental.pallas import tpu as pltpu
from jax.sharding import PartitionSpec as P

ITERS = 3
CAP = 32
LANES = 128

HIGH = lax.Precision.HIGHEST
MESH = pl.DeviceIdType.MESH


def from_behind(x, axis, by):
    devices = lax.axis_size(axis)
    pairs = [(i, i + by) for i in range(devices) if 0 <= i + by < devices]
    return lax.ppermute(x, axis, pairs)


def lag_table(kernels, lag):
    classes, taps = kernels.shape
    rows, hours = lag.shape
    onehot = (lag[None, :, :] == jnp.arange(taps)[:, None, None]).astype(jnp.float32)
    picked = jnp.dot(kernels, onehot.reshape(taps, rows * hours), precision=HIGH)
    picked = picked.reshape(classes, rows, hours)
    return jnp.transpose(picked, (1, 0, 2)).reshape(rows, classes * hours)


def class_mix(extended, table, selector):
    gauges = extended.shape[0]
    classes = selector.shape[1]
    spread = jnp.dot(extended, table, precision=lax.Precision.HIGH).reshape(gauges, classes, -1)
    return jnp.sum(spread * selector[:, :, None], axis=1)


def squared(values):
    return jnp.sum(values * values)


def _total_body(x_ref, o_ref, landed, own_sem, send_sem, recv_sem, *, nb, nt):
    n = nb * nt
    me = lax.axis_index("basin") * nt + lax.axis_index("tm")

    def device(index):
        return (index // nt, index % nt)

    barrier = pltpu.get_barrier_semaphore()
    for k in range(1, n):
        pl.semaphore_signal(barrier, inc=1, device_id=device(lax.rem(me + k, n)), device_id_type=MESH)
    pl.semaphore_wait(barrier, n - 1)

    own = pltpu.make_async_copy(x_ref, landed.at[pl.ds(me, 1)], own_sem)
    own.start()
    copies = []
    for k in range(1, n):
        copy = pltpu.make_async_remote_copy(
            src_ref=x_ref,
            dst_ref=landed.at[pl.ds(me, 1)],
            send_sem=send_sem.at[k],
            recv_sem=recv_sem.at[k],
            device_id=device(lax.rem(me + k, n)),
            device_id_type=MESH,
        )
        copy.start()
        copies.append(copy)
    own.wait()
    for k in range(1, n):
        copies[k - 1].wait_send()
        origin = lax.rem(me + n - k, n)
        pltpu.make_async_remote_copy(
            src_ref=x_ref,
            dst_ref=landed.at[pl.ds(origin, 1)],
            send_sem=send_sem.at[k],
            recv_sem=recv_sem.at[k],
            device_id=device(origin),
            device_id_type=MESH,
        ).wait_recv()
    o_ref[...] = jnp.sum(landed[...], axis=0, keepdims=True)


def global_total(value):
    nb = lax.axis_size("basin")
    nt = lax.axis_size("tm")
    n = nb * nt
    x = jnp.broadcast_to(value.astype(jnp.float32), (1, LANES))
    out = pl.pallas_call(
        functools.partial(_total_body, nb=nb, nt=nt),
        out_shape=jax.ShapeDtypeStruct((1, LANES), jnp.float32),
        in_specs=[pl.BlockSpec(memory_space=pltpu.VMEM)],
        out_specs=pl.BlockSpec(memory_space=pltpu.VMEM),
        scratch_shapes=[
            pltpu.VMEM((n, LANES), jnp.float32),
            pltpu.SemaphoreType.DMA(()),
            pltpu.SemaphoreType.DMA((n,)),
            pltpu.SemaphoreType.DMA((n,)),
        ],
        compiler_params=pltpu.CompilerParams(collective_id=0, has_side_effects=True),
    )(x)
    return out[0, 0]


def _exchange_body(x_ref, c_ref, o_ref, t_ref, landed, carried, own_sem, send_sem, recv_sem, csend, crecv, *, nb):
    me = lax.axis_index("basin")
    hour_block = lax.axis_index("tm")
    barrier = pltpu.get_barrier_semaphore()
    for k in range(1, nb):
        pl.semaphore_signal(
            barrier, inc=1, device_id=(lax.rem(me + k, nb), hour_block), device_id_type=MESH
        )
    pl.semaphore_wait(barrier, nb - 1)
    own = pltpu.make_async_copy(x_ref.at[me], landed.at[me], own_sem.at[0])
    own.start()
    own_carry = pltpu.make_async_copy(c_ref, carried.at[pl.ds(me, 1)], own_sem.at[1])
    own_carry.start()
    copies = []
    for k in range(1, nb):
        peer = lax.rem(me + k, nb)
        copy = pltpu.make_async_remote_copy(
            src_ref=x_ref.at[peer],
            dst_ref=landed.at[me],
            send_sem=send_sem.at[k],
            recv_sem=recv_sem.at[k],
            device_id=(peer, hour_block),
            device_id_type=MESH,
        )
        copy.start()
        carry = pltpu.make_async_remote_copy(
            src_ref=c_ref,
            dst_ref=carried.at[pl.ds(me, 1)],
            send_sem=csend.at[k],
            recv_sem=crecv.at[k],
            device_id=(peer, hour_block),
            device_id_type=MESH,
        )
        carry.start()
        copies.append((copy, carry))
    own.wait()
    own_carry.wait()
    for k in range(1, nb):
        copies[k - 1][0].wait_send()
        copies[k - 1][1].wait_send()
        source = lax.rem(me + nb - k, nb)
        pltpu.make_async_remote_copy(
            src_ref=x_ref.at[source],
            dst_ref=landed.at[source],
            send_sem=send_sem.at[k],
            recv_sem=recv_sem.at[k],
            device_id=(source, hour_block),
            device_id_type=MESH,
        ).wait_recv()
        pltpu.make_async_remote_copy(
            src_ref=c_ref,
            dst_ref=carried.at[pl.ds(source, 1)],
            send_sem=csend.at[k],
            recv_sem=crecv.at[k],
            device_id=(source, hour_block),
            device_id_type=MESH,
        ).wait_recv()
    o_ref[...] = landed[...]
    t_ref[...] = jnp.sum(carried[...], axis=0, keepdims=True)


def as_row(value):
    if value.ndim == 2:
        return value
    return jnp.broadcast_to(value.astype(jnp.float32), (1, LANES))


def basin_exchange(x, carry):
    nb = lax.axis_size("basin")
    total, hours = x.shape
    shaped = x.reshape(nb, total // nb, hours)
    out, summed = pl.pallas_call(
        functools.partial(_exchange_body, nb=nb),
        out_shape=(
            jax.ShapeDtypeStruct(shaped.shape, jnp.float32),
            jax.ShapeDtypeStruct((1, LANES), jnp.float32),
        ),
        in_specs=[pl.BlockSpec(memory_space=pltpu.VMEM)] * 2,
        out_specs=(pl.BlockSpec(memory_space=pltpu.VMEM),) * 2,
        scratch_shapes=[
            pltpu.VMEM(shaped.shape, jnp.float32),
            pltpu.VMEM((nb, LANES), jnp.float32),
            pltpu.SemaphoreType.DMA((2,)),
            pltpu.SemaphoreType.DMA((nb,)),
            pltpu.SemaphoreType.DMA((nb,)),
            pltpu.SemaphoreType.DMA((nb,)),
            pltpu.SemaphoreType.DMA((nb,)),
        ],
        compiler_params=pltpu.CompilerParams(collective_id=1, has_side_effects=True),
    )(shaped, as_row(carry))
    return out.reshape(total, hours), summed


def _shift_body(x_ref, c_ref, o_ref, t_ref, held, carried, own_sem, dsend, drecv, csend, crecv, *, nt, by):
    basin = lax.axis_index("basin")
    me = lax.axis_index("tm")
    barrier = pltpu.get_barrier_semaphore()
    for k in range(1, nt):
        pl.semaphore_signal(
            barrier, inc=1, device_id=(basin, lax.rem(me + k, nt)), device_id_type=MESH
        )
    pl.semaphore_wait(barrier, nt - 1)

    target = me + by
    source = me - by
    has_target = jnp.logical_and(target >= 0, target < nt)
    has_source = jnp.logical_and(source >= 0, source < nt)
    data = pltpu.make_async_remote_copy(
        src_ref=x_ref,
        dst_ref=held,
        send_sem=dsend,
        recv_sem=drecv,
        device_id=(basin, lax.rem(target + nt, nt)),
        device_id_type=MESH,
    )

    @pl.when(has_target)
    def _():
        data.start()

    own = pltpu.make_async_copy(c_ref, carried.at[pl.ds(me, 1)], own_sem)
    own.start()
    copies = []
    for k in range(1, nt):
        copy = pltpu.make_async_remote_copy(
            src_ref=c_ref,
            dst_ref=carried.at[pl.ds(me, 1)],
            send_sem=csend.at[k],
            recv_sem=crecv.at[k],
            device_id=(basin, lax.rem(me + k, nt)),
            device_id_type=MESH,
        )
        copy.start()
        copies.append(copy)
    own.wait()
    for k in range(1, nt):
        copies[k - 1].wait_send()
        origin = lax.rem(me + nt - k, nt)
        pltpu.make_async_remote_copy(
            src_ref=c_ref,
            dst_ref=carried.at[pl.ds(origin, 1)],
            send_sem=csend.at[k],
            recv_sem=crecv.at[k],
            device_id=(basin, origin),
            device_id_type=MESH,
        ).wait_recv()
    t_ref[...] = jnp.sum(carried[...], axis=0, keepdims=True)

    @pl.when(has_target)
    def _():
        data.wait_send()

    @pl.when(has_source)
    def _():
        data.wait_recv()
        o_ref[...] = held[...]

    @pl.when(jnp.logical_not(has_source))
    def _():
        o_ref[...] = jnp.zeros(o_ref.shape, o_ref.dtype)


def tm_shift(x, carry, by, ident):
    nt = lax.axis_size("tm")
    c = as_row(carry)
    out, summed = pl.pallas_call(
        functools.partial(_shift_body, nt=nt, by=by),
        out_shape=(
            jax.ShapeDtypeStruct(x.shape, jnp.float32),
            jax.ShapeDtypeStruct((1, LANES), jnp.float32),
        ),
        in_specs=[pl.BlockSpec(memory_space=pltpu.VMEM)] * 2,
        out_specs=(pl.BlockSpec(memory_space=pltpu.VMEM),) * 2,
        scratch_shapes=[
            pltpu.VMEM(x.shape, jnp.float32),
            pltpu.VMEM((nt, LANES), jnp.float32),
            pltpu.SemaphoreType.DMA(()),
            pltpu.SemaphoreType.DMA(()),
            pltpu.SemaphoreType.DMA(()),
            pltpu.SemaphoreType.DMA((nt,)),
            pltpu.SemaphoreType.DMA((nt,)),
        ],
        compiler_params=pltpu.CompilerParams(collective_id=ident, has_side_effects=True),
    )(x, c)
    return out, summed


def shards(incidence, row_gauge, gauge_kernel, kernels, observed, first_guess):
    weights = incidence.astype(jnp.float32)
    blocks, slots, width = weights.shape
    gauges_here, hours = observed.shape
    owners = lax.axis_size("basin")
    classes = kernels.shape[0]
    partials = blocks * slots
    outer = jnp.arange(2 * hours)[:, None]
    inner = jnp.arange(hours)[None, :]
    table_fwd = lag_table(kernels, inner + hours - outer)
    table_bwd = lag_table(kernels, outer - inner)
    selector = (gauge_kernel[:, None] == jnp.arange(classes)[None, :]).astype(jnp.float32)

    owner = row_gauge // gauges_here
    local = row_gauge % gauges_here
    hit = owner[:, None] == jnp.arange(owners)[None, :]
    rank = jnp.cumsum(hit.astype(jnp.int32), axis=0) - 1
    dest = owner * CAP + jnp.sum(jnp.where(hit, rank, 0), axis=1)
    entries = owners * CAP
    place = (jnp.arange(entries)[:, None] == dest[None, :]).astype(jnp.float32)
    sent_ids = jnp.full((entries,), -1, jnp.int32).at[dest].set(local)
    got_ids = lax.all_to_all(sent_ids, "basin", 0, 0, tiled=True)
    gather = (jnp.arange(gauges_here)[:, None] == got_ids[None, :]).astype(jnp.float32)

    def forward(field):
        partial_value = jnp.einsum(
            "bjr,brt->bjt", weights, field.reshape(blocks, width, hours), precision=HIGH
        )
        outgoing = jnp.dot(place, partial_value.reshape(partials, hours), precision=HIGH)
        incoming, basin_sq = basin_exchange(outgoing, squared(field))
        sums = jnp.dot(gather, incoming, precision=HIGH)
        earlier, total_sq = tm_shift(sums, basin_sq, 1, 2)
        return class_mix(jnp.concatenate([earlier, sums], axis=1), table_fwd, selector), total_sq[0, 0]

    def backward(series):
        later, tm_sq = tm_shift(series, squared(series), -1, 3)
        upstream = class_mix(jnp.concatenate([series, later], axis=1), table_bwd, selector)
        outgoing = jnp.dot(gather.T, upstream, precision=HIGH)
        incoming, total_sq = basin_exchange(outgoing, tm_sq)
        rows = jnp.dot(place.T, incoming, precision=HIGH)
        spread = jnp.einsum(
            "bjr,bjt->brt", weights, rows.reshape(blocks, slots, hours), precision=HIGH
        )
        return spread.reshape(blocks * width, hours), total_sq[0, 0]

    start = observed - forward(first_guess)[0]
    pulled_start, beta_sq = backward(start)
    beta = jnp.sqrt(beta_sq)
    u = start / beta
    pulled = pulled_start / beta
    forward_pulled, alpha_sq = forward(pulled)
    alpha = jnp.sqrt(alpha_sq)
    v = pulled / alpha
    w = v
    correction = jnp.zeros(first_guess.shape, jnp.float32)
    phibar = beta
    rhobar = alpha
    for step in range(ITERS):
        final = step == ITERS - 1
        p = forward_pulled / alpha - alpha * u
        if final:
            beta = jnp.sqrt(global_total(squared(p)))
        else:
            pulled_p, beta_sq = backward(p)
            beta = jnp.sqrt(beta_sq)
            pulled = pulled_p / beta - beta * v
            forward_pulled, alpha_next = forward(pulled)
            alpha_next = jnp.sqrt(alpha_next)
            v_next = pulled / alpha_next
        u = p / beta
        rho = jnp.sqrt(rhobar * rhobar + beta * beta)
        cosine = rhobar / rho
        sine = beta / rho
        phi = cosine * phibar
        phibar = sine * phibar
        correction = correction + phi / rho * w
        if not final:
            theta = sine * alpha_next
            rhobar = -cosine * alpha_next
            w = v_next - theta / rho * w
            v = v_next
            alpha = alpha_next
    return first_guess + correction


def solution(mesh):
    in_specs = (
        P("basin", None, None),
        P("basin"),
        P("basin"),
        P(),
        P("basin", "tm"),
        P("basin", "tm"),
    )
    out_specs = P("basin", "tm")
    return jax.shard_map(shards, mesh=mesh, in_specs=in_specs, out_specs=out_specs, check_vma=False)
```

```python
import functools

import jax
import jax.numpy as jnp
from jax import lax
from jax.experimental import pallas as pl
from jax.experimental.pallas import tpu as pltpu
from jax.sharding import PartitionSpec as P

ITERS = 3
CAP = 32
LANES = 128

HIGH = lax.Precision.HIGHEST
MESH = pl.DeviceIdType.MESH


def from_behind(x, axis, by):
    devices = lax.axis_size(axis)
    pairs = [(i, i + by) for i in range(devices) if 0 <= i + by < devices]
    return lax.ppermute(x, axis, pairs)


def lag_table(kernels, lag):
    classes, taps = kernels.shape
    rows, hours = lag.shape
    onehot = (lag.T[:, :, None] == jnp.arange(taps)[None, None, :]).astype(jnp.float32)
    stacked = jnp.broadcast_to(kernels[None], (hours, classes, taps))
    return lax.dot_general(stacked, onehot, (((2,), (2,)), ((0,), (0,))), precision=HIGH)


def class_mix(extended, table, selector):
    spread = lax.dot_general(table, extended, (((2,), (1,)), ((), ())), precision=lax.Precision.HIGH)
    return jnp.sum(spread * selector.T[None, :, :], axis=1).T


def squared(values):
    return jnp.sum(values * values)


def _total_body(x_ref, o_ref, landed, own_sem, send_sem, recv_sem, *, nb, nt):
    n = nb * nt
    me = lax.axis_index("basin") * nt + lax.axis_index("tm")

    def device(index):
        return (index // nt, index % nt)

    barrier = pltpu.get_barrier_semaphore()
    for k in range(1, n):
        pl.semaphore_signal(barrier, inc=1, device_id=device(lax.rem(me + k, n)), device_id_type=MESH)
    pl.semaphore_wait(barrier, n - 1)

    own = pltpu.make_async_copy(x_ref, landed.at[pl.ds(me, 1)], own_sem)
    own.start()
    copies = []
    for k in range(1, n):
        copy = pltpu.make_async_remote_copy(
            src_ref=x_ref,
            dst_ref=landed.at[pl.ds(me, 1)],
            send_sem=send_sem.at[k],
            recv_sem=recv_sem.at[k],
            device_id=device(lax.rem(me + k, n)),
            device_id_type=MESH,
        )
        copy.start()
        copies.append(copy)
    own.wait()
    for k in range(1, n):
        copies[k - 1].wait_send()
        origin = lax.rem(me + n - k, n)
        pltpu.make_async_remote_copy(
            src_ref=x_ref,
            dst_ref=landed.at[pl.ds(origin, 1)],
            send_sem=send_sem.at[k],
            recv_sem=recv_sem.at[k],
            device_id=device(origin),
            device_id_type=MESH,
        ).wait_recv()
    o_ref[...] = jnp.sum(landed[...], axis=0, keepdims=True)


def global_total(value):
    nb = lax.axis_size("basin")
    nt = lax.axis_size("tm")
    n = nb * nt
    x = jnp.broadcast_to(value.astype(jnp.float32), (1, LANES))
    out = pl.pallas_call(
        functools.partial(_total_body, nb=nb, nt=nt),
        out_shape=jax.ShapeDtypeStruct((1, LANES), jnp.float32),
        in_specs=[pl.BlockSpec(memory_space=pltpu.VMEM)],
        out_specs=pl.BlockSpec(memory_space=pltpu.VMEM),
        scratch_shapes=[
            pltpu.VMEM((n, LANES), jnp.float32),
            pltpu.SemaphoreType.DMA(()),
            pltpu.SemaphoreType.DMA((n,)),
            pltpu.SemaphoreType.DMA((n,)),
        ],
        compiler_params=pltpu.CompilerParams(collective_id=0, has_side_effects=True),
    )(x)
    return out[0, 0]


def _exchange_body(x_ref, c_ref, o_ref, t_ref, landed, carried, own_sem, send_sem, recv_sem, csend, crecv, *, nb):
    me = lax.axis_index("basin")
    hour_block = lax.axis_index("tm")
    barrier = pltpu.get_barrier_semaphore()
    for k in range(1, nb):
        pl.semaphore_signal(
            barrier, inc=1, device_id=(lax.rem(me + k, nb), hour_block), device_id_type=MESH
        )
    pl.semaphore_wait(barrier, nb - 1)
    own = pltpu.make_async_copy(x_ref.at[me], landed.at[me], own_sem.at[0])
    own.start()
    own_carry = pltpu.make_async_copy(c_ref, carried.at[pl.ds(me, 1)], own_sem.at[1])
    own_carry.start()
    copies = []
    for k in range(1, nb):
        peer = lax.rem(me + k, nb)
        copy = pltpu.make_async_remote_copy(
            src_ref=x_ref.at[peer],
            dst_ref=landed.at[me],
            send_sem=send_sem.at[k],
            recv_sem=recv_sem.at[k],
            device_id=(peer, hour_block),
            device_id_type=MESH,
        )
        copy.start()
        carry = pltpu.make_async_remote_copy(
            src_ref=c_ref,
            dst_ref=carried.at[pl.ds(me, 1)],
            send_sem=csend.at[k],
            recv_sem=crecv.at[k],
            device_id=(peer, hour_block),
            device_id_type=MESH,
        )
        carry.start()
        copies.append((copy, carry))
    own.wait()
    own_carry.wait()
    for k in range(1, nb):
        copies[k - 1][0].wait_send()
        copies[k - 1][1].wait_send()
        source = lax.rem(me + nb - k, nb)
        pltpu.make_async_remote_copy(
            src_ref=x_ref.at[source],
            dst_ref=landed.at[source],
            send_sem=send_sem.at[k],
            recv_sem=recv_sem.at[k],
            device_id=(source, hour_block),
            device_id_type=MESH,
        ).wait_recv()
        pltpu.make_async_remote_copy(
            src_ref=c_ref,
            dst_ref=carried.at[pl.ds(source, 1)],
            send_sem=csend.at[k],
            recv_sem=crecv.at[k],
            device_id=(source, hour_block),
            device_id_type=MESH,
        ).wait_recv()
    o_ref[...] = landed[...]
    t_ref[...] = jnp.sum(carried[...], axis=0, keepdims=True)


def as_row(value):
    if value.ndim == 2:
        return value
    return jnp.broadcast_to(value.astype(jnp.float32), (1, LANES))


def basin_exchange(x, carry):
    nb = lax.axis_size("basin")
    total, hours = x.shape
    shaped = x.reshape(nb, total // nb, hours)
    out, summed = pl.pallas_call(
        functools.partial(_exchange_body, nb=nb),
        out_shape=(
            jax.ShapeDtypeStruct(shaped.shape, jnp.float32),
            jax.ShapeDtypeStruct((1, LANES), jnp.float32),
        ),
        in_specs=[pl.BlockSpec(memory_space=pltpu.VMEM)] * 2,
        out_specs=(pl.BlockSpec(memory_space=pltpu.VMEM),) * 2,
        scratch_shapes=[
            pltpu.VMEM(shaped.shape, jnp.float32),
            pltpu.VMEM((nb, LANES), jnp.float32),
            pltpu.SemaphoreType.DMA((2,)),
            pltpu.SemaphoreType.DMA((nb,)),
            pltpu.SemaphoreType.DMA((nb,)),
            pltpu.SemaphoreType.DMA((nb,)),
            pltpu.SemaphoreType.DMA((nb,)),
        ],
        compiler_params=pltpu.CompilerParams(collective_id=1, has_side_effects=True),
    )(shaped, as_row(carry))
    return out.reshape(total, hours), summed


def _shift_body(x_ref, c_ref, o_ref, t_ref, held, carried, own_sem, dsend, drecv, csend, crecv, *, nt, by):
    basin = lax.axis_index("basin")
    me = lax.axis_index("tm")
    barrier = pltpu.get_barrier_semaphore()
    for k in range(1, nt):
        pl.semaphore_signal(
            barrier, inc=1, device_id=(basin, lax.rem(me + k, nt)), device_id_type=MESH
        )
    pl.semaphore_wait(barrier, nt - 1)

    target = me + by
    source = me - by
    has_target = jnp.logical_and(target >= 0, target < nt)
    has_source = jnp.logical_and(source >= 0, source < nt)
    data = pltpu.make_async_remote_copy(
        src_ref=x_ref,
        dst_ref=held,
        send_sem=dsend,
        recv_sem=drecv,
        device_id=(basin, lax.rem(target + nt, nt)),
        device_id_type=MESH,
    )

    @pl.when(has_target)
    def _():
        data.start()

    own = pltpu.make_async_copy(c_ref, carried.at[pl.ds(me, 1)], own_sem)
    own.start()
    copies = []
    for k in range(1, nt):
        copy = pltpu.make_async_remote_copy(
            src_ref=c_ref,
            dst_ref=carried.at[pl.ds(me, 1)],
            send_sem=csend.at[k],
            recv_sem=crecv.at[k],
            device_id=(basin, lax.rem(me + k, nt)),
            device_id_type=MESH,
        )
        copy.start()
        copies.append(copy)
    own.wait()
    for k in range(1, nt):
        copies[k - 1].wait_send()
        origin = lax.rem(me + nt - k, nt)
        pltpu.make_async_remote_copy(
            src_ref=c_ref,
            dst_ref=carried.at[pl.ds(origin, 1)],
            send_sem=csend.at[k],
            recv_sem=crecv.at[k],
            device_id=(basin, origin),
            device_id_type=MESH,
        ).wait_recv()
    t_ref[...] = jnp.sum(carried[...], axis=0, keepdims=True)

    @pl.when(has_target)
    def _():
        data.wait_send()

    @pl.when(has_source)
    def _():
        data.wait_recv()
        o_ref[...] = held[...]

    @pl.when(jnp.logical_not(has_source))
    def _():
        o_ref[...] = jnp.zeros(o_ref.shape, o_ref.dtype)


def tm_shift(x, carry, by, ident):
    nt = lax.axis_size("tm")
    c = as_row(carry)
    out, summed = pl.pallas_call(
        functools.partial(_shift_body, nt=nt, by=by),
        out_shape=(
            jax.ShapeDtypeStruct(x.shape, jnp.float32),
            jax.ShapeDtypeStruct((1, LANES), jnp.float32),
        ),
        in_specs=[pl.BlockSpec(memory_space=pltpu.VMEM)] * 2,
        out_specs=(pl.BlockSpec(memory_space=pltpu.VMEM),) * 2,
        scratch_shapes=[
            pltpu.VMEM(x.shape, jnp.float32),
            pltpu.VMEM((nt, LANES), jnp.float32),
            pltpu.SemaphoreType.DMA(()),
            pltpu.SemaphoreType.DMA(()),
            pltpu.SemaphoreType.DMA(()),
            pltpu.SemaphoreType.DMA((nt,)),
            pltpu.SemaphoreType.DMA((nt,)),
        ],
        compiler_params=pltpu.CompilerParams(collective_id=ident, has_side_effects=True),
    )(x, c)
    return out, summed


def shards(incidence, row_gauge, gauge_kernel, kernels, observed, first_guess):
    weights = incidence.astype(jnp.float32)
    blocks, slots, width = weights.shape
    gauges_here, hours = observed.shape
    owners = lax.axis_size("basin")
    classes = kernels.shape[0]
    partials = blocks * slots
    outer = jnp.arange(2 * hours)[:, None]
    inner = jnp.arange(hours)[None, :]
    table_fwd = lag_table(kernels, inner + hours - outer)
    table_bwd = lag_table(kernels, outer - inner)
    selector = (gauge_kernel[:, None] == jnp.arange(classes)[None, :]).astype(jnp.float32)

    owner = row_gauge // gauges_here
    local = row_gauge % gauges_here
    hit = owner[:, None] == jnp.arange(owners)[None, :]
    rank = jnp.cumsum(hit.astype(jnp.int32), axis=0) - 1
    dest = owner * CAP + jnp.sum(jnp.where(hit, rank, 0), axis=1)
    entries = owners * CAP
    place = (jnp.arange(entries)[:, None] == dest[None, :]).astype(jnp.float32)
    sent_ids = jnp.full((entries,), -1, jnp.int32).at[dest].set(local)
    got_ids = lax.all_to_all(sent_ids, "basin", 0, 0, tiled=True)
    gather = (jnp.arange(gauges_here)[:, None] == got_ids[None, :]).astype(jnp.float32)

    def forward(field):
        partial_value = jnp.einsum(
            "bjr,brt->bjt", weights, field.reshape(blocks, width, hours), precision=HIGH
        )
        outgoing = jnp.dot(place, partial_value.reshape(partials, hours), precision=HIGH)
        incoming, basin_sq = basin_exchange(outgoing, squared(field))
        sums = jnp.dot(gather, incoming, precision=HIGH)
        earlier, total_sq = tm_shift(sums, basin_sq, 1, 2)
        return class_mix(jnp.concatenate([earlier, sums], axis=1), table_fwd, selector), total_sq[0, 0]

    def backward(series):
        later, tm_sq = tm_shift(series, squared(series), -1, 3)
        upstream = class_mix(jnp.concatenate([series, later], axis=1), table_bwd, selector)
        outgoing = jnp.dot(gather.T, upstream, precision=HIGH)
        incoming, total_sq = basin_exchange(outgoing, tm_sq)
        rows = jnp.dot(place.T, incoming, precision=HIGH)
        spread = jnp.einsum(
            "bjr,bjt->brt", weights, rows.reshape(blocks, slots, hours), precision=HIGH
        )
        return spread.reshape(blocks * width, hours), total_sq[0, 0]

    start = observed - forward(first_guess)[0]
    pulled_start, beta_sq = backward(start)
    beta = jnp.sqrt(beta_sq)
    u = start / beta
    pulled = pulled_start / beta
    forward_pulled, alpha_sq = forward(pulled)
    alpha = jnp.sqrt(alpha_sq)
    v = pulled / alpha
    w = v
    correction = jnp.zeros(first_guess.shape, jnp.float32)
    phibar = beta
    rhobar = alpha
    for step in range(ITERS):
        final = step == ITERS - 1
        p = forward_pulled / alpha - alpha * u
        if final:
            beta = jnp.sqrt(global_total(squared(p)))
        else:
            pulled_p, beta_sq = backward(p)
            beta = jnp.sqrt(beta_sq)
            pulled = pulled_p / beta - beta * v
            forward_pulled, alpha_next = forward(pulled)
            alpha_next = jnp.sqrt(alpha_next)
            v_next = pulled / alpha_next
        u = p / beta
        rho = jnp.sqrt(rhobar * rhobar + beta * beta)
        cosine = rhobar / rho
        sine = beta / rho
        phi = cosine * phibar
        phibar = sine * phibar
        correction = correction + phi / rho * w
        if not final:
            theta = sine * alpha_next
            rhobar = -cosine * alpha_next
            w = v_next - theta / rho * w
            v = v_next
            alpha = alpha_next
    return first_guess + correction


def solution(mesh):
    in_specs = (
        P("basin", None, None),
        P("basin"),
        P("basin"),
        P(),
        P("basin", "tm"),
        P("basin", "tm"),
    )
    out_specs = P("basin", "tm")
    return jax.shard_map(shards, mesh=mesh, in_specs=in_specs, out_specs=out_specs, check_vma=False)
```

```python
import functools

import jax
import jax.numpy as jnp
from jax import lax
from jax.experimental import pallas as pl
from jax.experimental.pallas import tpu as pltpu
from jax.sharding import PartitionSpec as P

ITERS = 3
CAP = 32
LANES = 128

HIGH = lax.Precision.HIGHEST
MESH = pl.DeviceIdType.MESH


def from_behind(x, axis, by):
    devices = lax.axis_size(axis)
    pairs = [(i, i + by) for i in range(devices) if 0 <= i + by < devices]
    return lax.ppermute(x, axis, pairs)


def lag_table(kernels, lag):
    classes, taps = kernels.shape
    rows, hours = lag.shape
    onehot = (lag[None, :, :] == jnp.arange(taps)[:, None, None]).astype(jnp.float32)
    picked = jnp.dot(kernels, onehot.reshape(taps, rows * hours), precision=HIGH)
    picked = picked.reshape(classes, rows, hours)
    return jnp.transpose(picked, (1, 0, 2)).reshape(rows, classes * hours)


def class_mix(extended, table, selector):
    gauges = extended.shape[0]
    classes = selector.shape[1]
    spread = jnp.dot(extended, table, precision=lax.Precision.HIGH).reshape(gauges, classes, -1)
    return jnp.sum(spread * selector[:, :, None], axis=1)


def squared(values):
    return jnp.sum(values * values)


def _total_body(x_ref, o_ref, landed, own_sem, send_sem, recv_sem, *, nb, nt):
    n = nb * nt
    me = lax.axis_index("basin") * nt + lax.axis_index("tm")

    def device(index):
        return (index // nt, index % nt)

    barrier = pltpu.get_barrier_semaphore()
    for k in range(1, n):
        pl.semaphore_signal(barrier, inc=1, device_id=device(lax.rem(me + k, n)), device_id_type=MESH)
    pl.semaphore_wait(barrier, n - 1)

    own = pltpu.make_async_copy(x_ref, landed.at[pl.ds(me, 1)], own_sem)
    own.start()
    copies = []
    for k in range(1, n):
        copy = pltpu.make_async_remote_copy(
            src_ref=x_ref,
            dst_ref=landed.at[pl.ds(me, 1)],
            send_sem=send_sem.at[k],
            recv_sem=recv_sem.at[k],
            device_id=device(lax.rem(me + k, n)),
            device_id_type=MESH,
        )
        copy.start()
        copies.append(copy)
    own.wait()
    for k in range(1, n):
        copies[k - 1].wait_send()
        origin = lax.rem(me + n - k, n)
        pltpu.make_async_remote_copy(
            src_ref=x_ref,
            dst_ref=landed.at[pl.ds(origin, 1)],
            send_sem=send_sem.at[k],
            recv_sem=recv_sem.at[k],
            device_id=device(origin),
            device_id_type=MESH,
        ).wait_recv()
    o_ref[...] = jnp.sum(landed[...], axis=0, keepdims=True)


def global_total(value):
    nb = lax.axis_size("basin")
    nt = lax.axis_size("tm")
    n = nb * nt
    x = jnp.broadcast_to(value.astype(jnp.float32), (1, LANES))
    out = pl.pallas_call(
        functools.partial(_total_body, nb=nb, nt=nt),
        out_shape=jax.ShapeDtypeStruct((1, LANES), jnp.float32),
        in_specs=[pl.BlockSpec(memory_space=pltpu.VMEM)],
        out_specs=pl.BlockSpec(memory_space=pltpu.VMEM),
        scratch_shapes=[
            pltpu.VMEM((n, LANES), jnp.float32),
            pltpu.SemaphoreType.DMA(()),
            pltpu.SemaphoreType.DMA((n,)),
            pltpu.SemaphoreType.DMA((n,)),
        ],
        compiler_params=pltpu.CompilerParams(collective_id=0, has_side_effects=True),
    )(x)
    return out[0, 0]


def _exchange_body(x_ref, c_ref, o_ref, t_ref, landed, carried, own_sem, send_sem, recv_sem, csend, crecv, *, nb):
    me = lax.axis_index("basin")
    hour_block = lax.axis_index("tm")
    barrier = pltpu.get_barrier_semaphore()
    for k in range(1, nb):
        pl.semaphore_signal(
            barrier, inc=1, device_id=(lax.rem(me + k, nb), hour_block), device_id_type=MESH
        )
    pl.semaphore_wait(barrier, nb - 1)
    own = pltpu.make_async_copy(x_ref.at[me], landed.at[me], own_sem.at[0])
    own.start()
    own_carry = pltpu.make_async_copy(c_ref, carried.at[pl.ds(me, 1)], own_sem.at[1])
    own_carry.start()
    copies = []
    for k in range(1, nb):
        peer = lax.rem(me + k, nb)
        copy = pltpu.make_async_remote_copy(
            src_ref=x_ref.at[peer],
            dst_ref=landed.at[me],
            send_sem=send_sem.at[k],
            recv_sem=recv_sem.at[k],
            device_id=(peer, hour_block),
            device_id_type=MESH,
        )
        copy.start()
        carry = pltpu.make_async_remote_copy(
            src_ref=c_ref,
            dst_ref=carried.at[pl.ds(me, 1)],
            send_sem=csend.at[k],
            recv_sem=crecv.at[k],
            device_id=(peer, hour_block),
            device_id_type=MESH,
        )
        carry.start()
        copies.append((copy, carry))
    own.wait()
    own_carry.wait()
    for k in range(1, nb):
        copies[k - 1][0].wait_send()
        copies[k - 1][1].wait_send()
        source = lax.rem(me + nb - k, nb)
        pltpu.make_async_remote_copy(
            src_ref=x_ref.at[source],
            dst_ref=landed.at[source],
            send_sem=send_sem.at[k],
            recv_sem=recv_sem.at[k],
            device_id=(source, hour_block),
            device_id_type=MESH,
        ).wait_recv()
        pltpu.make_async_remote_copy(
            src_ref=c_ref,
            dst_ref=carried.at[pl.ds(source, 1)],
            send_sem=csend.at[k],
            recv_sem=crecv.at[k],
            device_id=(source, hour_block),
            device_id_type=MESH,
        ).wait_recv()
    o_ref[...] = landed[...]
    t_ref[...] = jnp.sum(carried[...], axis=0, keepdims=True)


def as_row(value):
    if value.ndim == 2:
        return value
    return jnp.broadcast_to(value.astype(jnp.float32), (1, LANES))


def basin_exchange(x, carry):
    nb = lax.axis_size("basin")
    total, hours = x.shape
    shaped = x.reshape(nb, total // nb, hours)
    out, summed = pl.pallas_call(
        functools.partial(_exchange_body, nb=nb),
        out_shape=(
            jax.ShapeDtypeStruct(shaped.shape, jnp.float32),
            jax.ShapeDtypeStruct((1, LANES), jnp.float32),
        ),
        in_specs=[pl.BlockSpec(memory_space=pltpu.VMEM)] * 2,
        out_specs=(pl.BlockSpec(memory_space=pltpu.VMEM),) * 2,
        scratch_shapes=[
            pltpu.VMEM(shaped.shape, jnp.float32),
            pltpu.VMEM((nb, LANES), jnp.float32),
            pltpu.SemaphoreType.DMA((2,)),
            pltpu.SemaphoreType.DMA((nb,)),
            pltpu.SemaphoreType.DMA((nb,)),
            pltpu.SemaphoreType.DMA((nb,)),
            pltpu.SemaphoreType.DMA((nb,)),
        ],
        compiler_params=pltpu.CompilerParams(collective_id=1, has_side_effects=True),
    )(shaped, as_row(carry))
    return out.reshape(total, hours), summed


def _shift_body(x_ref, c_ref, o_ref, t_ref, held, carried, own_sem, dsend, drecv, csend, crecv, *, nt, by):
    basin = lax.axis_index("basin")
    me = lax.axis_index("tm")
    barrier = pltpu.get_barrier_semaphore()
    for k in range(1, nt):
        pl.semaphore_signal(
            barrier, inc=1, device_id=(basin, lax.rem(me + k, nt)), device_id_type=MESH
        )
    pl.semaphore_wait(barrier, nt - 1)

    target = me + by
    source = me - by
    has_target = jnp.logical_and(target >= 0, target < nt)
    has_source = jnp.logical_and(source >= 0, source < nt)
    data = pltpu.make_async_remote_copy(
        src_ref=x_ref,
        dst_ref=held,
        send_sem=dsend,
        recv_sem=drecv,
        device_id=(basin, lax.rem(target + nt, nt)),
        device_id_type=MESH,
    )

    @pl.when(has_target)
    def _():
        data.start()

    own = pltpu.make_async_copy(c_ref, carried.at[pl.ds(me, 1)], own_sem)
    own.start()
    copies = []
    for k in range(1, nt):
        copy = pltpu.make_async_remote_copy(
            src_ref=c_ref,
            dst_ref=carried.at[pl.ds(me, 1)],
            send_sem=csend.at[k],
            recv_sem=crecv.at[k],
            device_id=(basin, lax.rem(me + k, nt)),
            device_id_type=MESH,
        )
        copy.start()
        copies.append(copy)
    own.wait()
    for k in range(1, nt):
        copies[k - 1].wait_send()
        origin = lax.rem(me + nt - k, nt)
        pltpu.make_async_remote_copy(
            src_ref=c_ref,
            dst_ref=carried.at[pl.ds(origin, 1)],
            send_sem=csend.at[k],
            recv_sem=crecv.at[k],
            device_id=(basin, origin),
            device_id_type=MESH,
        ).wait_recv()
    t_ref[...] = jnp.sum(carried[...], axis=0, keepdims=True)

    @pl.when(has_target)
    def _():
        data.wait_send()

    @pl.when(has_source)
    def _():
        data.wait_recv()
        o_ref[...] = held[...]

    @pl.when(jnp.logical_not(has_source))
    def _():
        o_ref[...] = jnp.zeros(o_ref.shape, o_ref.dtype)


def tm_shift(x, carry, by, ident):
    nt = lax.axis_size("tm")
    c = as_row(carry)
    out, summed = pl.pallas_call(
        functools.partial(_shift_body, nt=nt, by=by),
        out_shape=(
            jax.ShapeDtypeStruct(x.shape, jnp.float32),
            jax.ShapeDtypeStruct((1, LANES), jnp.float32),
        ),
        in_specs=[pl.BlockSpec(memory_space=pltpu.VMEM)] * 2,
        out_specs=(pl.BlockSpec(memory_space=pltpu.VMEM),) * 2,
        scratch_shapes=[
            pltpu.VMEM(x.shape, jnp.float32),
            pltpu.VMEM((nt, LANES), jnp.float32),
            pltpu.SemaphoreType.DMA(()),
            pltpu.SemaphoreType.DMA(()),
            pltpu.SemaphoreType.DMA(()),
            pltpu.SemaphoreType.DMA((nt,)),
            pltpu.SemaphoreType.DMA((nt,)),
        ],
        compiler_params=pltpu.CompilerParams(collective_id=ident, has_side_effects=True),
    )(x, c)
    return out, summed


def shards(incidence, row_gauge, gauge_kernel, kernels, observed, first_guess):
    weights = incidence.astype(jnp.float32)
    blocks, slots, width = weights.shape
    gauges_here, hours = observed.shape
    owners = lax.axis_size("basin")
    classes = kernels.shape[0]
    partials = blocks * slots
    outer = jnp.arange(2 * hours)[:, None]
    inner = jnp.arange(hours)[None, :]
    table_fwd = lag_table(kernels, inner + hours - outer)
    table_bwd = lag_table(kernels, outer - inner)
    selector = (gauge_kernel[:, None] == jnp.arange(classes)[None, :]).astype(jnp.float32)

    owner = row_gauge // gauges_here
    local = row_gauge % gauges_here
    hit = owner[:, None] == jnp.arange(owners)[None, :]
    rank = jnp.cumsum(hit.astype(jnp.int32), axis=0) - 1
    dest = owner * CAP + jnp.sum(jnp.where(hit, rank, 0), axis=1)
    entries = owners * CAP
    place = (jnp.arange(entries)[:, None] == dest[None, :]).astype(jnp.float32)
    sent_ids = jnp.full((entries,), -1, jnp.int32).at[dest].set(local)
    got_ids = lax.all_to_all(sent_ids, "basin", 0, 0, tiled=True)
    gather = (jnp.arange(gauges_here)[:, None] == got_ids[None, :]).astype(jnp.float32)

    def forward(field):
        partial_value = jnp.einsum(
            "bjr,brt->bjt", weights, field.reshape(blocks, width, hours), precision=HIGH
        )
        outgoing = jnp.dot(place, partial_value.reshape(partials, hours), precision=HIGH)
        incoming, basin_sq = basin_exchange(outgoing, squared(field))
        sums = jnp.dot(gather, incoming, precision=HIGH)
        earlier, total_sq = tm_shift(sums, basin_sq, 1, 2)
        return class_mix(jnp.concatenate([earlier, sums], axis=1), table_fwd, selector), total_sq[0, 0]

    def backward(series):
        later, tm_sq = tm_shift(series, squared(series), -1, 3)
        upstream = class_mix(jnp.concatenate([series, later], axis=1), table_bwd, selector)
        outgoing = jnp.dot(gather.T, upstream, precision=lax.Precision.HIGH)
        incoming, total_sq = basin_exchange(outgoing, tm_sq)
        rows = jnp.dot(place.T, incoming, precision=lax.Precision.HIGH)
        spread = jnp.einsum(
            "bjr,bjt->brt", weights, rows.reshape(blocks, slots, hours), precision=lax.Precision.HIGH
        )
        return spread.reshape(blocks * width, hours), total_sq[0, 0]

    start = observed - forward(first_guess)[0]
    pulled_start, beta_sq = backward(start)
    beta = jnp.sqrt(beta_sq)
    u = start / beta
    pulled = pulled_start / beta
    forward_pulled, alpha_sq = forward(pulled)
    alpha = jnp.sqrt(alpha_sq)
    v = pulled / alpha
    w = v
    correction = jnp.zeros(first_guess.shape, jnp.float32)
    phibar = beta
    rhobar = alpha
    for step in range(ITERS):
        final = step == ITERS - 1
        p = forward_pulled / alpha - alpha * u
        if final:
            beta = jnp.sqrt(global_total(squared(p)))
        else:
            pulled_p, beta_sq = backward(p)
            beta = jnp.sqrt(beta_sq)
            pulled = pulled_p / beta - beta * v
            forward_pulled, alpha_next = forward(pulled)
            alpha_next = jnp.sqrt(alpha_next)
            v_next = pulled / alpha_next
        u = p / beta
        rho = jnp.sqrt(rhobar * rhobar + beta * beta)
        cosine = rhobar / rho
        sine = beta / rho
        phi = cosine * phibar
        phibar = sine * phibar
        correction = correction + phi / rho * w
        if not final:
            theta = sine * alpha_next
            rhobar = -cosine * alpha_next
            w = v_next - theta / rho * w
            v = v_next
            alpha = alpha_next
    return first_guess + correction


def solution(mesh):
    in_specs = (
        P("basin", None, None),
        P("basin"),
        P("basin"),
        P(),
        P("basin", "tm"),
        P("basin", "tm"),
    )
    out_specs = P("basin", "tm")
    return jax.shard_map(shards, mesh=mesh, in_specs=in_specs, out_specs=out_specs, check_vma=False)
```

```python
import functools

import jax
import jax.numpy as jnp
from jax import lax
from jax.experimental import pallas as pl
from jax.experimental.pallas import tpu as pltpu
from jax.sharding import PartitionSpec as P

ITERS = 3
CAP = 32
LANES = 128

HIGH = lax.Precision.HIGHEST
MESH = pl.DeviceIdType.MESH


def from_behind(x, axis, by):
    devices = lax.axis_size(axis)
    pairs = [(i, i + by) for i in range(devices) if 0 <= i + by < devices]
    return lax.ppermute(x, axis, pairs)


def lag_table(kernels, lag):
    classes, taps = kernels.shape
    rows, hours = lag.shape
    onehot = (lag[None, :, :] == jnp.arange(taps)[:, None, None]).astype(jnp.float32)
    picked = jnp.dot(kernels, onehot.reshape(taps, rows * hours), precision=HIGH)
    picked = picked.reshape(classes, rows, hours)
    return jnp.transpose(picked, (1, 0, 2)).reshape(rows, classes * hours)


def class_mix(extended, table, selector):
    gauges = extended.shape[0]
    classes = selector.shape[1]
    spread = jnp.dot(extended, table, precision=lax.Precision.HIGH).reshape(gauges, classes, -1)
    return jnp.sum(spread * selector[:, :, None], axis=1)


def squared(values):
    return jnp.sum(values * values)


def _total_body(x_ref, o_ref, landed, own_sem, send_sem, recv_sem, *, nb, nt):
    n = nb * nt
    me = lax.axis_index("basin") * nt + lax.axis_index("tm")

    def device(index):
        return (index // nt, index % nt)

    barrier = pltpu.get_barrier_semaphore()
    for k in range(1, n):
        pl.semaphore_signal(barrier, inc=1, device_id=device(lax.rem(me + k, n)), device_id_type=MESH)
    pl.semaphore_wait(barrier, n - 1)

    own = pltpu.make_async_copy(x_ref, landed.at[pl.ds(me, 1)], own_sem)
    own.start()
    copies = []
    for k in range(1, n):
        copy = pltpu.make_async_remote_copy(
            src_ref=x_ref,
            dst_ref=landed.at[pl.ds(me, 1)],
            send_sem=send_sem.at[k],
            recv_sem=recv_sem.at[k],
            device_id=device(lax.rem(me + k, n)),
            device_id_type=MESH,
        )
        copy.start()
        copies.append(copy)
    own.wait()
    for k in range(1, n):
        copies[k - 1].wait_send()
        origin = lax.rem(me + n - k, n)
        pltpu.make_async_remote_copy(
            src_ref=x_ref,
            dst_ref=landed.at[pl.ds(origin, 1)],
            send_sem=send_sem.at[k],
            recv_sem=recv_sem.at[k],
            device_id=device(origin),
            device_id_type=MESH,
        ).wait_recv()
    o_ref[...] = jnp.sum(landed[...], axis=0, keepdims=True)


def global_total(value):
    nb = lax.axis_size("basin")
    nt = lax.axis_size("tm")
    n = nb * nt
    x = jnp.broadcast_to(value.astype(jnp.float32), (1, LANES))
    out = pl.pallas_call(
        functools.partial(_total_body, nb=nb, nt=nt),
        out_shape=jax.ShapeDtypeStruct((1, LANES), jnp.float32),
        in_specs=[pl.BlockSpec(memory_space=pltpu.VMEM)],
        out_specs=pl.BlockSpec(memory_space=pltpu.VMEM),
        scratch_shapes=[
            pltpu.VMEM((n, LANES), jnp.float32),
            pltpu.SemaphoreType.DMA(()),
            pltpu.SemaphoreType.DMA((n,)),
            pltpu.SemaphoreType.DMA((n,)),
        ],
        compiler_params=pltpu.CompilerParams(collective_id=0, has_side_effects=True),
    )(x)
    return out[0, 0]


def _exchange_body(x_ref, c_ref, o_ref, t_ref, landed, carried, own_sem, send_sem, recv_sem, csend, crecv, *, nb):
    me = lax.axis_index("basin")
    hour_block = lax.axis_index("tm")
    barrier = pltpu.get_barrier_semaphore()
    for k in range(1, nb):
        pl.semaphore_signal(
            barrier, inc=1, device_id=(lax.rem(me + k, nb), hour_block), device_id_type=MESH
        )
    pl.semaphore_wait(barrier, nb - 1)
    own = pltpu.make_async_copy(x_ref.at[me], landed.at[me], own_sem.at[0])
    own.start()
    own_carry = pltpu.make_async_copy(c_ref, carried.at[pl.ds(me, 1)], own_sem.at[1])
    own_carry.start()
    copies = []
    for k in range(1, nb):
        peer = lax.rem(me + k, nb)
        copy = pltpu.make_async_remote_copy(
            src_ref=x_ref.at[peer],
            dst_ref=landed.at[me],
            send_sem=send_sem.at[k],
            recv_sem=recv_sem.at[k],
            device_id=(peer, hour_block),
            device_id_type=MESH,
        )
        copy.start()
        carry = pltpu.make_async_remote_copy(
            src_ref=c_ref,
            dst_ref=carried.at[pl.ds(me, 1)],
            send_sem=csend.at[k],
            recv_sem=crecv.at[k],
            device_id=(peer, hour_block),
            device_id_type=MESH,
        )
        carry.start()
        copies.append((copy, carry))
    own.wait()
    own_carry.wait()
    for k in range(1, nb):
        copies[k - 1][0].wait_send()
        copies[k - 1][1].wait_send()
        source = lax.rem(me + nb - k, nb)
        pltpu.make_async_remote_copy(
            src_ref=x_ref.at[source],
            dst_ref=landed.at[source],
            send_sem=send_sem.at[k],
            recv_sem=recv_sem.at[k],
            device_id=(source, hour_block),
            device_id_type=MESH,
        ).wait_recv()
        pltpu.make_async_remote_copy(
            src_ref=c_ref,
            dst_ref=carried.at[pl.ds(source, 1)],
            send_sem=csend.at[k],
            recv_sem=crecv.at[k],
            device_id=(source, hour_block),
            device_id_type=MESH,
        ).wait_recv()
    o_ref[...] = landed[...]
    t_ref[...] = jnp.sum(carried[...], axis=0, keepdims=True)


def as_row(value):
    if value.ndim == 2:
        return value
    return jnp.broadcast_to(value.astype(jnp.float32), (1, LANES))


def basin_exchange(x, carry):
    nb = lax.axis_size("basin")
    total, hours = x.shape
    shaped = x.reshape(nb, total // nb, hours)
    out, summed = pl.pallas_call(
        functools.partial(_exchange_body, nb=nb),
        out_shape=(
            jax.ShapeDtypeStruct(shaped.shape, jnp.float32),
            jax.ShapeDtypeStruct((1, LANES), jnp.float32),
        ),
        in_specs=[pl.BlockSpec(memory_space=pltpu.VMEM)] * 2,
        out_specs=(pl.BlockSpec(memory_space=pltpu.VMEM),) * 2,
        scratch_shapes=[
            pltpu.VMEM(shaped.shape, jnp.float32),
            pltpu.VMEM((nb, LANES), jnp.float32),
            pltpu.SemaphoreType.DMA((2,)),
            pltpu.SemaphoreType.DMA((nb,)),
            pltpu.SemaphoreType.DMA((nb,)),
            pltpu.SemaphoreType.DMA((nb,)),
            pltpu.SemaphoreType.DMA((nb,)),
        ],
        compiler_params=pltpu.CompilerParams(collective_id=1, has_side_effects=True),
    )(shaped, as_row(carry))
    return out.reshape(total, hours), summed


def _forward_body(x_ref, c_ref, o_ref, prev_ref, t_ref, landed, before, carried, gathered,
                  own_sem, send_sem, recv_sem, csend, crecv, fsend, frecv, gsend, grecv, *, nb, nt):
    me = lax.axis_index("basin")
    hb = lax.axis_index("tm")
    has_next = hb + 1 < nt
    has_prev = hb > 0
    nxt = lax.rem(hb + 1, nt)
    barrier = pltpu.get_barrier_semaphore()
    for k in range(1, nb):
        pl.semaphore_signal(barrier, inc=1, device_id=(lax.rem(me + k, nb), hb), device_id_type=MESH)
    for j in range(1, nt):
        pl.semaphore_signal(barrier, inc=1, device_id=(me, lax.rem(hb + j, nt)), device_id_type=MESH)
    pl.semaphore_wait(barrier, nb - 1 + nt - 1)

    own = pltpu.make_async_copy(x_ref.at[me], landed.at[me], own_sem.at[0])
    own.start()
    own_carry = pltpu.make_async_copy(c_ref, carried.at[pl.ds(me, 1)], own_sem.at[1])
    own_carry.start()
    copies = []
    for k in range(1, nb):
        peer = lax.rem(me + k, nb)
        copy = pltpu.make_async_remote_copy(
            src_ref=x_ref.at[peer], dst_ref=landed.at[me], send_sem=send_sem.at[k],
            recv_sem=recv_sem.at[k], device_id=(peer, hb), device_id_type=MESH,
        )
        copy.start()
        carry = pltpu.make_async_remote_copy(
            src_ref=c_ref, dst_ref=carried.at[pl.ds(me, 1)], send_sem=csend.at[k],
            recv_sem=crecv.at[k], device_id=(peer, hb), device_id_type=MESH,
        )
        carry.start()
        copies.append((copy, carry))

    def forwarded(k, source):
        return pltpu.make_async_remote_copy(
            src_ref=landed.at[source], dst_ref=before.at[source], send_sem=fsend.at[k],
            recv_sem=frecv.at[k], device_id=(me, nxt), device_id_type=MESH,
        )

    own.wait()

    @pl.when(has_next)
    def _():
        forwarded(0, me).start()

    for k in range(1, nb):
        source = lax.rem(me + nb - k, nb)
        pltpu.make_async_remote_copy(
            src_ref=x_ref.at[source], dst_ref=landed.at[source], send_sem=send_sem.at[k],
            recv_sem=recv_sem.at[k], device_id=(source, hb), device_id_type=MESH,
        ).wait_recv()

        @pl.when(has_next)
        def _():
            forwarded(k, source).start()

    own_carry.wait()
    for k in range(1, nb):
        source = lax.rem(me + nb - k, nb)
        pltpu.make_async_remote_copy(
            src_ref=c_ref, dst_ref=carried.at[pl.ds(source, 1)], send_sem=csend.at[k],
            recv_sem=crecv.at[k], device_id=(source, hb), device_id_type=MESH,
        ).wait_recv()
    own_group = pltpu.make_async_copy(carried, gathered.at[hb], own_sem.at[2])
    own_group.start()
    groups = []
    for j in range(1, nt):
        group = pltpu.make_async_remote_copy(
            src_ref=carried, dst_ref=gathered.at[hb], send_sem=gsend.at[j], recv_sem=grecv.at[j],
            device_id=(me, lax.rem(hb + j, nt)), device_id_type=MESH,
        )
        group.start()
        groups.append(group)

    for k in range(1, nb):
        copies[k - 1][0].wait_send()
        copies[k - 1][1].wait_send()
    own_group.wait()
    for j in range(1, nt):
        groups[j - 1].wait_send()
        origin = lax.rem(hb + nt - j, nt)
        pltpu.make_async_remote_copy(
            src_ref=carried, dst_ref=gathered.at[origin], send_sem=gsend.at[j], recv_sem=grecv.at[j],
            device_id=(me, origin), device_id_type=MESH,
        ).wait_recv()

    @pl.when(has_next)
    def _():
        for k in range(nb):
            forwarded(k, lax.rem(me + nb - k, nb)).wait_send()

    @pl.when(has_prev)
    def _():
        for k in range(nb):
            forwarded(k, lax.rem(me + nb - k, nb)).wait_recv()
        prev_ref[...] = before[...]

    @pl.when(jnp.logical_not(has_prev))
    def _():
        prev_ref[...] = jnp.zeros(prev_ref.shape, prev_ref.dtype)

    o_ref[...] = landed[...]
    t_ref[...] = jnp.sum(gathered[...].reshape(nt * nb, LANES), axis=0, keepdims=True)


def forward_exchange(x, carry):
    nb = lax.axis_size("basin")
    nt = lax.axis_size("tm")
    total, hours = x.shape
    shaped = x.reshape(nb, total // nb, hours)
    out, prev, summed = pl.pallas_call(
        functools.partial(_forward_body, nb=nb, nt=nt),
        out_shape=(
            jax.ShapeDtypeStruct(shaped.shape, jnp.float32),
            jax.ShapeDtypeStruct(shaped.shape, jnp.float32),
            jax.ShapeDtypeStruct((1, LANES), jnp.float32),
        ),
        in_specs=[pl.BlockSpec(memory_space=pltpu.VMEM)] * 2,
        out_specs=(pl.BlockSpec(memory_space=pltpu.VMEM),) * 3,
        scratch_shapes=[
            pltpu.VMEM(shaped.shape, jnp.float32),
            pltpu.VMEM(shaped.shape, jnp.float32),
            pltpu.VMEM((nb, LANES), jnp.float32),
            pltpu.VMEM((nt, nb, LANES), jnp.float32),
            pltpu.SemaphoreType.DMA((3,)),
            pltpu.SemaphoreType.DMA((nb,)),
            pltpu.SemaphoreType.DMA((nb,)),
            pltpu.SemaphoreType.DMA((nb,)),
            pltpu.SemaphoreType.DMA((nb,)),
            pltpu.SemaphoreType.DMA((nb,)),
            pltpu.SemaphoreType.DMA((nb,)),
            pltpu.SemaphoreType.DMA((nt,)),
            pltpu.SemaphoreType.DMA((nt,)),
        ],
        compiler_params=pltpu.CompilerParams(collective_id=4, has_side_effects=True),
    )(shaped, as_row(carry))
    return out.reshape(total, hours), prev.reshape(total, hours), summed


def _shift_body(x_ref, c_ref, o_ref, t_ref, held, carried, own_sem, dsend, drecv, csend, crecv, *, nt, by):
    basin = lax.axis_index("basin")
    me = lax.axis_index("tm")
    barrier = pltpu.get_barrier_semaphore()
    for k in range(1, nt):
        pl.semaphore_signal(
            barrier, inc=1, device_id=(basin, lax.rem(me + k, nt)), device_id_type=MESH
        )
    pl.semaphore_wait(barrier, nt - 1)

    target = me + by
    source = me - by
    has_target = jnp.logical_and(target >= 0, target < nt)
    has_source = jnp.logical_and(source >= 0, source < nt)
    data = pltpu.make_async_remote_copy(
        src_ref=x_ref,
        dst_ref=held,
        send_sem=dsend,
        recv_sem=drecv,
        device_id=(basin, lax.rem(target + nt, nt)),
        device_id_type=MESH,
    )

    @pl.when(has_target)
    def _():
        data.start()

    own = pltpu.make_async_copy(c_ref, carried.at[pl.ds(me, 1)], own_sem)
    own.start()
    copies = []
    for k in range(1, nt):
        copy = pltpu.make_async_remote_copy(
            src_ref=c_ref,
            dst_ref=carried.at[pl.ds(me, 1)],
            send_sem=csend.at[k],
            recv_sem=crecv.at[k],
            device_id=(basin, lax.rem(me + k, nt)),
            device_id_type=MESH,
        )
        copy.start()
        copies.append(copy)
    own.wait()
    for k in range(1, nt):
        copies[k - 1].wait_send()
        origin = lax.rem(me + nt - k, nt)
        pltpu.make_async_remote_copy(
            src_ref=c_ref,
            dst_ref=carried.at[pl.ds(origin, 1)],
            send_sem=csend.at[k],
            recv_sem=crecv.at[k],
            device_id=(basin, origin),
            device_id_type=MESH,
        ).wait_recv()
    t_ref[...] = jnp.sum(carried[...], axis=0, keepdims=True)

    @pl.when(has_target)
    def _():
        data.wait_send()

    @pl.when(has_source)
    def _():
        data.wait_recv()
        o_ref[...] = held[...]

    @pl.when(jnp.logical_not(has_source))
    def _():
        o_ref[...] = jnp.zeros(o_ref.shape, o_ref.dtype)


def tm_shift(x, carry, by, ident):
    nt = lax.axis_size("tm")
    c = as_row(carry)
    out, summed = pl.pallas_call(
        functools.partial(_shift_body, nt=nt, by=by),
        out_shape=(
            jax.ShapeDtypeStruct(x.shape, jnp.float32),
            jax.ShapeDtypeStruct((1, LANES), jnp.float32),
        ),
        in_specs=[pl.BlockSpec(memory_space=pltpu.VMEM)] * 2,
        out_specs=(pl.BlockSpec(memory_space=pltpu.VMEM),) * 2,
        scratch_shapes=[
            pltpu.VMEM(x.shape, jnp.float32),
            pltpu.VMEM((nt, LANES), jnp.float32),
            pltpu.SemaphoreType.DMA(()),
            pltpu.SemaphoreType.DMA(()),
            pltpu.SemaphoreType.DMA(()),
            pltpu.SemaphoreType.DMA((nt,)),
            pltpu.SemaphoreType.DMA((nt,)),
        ],
        compiler_params=pltpu.CompilerParams(collective_id=ident, has_side_effects=True),
    )(x, c)
    return out, summed


def shards(incidence, row_gauge, gauge_kernel, kernels, observed, first_guess):
    weights = incidence.astype(jnp.float32)
    blocks, slots, width = weights.shape
    gauges_here, hours = observed.shape
    owners = lax.axis_size("basin")
    classes = kernels.shape[0]
    partials = blocks * slots
    outer = jnp.arange(2 * hours)[:, None]
    inner = jnp.arange(hours)[None, :]
    table_fwd = lag_table(kernels, inner + hours - outer)
    table_bwd = lag_table(kernels, outer - inner)
    selector = (gauge_kernel[:, None] == jnp.arange(classes)[None, :]).astype(jnp.float32)

    owner = row_gauge // gauges_here
    local = row_gauge % gauges_here
    hit = owner[:, None] == jnp.arange(owners)[None, :]
    rank = jnp.cumsum(hit.astype(jnp.int32), axis=0) - 1
    dest = owner * CAP + jnp.sum(jnp.where(hit, rank, 0), axis=1)
    entries = owners * CAP
    place = (jnp.arange(entries)[:, None] == dest[None, :]).astype(jnp.float32)
    sent_ids = jnp.full((entries,), -1, jnp.int32).at[dest].set(local)
    got_ids = lax.all_to_all(sent_ids, "basin", 0, 0, tiled=True)
    gather = (jnp.arange(gauges_here)[:, None] == got_ids[None, :]).astype(jnp.float32)

    def forward(field):
        partial_value = jnp.einsum(
            "bjr,brt->bjt", weights, field.reshape(blocks, width, hours), precision=HIGH
        )
        outgoing = jnp.dot(place, partial_value.reshape(partials, hours), precision=HIGH)
        incoming, previous, total_sq = forward_exchange(outgoing, squared(field))
        extended = jnp.dot(gather, jnp.concatenate([previous, incoming], axis=1), precision=HIGH)
        return class_mix(extended, table_fwd, selector), total_sq[0, 0]

    def backward(series):
        later, tm_sq = tm_shift(series, squared(series), -1, 3)
        upstream = class_mix(jnp.concatenate([series, later], axis=1), table_bwd, selector)
        outgoing = jnp.dot(gather.T, upstream, precision=lax.Precision.HIGH)
        incoming, total_sq = basin_exchange(outgoing, tm_sq)
        rows = jnp.dot(place.T, incoming, precision=lax.Precision.HIGH)
        spread = jnp.einsum(
            "bjr,bjt->brt", weights, rows.reshape(blocks, slots, hours), precision=lax.Precision.HIGH
        )
        return spread.reshape(blocks * width, hours), total_sq[0, 0]

    start = observed - forward(first_guess)[0]
    pulled_start, beta_sq = backward(start)
    beta = jnp.sqrt(beta_sq)
    u = start / beta
    pulled = pulled_start / beta
    forward_pulled, alpha_sq = forward(pulled)
    alpha = jnp.sqrt(alpha_sq)
    v = pulled / alpha
    w = v
    correction = jnp.zeros(first_guess.shape, jnp.float32)
    phibar = beta
    rhobar = alpha
    for step in range(ITERS):
        final = step == ITERS - 1
        p = forward_pulled / alpha - alpha * u
        if final:
            beta = jnp.sqrt(global_total(squared(p)))
        else:
            pulled_p, beta_sq = backward(p)
            beta = jnp.sqrt(beta_sq)
            pulled = pulled_p / beta - beta * v
            forward_pulled, alpha_next = forward(pulled)
            alpha_next = jnp.sqrt(alpha_next)
            v_next = pulled / alpha_next
        u = p / beta
        rho = jnp.sqrt(rhobar * rhobar + beta * beta)
        cosine = rhobar / rho
        sine = beta / rho
        phi = cosine * phibar
        phibar = sine * phibar
        correction = correction + phi / rho * w
        if not final:
            theta = sine * alpha_next
            rhobar = -cosine * alpha_next
            w = v_next - theta / rho * w
            v = v_next
            alpha = alpha_next
    return first_guess + correction


def solution(mesh):
    in_specs = (
        P("basin", None, None),
        P("basin"),
        P("basin"),
        P(),
        P("basin", "tm"),
        P("basin", "tm"),
    )
    out_specs = P("basin", "tm")
    return jax.shard_map(shards, mesh=mesh, in_specs=in_specs, out_specs=out_specs, check_vma=False)
```

```python
import functools

import jax
import jax.numpy as jnp
from jax import lax
from jax.experimental import pallas as pl
from jax.experimental.pallas import tpu as pltpu
from jax.sharding import PartitionSpec as P

ITERS = 3
CAP = 32
LANES = 128

HIGH = lax.Precision.HIGHEST
MESH = pl.DeviceIdType.MESH


def from_behind(x, axis, by):
    devices = lax.axis_size(axis)
    pairs = [(i, i + by) for i in range(devices) if 0 <= i + by < devices]
    return lax.ppermute(x, axis, pairs)


def lag_table(kernels, lag):
    classes, taps = kernels.shape
    rows, hours = lag.shape
    onehot = (lag.T[None, :, :] == jnp.arange(taps)[:, None, None]).astype(jnp.float32)
    picked = jnp.dot(kernels, onehot.reshape(taps, hours * rows), precision=HIGH)
    return picked.reshape(classes, hours, rows)


def class_mix(extended, table, selector):
    spread = lax.dot_general(extended, table, (((1,), (2,)), ((), ())), precision=lax.Precision.HIGH)
    return jnp.sum(spread * selector[:, :, None], axis=1)


def squared(values):
    return jnp.sum(values * values)


def _total_body(x_ref, o_ref, landed, own_sem, send_sem, recv_sem, *, nb, nt):
    n = nb * nt
    me = lax.axis_index("basin") * nt + lax.axis_index("tm")

    def device(index):
        return (index // nt, index % nt)

    barrier = pltpu.get_barrier_semaphore()
    for k in range(1, n):
        pl.semaphore_signal(barrier, inc=1, device_id=device(lax.rem(me + k, n)), device_id_type=MESH)
    pl.semaphore_wait(barrier, n - 1)

    own = pltpu.make_async_copy(x_ref, landed.at[pl.ds(me, 1)], own_sem)
    own.start()
    copies = []
    for k in range(1, n):
        copy = pltpu.make_async_remote_copy(
            src_ref=x_ref,
            dst_ref=landed.at[pl.ds(me, 1)],
            send_sem=send_sem.at[k],
            recv_sem=recv_sem.at[k],
            device_id=device(lax.rem(me + k, n)),
            device_id_type=MESH,
        )
        copy.start()
        copies.append(copy)
    own.wait()
    for k in range(1, n):
        copies[k - 1].wait_send()
        origin = lax.rem(me + n - k, n)
        pltpu.make_async_remote_copy(
            src_ref=x_ref,
            dst_ref=landed.at[pl.ds(origin, 1)],
            send_sem=send_sem.at[k],
            recv_sem=recv_sem.at[k],
            device_id=device(origin),
            device_id_type=MESH,
        ).wait_recv()
    o_ref[...] = jnp.sum(landed[...], axis=0, keepdims=True)


def global_total(value):
    nb = lax.axis_size("basin")
    nt = lax.axis_size("tm")
    n = nb * nt
    x = jnp.broadcast_to(value.astype(jnp.float32), (1, LANES))
    out = pl.pallas_call(
        functools.partial(_total_body, nb=nb, nt=nt),
        out_shape=jax.ShapeDtypeStruct((1, LANES), jnp.float32),
        in_specs=[pl.BlockSpec(memory_space=pltpu.VMEM)],
        out_specs=pl.BlockSpec(memory_space=pltpu.VMEM),
        scratch_shapes=[
            pltpu.VMEM((n, LANES), jnp.float32),
            pltpu.SemaphoreType.DMA(()),
            pltpu.SemaphoreType.DMA((n,)),
            pltpu.SemaphoreType.DMA((n,)),
        ],
        compiler_params=pltpu.CompilerParams(collective_id=0, has_side_effects=True),
    )(x)
    return out[0, 0]


def _exchange_body(x_ref, c_ref, o_ref, t_ref, landed, carried, own_sem, send_sem, recv_sem, csend, crecv, *, nb):
    me = lax.axis_index("basin")
    hour_block = lax.axis_index("tm")
    barrier = pltpu.get_barrier_semaphore()
    for k in range(1, nb):
        pl.semaphore_signal(
            barrier, inc=1, device_id=(lax.rem(me + k, nb), hour_block), device_id_type=MESH
        )
    pl.semaphore_wait(barrier, nb - 1)
    own = pltpu.make_async_copy(x_ref.at[me], landed.at[me], own_sem.at[0])
    own.start()
    own_carry = pltpu.make_async_copy(c_ref, carried.at[pl.ds(me, 1)], own_sem.at[1])
    own_carry.start()
    copies = []
    for k in range(1, nb):
        peer = lax.rem(me + k, nb)
        copy = pltpu.make_async_remote_copy(
            src_ref=x_ref.at[peer],
            dst_ref=landed.at[me],
            send_sem=send_sem.at[k],
            recv_sem=recv_sem.at[k],
            device_id=(peer, hour_block),
            device_id_type=MESH,
        )
        copy.start()
        carry = pltpu.make_async_remote_copy(
            src_ref=c_ref,
            dst_ref=carried.at[pl.ds(me, 1)],
            send_sem=csend.at[k],
            recv_sem=crecv.at[k],
            device_id=(peer, hour_block),
            device_id_type=MESH,
        )
        carry.start()
        copies.append((copy, carry))
    own.wait()
    own_carry.wait()
    for k in range(1, nb):
        copies[k - 1][0].wait_send()
        copies[k - 1][1].wait_send()
        source = lax.rem(me + nb - k, nb)
        pltpu.make_async_remote_copy(
            src_ref=x_ref.at[source],
            dst_ref=landed.at[source],
            send_sem=send_sem.at[k],
            recv_sem=recv_sem.at[k],
            device_id=(source, hour_block),
            device_id_type=MESH,
        ).wait_recv()
        pltpu.make_async_remote_copy(
            src_ref=c_ref,
            dst_ref=carried.at[pl.ds(source, 1)],
            send_sem=csend.at[k],
            recv_sem=crecv.at[k],
            device_id=(source, hour_block),
            device_id_type=MESH,
        ).wait_recv()
    o_ref[...] = landed[...]
    t_ref[...] = jnp.sum(carried[...], axis=0, keepdims=True)


def as_row(value):
    if value.ndim == 2:
        return value
    return jnp.broadcast_to(value.astype(jnp.float32), (1, LANES))


def basin_exchange(x, carry):
    nb = lax.axis_size("basin")
    total, hours = x.shape
    shaped = x.reshape(nb, total // nb, hours)
    out, summed = pl.pallas_call(
        functools.partial(_exchange_body, nb=nb),
        out_shape=(
            jax.ShapeDtypeStruct(shaped.shape, jnp.float32),
            jax.ShapeDtypeStruct((1, LANES), jnp.float32),
        ),
        in_specs=[pl.BlockSpec(memory_space=pltpu.VMEM)] * 2,
        out_specs=(pl.BlockSpec(memory_space=pltpu.VMEM),) * 2,
        scratch_shapes=[
            pltpu.VMEM(shaped.shape, jnp.float32),
            pltpu.VMEM((nb, LANES), jnp.float32),
            pltpu.SemaphoreType.DMA((2,)),
            pltpu.SemaphoreType.DMA((nb,)),
            pltpu.SemaphoreType.DMA((nb,)),
            pltpu.SemaphoreType.DMA((nb,)),
            pltpu.SemaphoreType.DMA((nb,)),
        ],
        compiler_params=pltpu.CompilerParams(collective_id=1, has_side_effects=True),
    )(shaped, as_row(carry))
    return out.reshape(total, hours), summed


def _shift_body(x_ref, c_ref, o_ref, t_ref, held, carried, own_sem, dsend, drecv, csend, crecv, *, nt, by):
    basin = lax.axis_index("basin")
    me = lax.axis_index("tm")
    barrier = pltpu.get_barrier_semaphore()
    for k in range(1, nt):
        pl.semaphore_signal(
            barrier, inc=1, device_id=(basin, lax.rem(me + k, nt)), device_id_type=MESH
        )
    pl.semaphore_wait(barrier, nt - 1)

    target = me + by
    source = me - by
    has_target = jnp.logical_and(target >= 0, target < nt)
    has_source = jnp.logical_and(source >= 0, source < nt)
    data = pltpu.make_async_remote_copy(
        src_ref=x_ref,
        dst_ref=held,
        send_sem=dsend,
        recv_sem=drecv,
        device_id=(basin, lax.rem(target + nt, nt)),
        device_id_type=MESH,
    )

    @pl.when(has_target)
    def _():
        data.start()

    own = pltpu.make_async_copy(c_ref, carried.at[pl.ds(me, 1)], own_sem)
    own.start()
    copies = []
    for k in range(1, nt):
        copy = pltpu.make_async_remote_copy(
            src_ref=c_ref,
            dst_ref=carried.at[pl.ds(me, 1)],
            send_sem=csend.at[k],
            recv_sem=crecv.at[k],
            device_id=(basin, lax.rem(me + k, nt)),
            device_id_type=MESH,
        )
        copy.start()
        copies.append(copy)
    own.wait()
    for k in range(1, nt):
        copies[k - 1].wait_send()
        origin = lax.rem(me + nt - k, nt)
        pltpu.make_async_remote_copy(
            src_ref=c_ref,
            dst_ref=carried.at[pl.ds(origin, 1)],
            send_sem=csend.at[k],
            recv_sem=crecv.at[k],
            device_id=(basin, origin),
            device_id_type=MESH,
        ).wait_recv()
    t_ref[...] = jnp.sum(carried[...], axis=0, keepdims=True)

    @pl.when(has_target)
    def _():
        data.wait_send()

    @pl.when(has_source)
    def _():
        data.wait_recv()
        o_ref[...] = held[...]

    @pl.when(jnp.logical_not(has_source))
    def _():
        o_ref[...] = jnp.zeros(o_ref.shape, o_ref.dtype)


def tm_shift(x, carry, by, ident):
    nt = lax.axis_size("tm")
    c = as_row(carry)
    out, summed = pl.pallas_call(
        functools.partial(_shift_body, nt=nt, by=by),
        out_shape=(
            jax.ShapeDtypeStruct(x.shape, jnp.float32),
            jax.ShapeDtypeStruct((1, LANES), jnp.float32),
        ),
        in_specs=[pl.BlockSpec(memory_space=pltpu.VMEM)] * 2,
        out_specs=(pl.BlockSpec(memory_space=pltpu.VMEM),) * 2,
        scratch_shapes=[
            pltpu.VMEM(x.shape, jnp.float32),
            pltpu.VMEM((nt, LANES), jnp.float32),
            pltpu.SemaphoreType.DMA(()),
            pltpu.SemaphoreType.DMA(()),
            pltpu.SemaphoreType.DMA(()),
            pltpu.SemaphoreType.DMA((nt,)),
            pltpu.SemaphoreType.DMA((nt,)),
        ],
        compiler_params=pltpu.CompilerParams(collective_id=ident, has_side_effects=True),
    )(x, c)
    return out, summed


def shards(incidence, row_gauge, gauge_kernel, kernels, observed, first_guess):
    weights = incidence.astype(jnp.float32)
    blocks, slots, width = weights.shape
    gauges_here, hours = observed.shape
    owners = lax.axis_size("basin")
    classes = kernels.shape[0]
    partials = blocks * slots
    outer = jnp.arange(2 * hours)[:, None]
    inner = jnp.arange(hours)[None, :]
    table_fwd = lag_table(kernels, inner + hours - outer)
    table_bwd = lag_table(kernels, outer - inner)
    selector = (gauge_kernel[:, None] == jnp.arange(classes)[None, :]).astype(jnp.float32)

    owner = row_gauge // gauges_here
    local = row_gauge % gauges_here
    hit = owner[:, None] == jnp.arange(owners)[None, :]
    rank = jnp.cumsum(hit.astype(jnp.int32), axis=0) - 1
    dest = owner * CAP + jnp.sum(jnp.where(hit, rank, 0), axis=1)
    entries = owners * CAP
    place = (jnp.arange(entries)[:, None] == dest[None, :]).astype(jnp.float32)
    sent_ids = jnp.full((entries,), -1, jnp.int32).at[dest].set(local)
    got_ids = lax.all_to_all(sent_ids, "basin", 0, 0, tiled=True)
    gather = (jnp.arange(gauges_here)[:, None] == got_ids[None, :]).astype(jnp.float32)

    def forward(field):
        partial_value = jnp.einsum(
            "bjr,brt->bjt", weights, field.reshape(blocks, width, hours), precision=HIGH
        )
        outgoing = jnp.dot(place, partial_value.reshape(partials, hours), precision=HIGH)
        incoming, basin_sq = basin_exchange(outgoing, squared(field))
        sums = jnp.dot(gather, incoming, precision=HIGH)
        earlier, total_sq = tm_shift(sums, basin_sq, 1, 2)
        return class_mix(jnp.concatenate([earlier, sums], axis=1), table_fwd, selector), total_sq[0, 0]

    def backward(series):
        later, tm_sq = tm_shift(series, squared(series), -1, 3)
        upstream = class_mix(jnp.concatenate([series, later], axis=1), table_bwd, selector)
        outgoing = jnp.dot(gather.T, upstream, precision=lax.Precision.HIGH)
        incoming, total_sq = basin_exchange(outgoing, tm_sq)
        rows = jnp.dot(place.T, incoming, precision=lax.Precision.HIGH)
        spread = jnp.einsum(
            "bjr,bjt->brt", weights, rows.reshape(blocks, slots, hours), precision=lax.Precision.HIGH
        )
        return spread.reshape(blocks * width, hours), total_sq[0, 0]

    start = observed - forward(first_guess)[0]
    pulled_start, beta_sq = backward(start)
    beta = jnp.sqrt(beta_sq)
    u = start / beta
    pulled = pulled_start / beta
    forward_pulled, alpha_sq = forward(pulled)
    alpha = jnp.sqrt(alpha_sq)
    v = pulled / alpha
    w = v
    correction = jnp.zeros(first_guess.shape, jnp.float32)
    phibar = beta
    rhobar = alpha
    for step in range(ITERS):
        final = step == ITERS - 1
        p = forward_pulled / alpha - alpha * u
        if final:
            beta = jnp.sqrt(global_total(squared(p)))
        else:
            pulled_p, beta_sq = backward(p)
            beta = jnp.sqrt(beta_sq)
            pulled = pulled_p / beta - beta * v
            forward_pulled, alpha_next = forward(pulled)
            alpha_next = jnp.sqrt(alpha_next)
            v_next = pulled / alpha_next
        u = p / beta
        rho = jnp.sqrt(rhobar * rhobar + beta * beta)
        cosine = rhobar / rho
        sine = beta / rho
        phi = cosine * phibar
        phibar = sine * phibar
        correction = correction + phi / rho * w
        if not final:
            theta = sine * alpha_next
            rhobar = -cosine * alpha_next
            w = v_next - theta / rho * w
            v = v_next
            alpha = alpha_next
    return first_guess + correction


def solution(mesh):
    in_specs = (
        P("basin", None, None),
        P("basin"),
        P("basin"),
        P(),
        P("basin", "tm"),
        P("basin", "tm"),
    )
    out_specs = P("basin", "tm")
    return jax.shard_map(shards, mesh=mesh, in_specs=in_specs, out_specs=out_specs, check_vma=False)
```

```python
import functools

import jax
import jax.numpy as jnp
from jax import lax
from jax.experimental import pallas as pl
from jax.experimental.pallas import tpu as pltpu
from jax.sharding import PartitionSpec as P

ITERS = 3
CAP = 32
LANES = 128

HIGH = lax.Precision.HIGHEST
MESH = pl.DeviceIdType.MESH


def from_behind(x, axis, by):
    devices = lax.axis_size(axis)
    pairs = [(i, i + by) for i in range(devices) if 0 <= i + by < devices]
    return lax.ppermute(x, axis, pairs)


def lag_table(kernels, lag):
    classes, taps = kernels.shape
    rows, hours = lag.shape
    onehot = (lag.T[None, :, :] == jnp.arange(taps)[:, None, None]).astype(jnp.float32)
    picked = jnp.dot(kernels, onehot.reshape(taps, hours * rows), precision=HIGH)
    return picked.reshape(classes, hours, rows)


def class_mix(extended, table, selector):
    spread = lax.dot_general(extended, table, (((1,), (2,)), ((), ())), precision=lax.Precision.HIGH)
    return jnp.sum(spread * selector[:, :, None], axis=1)


def squared(values):
    return jnp.sum(values * values)


def _total_body(x_ref, o_ref, tm_rows, all_rows, own_sem, tsend, trecv, bsend, brecv, *, nb, nt):
    me = lax.axis_index("basin")
    hb = lax.axis_index("tm")
    barrier = pltpu.get_barrier_semaphore()
    for j in range(1, nt):
        pl.semaphore_signal(barrier, inc=1, device_id=(me, lax.rem(hb + j, nt)), device_id_type=MESH)
    for k in range(1, nb):
        pl.semaphore_signal(barrier, inc=1, device_id=(lax.rem(me + k, nb), hb), device_id_type=MESH)
    pl.semaphore_wait(barrier, nt - 1 + nb - 1)

    own = pltpu.make_async_copy(x_ref, tm_rows.at[pl.ds(hb, 1)], own_sem.at[0])
    own.start()
    sends = []
    for j in range(1, nt):
        copy = pltpu.make_async_remote_copy(
            src_ref=x_ref, dst_ref=tm_rows.at[pl.ds(hb, 1)], send_sem=tsend.at[j], recv_sem=trecv.at[j],
            device_id=(me, lax.rem(hb + j, nt)), device_id_type=MESH,
        )
        copy.start()
        sends.append(copy)
    own.wait()
    for j in range(1, nt):
        sends[j - 1].wait_send()
        origin = lax.rem(hb + nt - j, nt)
        pltpu.make_async_remote_copy(
            src_ref=x_ref, dst_ref=tm_rows.at[pl.ds(origin, 1)], send_sem=tsend.at[j], recv_sem=trecv.at[j],
            device_id=(me, origin), device_id_type=MESH,
        ).wait_recv()

    own_block = pltpu.make_async_copy(tm_rows, all_rows.at[me], own_sem.at[1])
    own_block.start()
    blocks = []
    for k in range(1, nb):
        copy = pltpu.make_async_remote_copy(
            src_ref=tm_rows, dst_ref=all_rows.at[me], send_sem=bsend.at[k], recv_sem=brecv.at[k],
            device_id=(lax.rem(me + k, nb), hb), device_id_type=MESH,
        )
        copy.start()
        blocks.append(copy)
    own_block.wait()
    for k in range(1, nb):
        blocks[k - 1].wait_send()
        source = lax.rem(me + nb - k, nb)
        pltpu.make_async_remote_copy(
            src_ref=tm_rows, dst_ref=all_rows.at[source], send_sem=bsend.at[k], recv_sem=brecv.at[k],
            device_id=(source, hb), device_id_type=MESH,
        ).wait_recv()
    o_ref[...] = jnp.sum(all_rows[...].reshape(nb * nt, LANES), axis=0, keepdims=True)


def global_total(value):
    nb = lax.axis_size("basin")
    nt = lax.axis_size("tm")
    out = pl.pallas_call(
        functools.partial(_total_body, nb=nb, nt=nt),
        out_shape=jax.ShapeDtypeStruct((1, LANES), jnp.float32),
        in_specs=[pl.BlockSpec(memory_space=pltpu.VMEM)],
        out_specs=pl.BlockSpec(memory_space=pltpu.VMEM),
        scratch_shapes=[
            pltpu.VMEM((nt, LANES), jnp.float32),
            pltpu.VMEM((nb, nt, LANES), jnp.float32),
            pltpu.SemaphoreType.DMA((2,)),
            pltpu.SemaphoreType.DMA((nt,)),
            pltpu.SemaphoreType.DMA((nt,)),
            pltpu.SemaphoreType.DMA((nb,)),
            pltpu.SemaphoreType.DMA((nb,)),
        ],
        compiler_params=pltpu.CompilerParams(collective_id=0, has_side_effects=True),
    )(as_row(value))
    return out[0, 0]


def _exchange_body(x_ref, c_ref, o_ref, t_ref, landed, carried, own_sem, send_sem, recv_sem, csend, crecv, *, nb):
    me = lax.axis_index("basin")
    hour_block = lax.axis_index("tm")
    barrier = pltpu.get_barrier_semaphore()
    for k in range(1, nb):
        pl.semaphore_signal(
            barrier, inc=1, device_id=(lax.rem(me + k, nb), hour_block), device_id_type=MESH
        )
    pl.semaphore_wait(barrier, nb - 1)
    own = pltpu.make_async_copy(x_ref.at[me], landed.at[me], own_sem.at[0])
    own.start()
    own_carry = pltpu.make_async_copy(c_ref, carried.at[pl.ds(me, 1)], own_sem.at[1])
    own_carry.start()
    copies = []
    for k in range(1, nb):
        peer = lax.rem(me + k, nb)
        copy = pltpu.make_async_remote_copy(
            src_ref=x_ref.at[peer],
            dst_ref=landed.at[me],
            send_sem=send_sem.at[k],
            recv_sem=recv_sem.at[k],
            device_id=(peer, hour_block),
            device_id_type=MESH,
        )
        copy.start()
        carry = pltpu.make_async_remote_copy(
            src_ref=c_ref,
            dst_ref=carried.at[pl.ds(me, 1)],
            send_sem=csend.at[k],
            recv_sem=crecv.at[k],
            device_id=(peer, hour_block),
            device_id_type=MESH,
        )
        carry.start()
        copies.append((copy, carry))
    own.wait()
    own_carry.wait()
    for k in range(1, nb):
        copies[k - 1][0].wait_send()
        copies[k - 1][1].wait_send()
        source = lax.rem(me + nb - k, nb)
        pltpu.make_async_remote_copy(
            src_ref=x_ref.at[source],
            dst_ref=landed.at[source],
            send_sem=send_sem.at[k],
            recv_sem=recv_sem.at[k],
            device_id=(source, hour_block),
            device_id_type=MESH,
        ).wait_recv()
        pltpu.make_async_remote_copy(
            src_ref=c_ref,
            dst_ref=carried.at[pl.ds(source, 1)],
            send_sem=csend.at[k],
            recv_sem=crecv.at[k],
            device_id=(source, hour_block),
            device_id_type=MESH,
        ).wait_recv()
    o_ref[...] = landed[...]
    t_ref[...] = jnp.sum(carried[...], axis=0, keepdims=True)


def as_row(value):
    if value.ndim == 2:
        return value
    return jnp.broadcast_to(value.astype(jnp.float32), (1, LANES))


def basin_exchange(x, carry):
    nb = lax.axis_size("basin")
    total, hours = x.shape
    shaped = x.reshape(nb, total // nb, hours)
    out, summed = pl.pallas_call(
        functools.partial(_exchange_body, nb=nb),
        out_shape=(
            jax.ShapeDtypeStruct(shaped.shape, jnp.float32),
            jax.ShapeDtypeStruct((1, LANES), jnp.float32),
        ),
        in_specs=[pl.BlockSpec(memory_space=pltpu.VMEM)] * 2,
        out_specs=(pl.BlockSpec(memory_space=pltpu.VMEM),) * 2,
        scratch_shapes=[
            pltpu.VMEM(shaped.shape, jnp.float32),
            pltpu.VMEM((nb, LANES), jnp.float32),
            pltpu.SemaphoreType.DMA((2,)),
            pltpu.SemaphoreType.DMA((nb,)),
            pltpu.SemaphoreType.DMA((nb,)),
            pltpu.SemaphoreType.DMA((nb,)),
            pltpu.SemaphoreType.DMA((nb,)),
        ],
        compiler_params=pltpu.CompilerParams(collective_id=1, has_side_effects=True),
    )(shaped, as_row(carry))
    return out.reshape(total, hours), summed


def _shift_body(x_ref, c_ref, o_ref, t_ref, held, carried, own_sem, dsend, drecv, csend, crecv, *, nt, by):
    basin = lax.axis_index("basin")
    me = lax.axis_index("tm")
    barrier = pltpu.get_barrier_semaphore()
    for k in range(1, nt):
        pl.semaphore_signal(
            barrier, inc=1, device_id=(basin, lax.rem(me + k, nt)), device_id_type=MESH
        )
    pl.semaphore_wait(barrier, nt - 1)

    target = me + by
    source = me - by
    has_target = jnp.logical_and(target >= 0, target < nt)
    has_source = jnp.logical_and(source >= 0, source < nt)
    data = pltpu.make_async_remote_copy(
        src_ref=x_ref,
        dst_ref=held,
        send_sem=dsend,
        recv_sem=drecv,
        device_id=(basin, lax.rem(target + nt, nt)),
        device_id_type=MESH,
    )

    @pl.when(has_target)
    def _():
        data.start()

    own = pltpu.make_async_copy(c_ref, carried.at[pl.ds(me, 1)], own_sem)
    own.start()
    copies = []
    for k in range(1, nt):
        copy = pltpu.make_async_remote_copy(
            src_ref=c_ref,
            dst_ref=carried.at[pl.ds(me, 1)],
            send_sem=csend.at[k],
            recv_sem=crecv.at[k],
            device_id=(basin, lax.rem(me + k, nt)),
            device_id_type=MESH,
        )
        copy.start()
        copies.append(copy)
    own.wait()
    for k in range(1, nt):
        copies[k - 1].wait_send()
        origin = lax.rem(me + nt - k, nt)
        pltpu.make_async_remote_copy(
            src_ref=c_ref,
            dst_ref=carried.at[pl.ds(origin, 1)],
            send_sem=csend.at[k],
            recv_sem=crecv.at[k],
            device_id=(basin, origin),
            device_id_type=MESH,
        ).wait_recv()
    t_ref[...] = jnp.sum(carried[...], axis=0, keepdims=True)

    @pl.when(has_target)
    def _():
        data.wait_send()

    @pl.when(has_source)
    def _():
        data.wait_recv()
        o_ref[...] = held[...]

    @pl.when(jnp.logical_not(has_source))
    def _():
        o_ref[...] = jnp.zeros(o_ref.shape, o_ref.dtype)


def tm_shift(x, carry, by, ident):
    nt = lax.axis_size("tm")
    c = as_row(carry)
    out, summed = pl.pallas_call(
        functools.partial(_shift_body, nt=nt, by=by),
        out_shape=(
            jax.ShapeDtypeStruct(x.shape, jnp.float32),
            jax.ShapeDtypeStruct((1, LANES), jnp.float32),
        ),
        in_specs=[pl.BlockSpec(memory_space=pltpu.VMEM)] * 2,
        out_specs=(pl.BlockSpec(memory_space=pltpu.VMEM),) * 2,
        scratch_shapes=[
            pltpu.VMEM(x.shape, jnp.float32),
            pltpu.VMEM((nt, LANES), jnp.float32),
            pltpu.SemaphoreType.DMA(()),
            pltpu.SemaphoreType.DMA(()),
            pltpu.SemaphoreType.DMA(()),
            pltpu.SemaphoreType.DMA((nt,)),
            pltpu.SemaphoreType.DMA((nt,)),
        ],
        compiler_params=pltpu.CompilerParams(collective_id=ident, has_side_effects=True),
    )(x, c)
    return out, summed


def shards(incidence, row_gauge, gauge_kernel, kernels, observed, first_guess):
    weights = incidence.astype(jnp.float32)
    blocks, slots, width = weights.shape
    gauges_here, hours = observed.shape
    owners = lax.axis_size("basin")
    classes = kernels.shape[0]
    partials = blocks * slots
    outer = jnp.arange(2 * hours)[:, None]
    inner = jnp.arange(hours)[None, :]
    table_fwd = lag_table(kernels, inner + hours - outer)
    table_bwd = lag_table(kernels, outer - inner)
    selector = (gauge_kernel[:, None] == jnp.arange(classes)[None, :]).astype(jnp.float32)

    owner = row_gauge // gauges_here
    local = row_gauge % gauges_here
    hit = owner[:, None] == jnp.arange(owners)[None, :]
    rank = jnp.cumsum(hit.astype(jnp.int32), axis=0) - 1
    dest = owner * CAP + jnp.sum(jnp.where(hit, rank, 0), axis=1)
    entries = owners * CAP
    place = (jnp.arange(entries)[:, None] == dest[None, :]).astype(jnp.float32)
    sent_ids = jnp.full((entries,), -1, jnp.int32).at[dest].set(local)
    got_ids = lax.all_to_all(sent_ids, "basin", 0, 0, tiled=True)
    gather = (jnp.arange(gauges_here)[:, None] == got_ids[None, :]).astype(jnp.float32)

    def forward(field):
        partial_value = jnp.einsum(
            "bjr,brt->bjt", weights, field.reshape(blocks, width, hours), precision=HIGH
        )
        outgoing = jnp.dot(place, partial_value.reshape(partials, hours), precision=HIGH)
        incoming, basin_sq = basin_exchange(outgoing, squared(field))
        sums = jnp.dot(gather, incoming, precision=HIGH)
        earlier, total_sq = tm_shift(sums, basin_sq, 1, 2)
        return class_mix(jnp.concatenate([earlier, sums], axis=1), table_fwd, selector), total_sq[0, 0]

    def backward(series):
        later, tm_sq = tm_shift(series, squared(series), -1, 3)
        upstream = class_mix(jnp.concatenate([series, later], axis=1), table_bwd, selector)
        outgoing = jnp.dot(gather.T, upstream, precision=lax.Precision.HIGH)
        incoming, total_sq = basin_exchange(outgoing, tm_sq)
        rows = jnp.dot(place.T, incoming, precision=lax.Precision.HIGH)
        spread = jnp.einsum(
            "bjr,bjt->brt", weights, rows.reshape(blocks, slots, hours), precision=lax.Precision.HIGH
        )
        return spread.reshape(blocks * width, hours), total_sq[0, 0]

    start = observed - forward(first_guess)[0]
    pulled_start, beta_sq = backward(start)
    beta = jnp.sqrt(beta_sq)
    u = start / beta
    pulled = pulled_start / beta
    forward_pulled, alpha_sq = forward(pulled)
    alpha = jnp.sqrt(alpha_sq)
    v = pulled / alpha
    w = v
    correction = jnp.zeros(first_guess.shape, jnp.float32)
    phibar = beta
    rhobar = alpha
    for step in range(ITERS):
        final = step == ITERS - 1
        p = forward_pulled / alpha - alpha * u
        if final:
            beta = jnp.sqrt(global_total(squared(p)))
        else:
            pulled_p, beta_sq = backward(p)
            beta = jnp.sqrt(beta_sq)
            pulled = pulled_p / beta - beta * v
            forward_pulled, alpha_next = forward(pulled)
            alpha_next = jnp.sqrt(alpha_next)
            v_next = pulled / alpha_next
        u = p / beta
        rho = jnp.sqrt(rhobar * rhobar + beta * beta)
        cosine = rhobar / rho
        sine = beta / rho
        phi = cosine * phibar
        phibar = sine * phibar
        correction = correction + phi / rho * w
        if not final:
            theta = sine * alpha_next
            rhobar = -cosine * alpha_next
            w = v_next - theta / rho * w
            v = v_next
            alpha = alpha_next
    return first_guess + correction


def solution(mesh):
    in_specs = (
        P("basin", None, None),
        P("basin"),
        P("basin"),
        P(),
        P("basin", "tm"),
        P("basin", "tm"),
    )
    out_specs = P("basin", "tm")
    return jax.shard_map(shards, mesh=mesh, in_specs=in_specs, out_specs=out_specs, check_vma=False)
```

```python
import functools

import jax
import jax.numpy as jnp
from jax import lax
from jax.experimental import pallas as pl
from jax.experimental.pallas import tpu as pltpu
from jax.sharding import PartitionSpec as P

ITERS = 3
CAP = 32
LANES = 128

HIGH = lax.Precision.HIGHEST
MESH = pl.DeviceIdType.MESH


def from_behind(x, axis, by):
    devices = lax.axis_size(axis)
    pairs = [(i, i + by) for i in range(devices) if 0 <= i + by < devices]
    return lax.ppermute(x, axis, pairs)


def lag_table(kernels, lag):
    classes, taps = kernels.shape
    rows, hours = lag.shape
    onehot = (lag.T[None, :, :] == jnp.arange(taps)[:, None, None]).astype(jnp.float32)
    picked = jnp.dot(kernels, onehot.reshape(taps, hours * rows), precision=HIGH)
    return picked.reshape(classes, hours, rows)


def class_mix(extended, table, selector):
    spread = lax.dot_general(extended, table, (((1,), (2,)), ((), ())), precision=lax.Precision.HIGH)
    return jnp.sum(spread * selector[:, :, None], axis=1)


def squared(values):
    return jnp.sum(values * values)


def _total_body(x_ref, o_ref, tm_rows, all_rows, own_sem, tsend, trecv, bsend, brecv, *, nb, nt):
    me = lax.axis_index("basin")
    hb = lax.axis_index("tm")
    barrier = pltpu.get_barrier_semaphore()
    for j in range(1, nt):
        pl.semaphore_signal(barrier, inc=1, device_id=(me, lax.rem(hb + j, nt)), device_id_type=MESH)
    for k in range(1, nb):
        pl.semaphore_signal(barrier, inc=1, device_id=(lax.rem(me + k, nb), hb), device_id_type=MESH)
    pl.semaphore_wait(barrier, nt - 1 + nb - 1)

    own = pltpu.make_async_copy(x_ref, tm_rows.at[pl.ds(hb, 1)], own_sem.at[0])
    own.start()
    sends = []
    for j in range(1, nt):
        copy = pltpu.make_async_remote_copy(
            src_ref=x_ref, dst_ref=tm_rows.at[pl.ds(hb, 1)], send_sem=tsend.at[j], recv_sem=trecv.at[j],
            device_id=(me, lax.rem(hb + j, nt)), device_id_type=MESH,
        )
        copy.start()
        sends.append(copy)
    own.wait()
    for j in range(1, nt):
        sends[j - 1].wait_send()
        origin = lax.rem(hb + nt - j, nt)
        pltpu.make_async_remote_copy(
            src_ref=x_ref, dst_ref=tm_rows.at[pl.ds(origin, 1)], send_sem=tsend.at[j], recv_sem=trecv.at[j],
            device_id=(me, origin), device_id_type=MESH,
        ).wait_recv()

    own_block = pltpu.make_async_copy(tm_rows, all_rows.at[me], own_sem.at[1])
    own_block.start()
    blocks = []
    for k in range(1, nb):
        copy = pltpu.make_async_remote_copy(
            src_ref=tm_rows, dst_ref=all_rows.at[me], send_sem=bsend.at[k], recv_sem=brecv.at[k],
            device_id=(lax.rem(me + k, nb), hb), device_id_type=MESH,
        )
        copy.start()
        blocks.append(copy)
    own_block.wait()
    for k in range(1, nb):
        blocks[k - 1].wait_send()
        source = lax.rem(me + nb - k, nb)
        pltpu.make_async_remote_copy(
            src_ref=tm_rows, dst_ref=all_rows.at[source], send_sem=bsend.at[k], recv_sem=brecv.at[k],
            device_id=(source, hb), device_id_type=MESH,
        ).wait_recv()
    o_ref[...] = jnp.sum(all_rows[...].reshape(nb * nt, LANES), axis=0, keepdims=True)


def global_total(value):
    nb = lax.axis_size("basin")
    nt = lax.axis_size("tm")
    out = pl.pallas_call(
        functools.partial(_total_body, nb=nb, nt=nt),
        out_shape=jax.ShapeDtypeStruct((1, LANES), jnp.float32),
        in_specs=[pl.BlockSpec(memory_space=pltpu.VMEM)],
        out_specs=pl.BlockSpec(memory_space=pltpu.VMEM),
        scratch_shapes=[
            pltpu.VMEM((nt, LANES), jnp.float32),
            pltpu.VMEM((nb, nt, LANES), jnp.float32),
            pltpu.SemaphoreType.DMA((2,)),
            pltpu.SemaphoreType.DMA((nt,)),
            pltpu.SemaphoreType.DMA((nt,)),
            pltpu.SemaphoreType.DMA((nb,)),
            pltpu.SemaphoreType.DMA((nb,)),
        ],
        compiler_params=pltpu.CompilerParams(collective_id=0, has_side_effects=True),
    )(as_row(value))
    return out[0, 0]


def _exchange_body(x_ref, c_ref, o_ref, t_ref, landed, carried, own_sem, send_sem, recv_sem, csend, crecv, *, nb):
    me = lax.axis_index("basin")
    hour_block = lax.axis_index("tm")
    barrier = pltpu.get_barrier_semaphore()
    for k in range(1, nb):
        pl.semaphore_signal(
            barrier, inc=1, device_id=(lax.rem(me + k, nb), hour_block), device_id_type=MESH
        )
    pl.semaphore_wait(barrier, nb - 1)
    own = pltpu.make_async_copy(x_ref.at[me], landed.at[me], own_sem.at[0])
    own.start()
    own_carry = pltpu.make_async_copy(c_ref, carried.at[pl.ds(me, 1)], own_sem.at[1])
    own_carry.start()
    copies = []
    for k in range(1, nb):
        peer = lax.rem(me + k, nb)
        copy = pltpu.make_async_remote_copy(
            src_ref=x_ref.at[peer],
            dst_ref=landed.at[me],
            send_sem=send_sem.at[k],
            recv_sem=recv_sem.at[k],
            device_id=(peer, hour_block),
            device_id_type=MESH,
        )
        copy.start()
        carry = pltpu.make_async_remote_copy(
            src_ref=c_ref,
            dst_ref=carried.at[pl.ds(me, 1)],
            send_sem=csend.at[k],
            recv_sem=crecv.at[k],
            device_id=(peer, hour_block),
            device_id_type=MESH,
        )
        carry.start()
        copies.append((copy, carry))
    own.wait()
    own_carry.wait()
    for k in range(1, nb):
        copies[k - 1][0].wait_send()
        copies[k - 1][1].wait_send()
        source = lax.rem(me + nb - k, nb)
        pltpu.make_async_remote_copy(
            src_ref=x_ref.at[source],
            dst_ref=landed.at[source],
            send_sem=send_sem.at[k],
            recv_sem=recv_sem.at[k],
            device_id=(source, hour_block),
            device_id_type=MESH,
        ).wait_recv()
        pltpu.make_async_remote_copy(
            src_ref=c_ref,
            dst_ref=carried.at[pl.ds(source, 1)],
            send_sem=csend.at[k],
            recv_sem=crecv.at[k],
            device_id=(source, hour_block),
            device_id_type=MESH,
        ).wait_recv()
    o_ref[...] = landed[...]
    t_ref[...] = jnp.sum(carried[...], axis=0, keepdims=True)


def as_row(value):
    if value.ndim == 2:
        return value
    return jnp.broadcast_to(value.astype(jnp.float32), (1, LANES))


def basin_exchange(x, carry):
    nb = lax.axis_size("basin")
    total, hours = x.shape
    shaped = x.reshape(nb, total // nb, hours)
    out, summed = pl.pallas_call(
        functools.partial(_exchange_body, nb=nb),
        out_shape=(
            jax.ShapeDtypeStruct(shaped.shape, jnp.float32),
            jax.ShapeDtypeStruct((1, LANES), jnp.float32),
        ),
        in_specs=[pl.BlockSpec(memory_space=pltpu.VMEM)] * 2,
        out_specs=(pl.BlockSpec(memory_space=pltpu.VMEM),) * 2,
        scratch_shapes=[
            pltpu.VMEM(shaped.shape, jnp.float32),
            pltpu.VMEM((nb, LANES), jnp.float32),
            pltpu.SemaphoreType.DMA((2,)),
            pltpu.SemaphoreType.DMA((nb,)),
            pltpu.SemaphoreType.DMA((nb,)),
            pltpu.SemaphoreType.DMA((nb,)),
            pltpu.SemaphoreType.DMA((nb,)),
        ],
        compiler_params=pltpu.CompilerParams(collective_id=1, has_side_effects=True),
    )(shaped, as_row(carry))
    return out.reshape(total, hours), summed


def _shift_body(x_ref, c_ref, o_ref, t_ref, held, carried, own_sem, dsend, drecv, csend, crecv, *, nt, by):
    basin = lax.axis_index("basin")
    me = lax.axis_index("tm")
    barrier = pltpu.get_barrier_semaphore()
    for k in range(1, nt):
        pl.semaphore_signal(
            barrier, inc=1, device_id=(basin, lax.rem(me + k, nt)), device_id_type=MESH
        )
    pl.semaphore_wait(barrier, nt - 1)

    target = me + by
    source = me - by
    has_target = jnp.logical_and(target >= 0, target < nt)
    has_source = jnp.logical_and(source >= 0, source < nt)
    data = pltpu.make_async_remote_copy(
        src_ref=x_ref,
        dst_ref=held,
        send_sem=dsend,
        recv_sem=drecv,
        device_id=(basin, lax.rem(target + nt, nt)),
        device_id_type=MESH,
    )

    @pl.when(has_target)
    def _():
        data.start()

    own = pltpu.make_async_copy(c_ref, carried.at[pl.ds(me, 1)], own_sem)
    own.start()
    copies = []
    for k in range(1, nt):
        copy = pltpu.make_async_remote_copy(
            src_ref=c_ref,
            dst_ref=carried.at[pl.ds(me, 1)],
            send_sem=csend.at[k],
            recv_sem=crecv.at[k],
            device_id=(basin, lax.rem(me + k, nt)),
            device_id_type=MESH,
        )
        copy.start()
        copies.append(copy)
    own.wait()
    for k in range(1, nt):
        copies[k - 1].wait_send()
        origin = lax.rem(me + nt - k, nt)
        pltpu.make_async_remote_copy(
            src_ref=c_ref,
            dst_ref=carried.at[pl.ds(origin, 1)],
            send_sem=csend.at[k],
            recv_sem=crecv.at[k],
            device_id=(basin, origin),
            device_id_type=MESH,
        ).wait_recv()
    t_ref[...] = jnp.sum(carried[...], axis=0, keepdims=True)

    @pl.when(has_target)
    def _():
        data.wait_send()

    @pl.when(has_source)
    def _():
        data.wait_recv()
        o_ref[...] = held[...]

    @pl.when(jnp.logical_not(has_source))
    def _():
        o_ref[...] = jnp.zeros(o_ref.shape, o_ref.dtype)


def tm_shift(x, carry, by, ident):
    nt = lax.axis_size("tm")
    c = as_row(carry)
    out, summed = pl.pallas_call(
        functools.partial(_shift_body, nt=nt, by=by),
        out_shape=(
            jax.ShapeDtypeStruct(x.shape, jnp.float32),
            jax.ShapeDtypeStruct((1, LANES), jnp.float32),
        ),
        in_specs=[pl.BlockSpec(memory_space=pltpu.VMEM)] * 2,
        out_specs=(pl.BlockSpec(memory_space=pltpu.VMEM),) * 2,
        scratch_shapes=[
            pltpu.VMEM(x.shape, jnp.float32),
            pltpu.VMEM((nt, LANES), jnp.float32),
            pltpu.SemaphoreType.DMA(()),
            pltpu.SemaphoreType.DMA(()),
            pltpu.SemaphoreType.DMA(()),
            pltpu.SemaphoreType.DMA((nt,)),
            pltpu.SemaphoreType.DMA((nt,)),
        ],
        compiler_params=pltpu.CompilerParams(collective_id=ident, has_side_effects=True),
    )(x, c)
    return out, summed


def shards(incidence, row_gauge, gauge_kernel, kernels, observed, first_guess):
    weights = incidence.astype(jnp.float32)
    blocks, slots, width = weights.shape
    gauges_here, hours = observed.shape
    owners = lax.axis_size("basin")
    classes = kernels.shape[0]
    partials = blocks * slots
    outer = jnp.arange(2 * hours)[:, None]
    inner = jnp.arange(hours)[None, :]
    table_fwd = lag_table(kernels, inner + hours - outer)
    table_bwd = lag_table(kernels, outer - inner)
    selector = (gauge_kernel[:, None] == jnp.arange(classes)[None, :]).astype(jnp.float32)

    owner = row_gauge // gauges_here
    local = row_gauge % gauges_here
    hit = owner[:, None] == jnp.arange(owners)[None, :]
    rank = jnp.cumsum(hit.astype(jnp.int32), axis=0) - 1
    dest = owner * CAP + jnp.sum(jnp.where(hit, rank, 0), axis=1)
    entries = owners * CAP
    place = (jnp.arange(entries)[:, None] == dest[None, :]).astype(jnp.float32)
    every = lax.all_gather(row_gauge, "basin")
    mine = every // gauges_here == lax.axis_index("basin")
    order = jnp.cumsum(mine.astype(jnp.int32), axis=1) - 1
    slot = mine[:, :, None] & (order[:, :, None] == jnp.arange(CAP)[None, None, :])
    got_ids = (jnp.sum(jnp.where(slot, every[:, :, None] % gauges_here + 1, 0), axis=1) - 1).reshape(entries)
    gather = (jnp.arange(gauges_here)[:, None] == got_ids[None, :]).astype(jnp.float32)

    def forward(field):
        partial_value = jnp.einsum(
            "bjr,brt->bjt", weights, field.reshape(blocks, width, hours), precision=HIGH
        )
        outgoing = jnp.dot(place, partial_value.reshape(partials, hours), precision=HIGH)
        incoming, basin_sq = basin_exchange(outgoing, squared(field))
        sums = jnp.dot(gather, incoming, precision=HIGH)
        earlier, total_sq = tm_shift(sums, basin_sq, 1, 2)
        return class_mix(jnp.concatenate([earlier, sums], axis=1), table_fwd, selector), total_sq[0, 0]

    def backward(series):
        later, tm_sq = tm_shift(series, squared(series), -1, 3)
        upstream = class_mix(jnp.concatenate([series, later], axis=1), table_bwd, selector)
        outgoing = jnp.dot(gather.T, upstream, precision=lax.Precision.HIGH)
        incoming, total_sq = basin_exchange(outgoing, tm_sq)
        rows = jnp.dot(place.T, incoming, precision=lax.Precision.HIGH)
        spread = jnp.einsum(
            "bjr,bjt->brt", weights, rows.reshape(blocks, slots, hours), precision=lax.Precision.HIGH
        )
        return spread.reshape(blocks * width, hours), total_sq[0, 0]

    start = observed - forward(first_guess)[0]
    pulled_start, beta_sq = backward(start)
    beta = jnp.sqrt(beta_sq)
    u = start / beta
    pulled = pulled_start / beta
    forward_pulled, alpha_sq = forward(pulled)
    alpha = jnp.sqrt(alpha_sq)
    v = pulled / alpha
    w = v
    correction = jnp.zeros(first_guess.shape, jnp.float32)
    phibar = beta
    rhobar = alpha
    for step in range(ITERS):
        final = step == ITERS - 1
        p = forward_pulled / alpha - alpha * u
        if final:
            beta = jnp.sqrt(global_total(squared(p)))
        else:
            pulled_p, beta_sq = backward(p)
            beta = jnp.sqrt(beta_sq)
            pulled = pulled_p / beta - beta * v
            forward_pulled, alpha_next = forward(pulled)
            alpha_next = jnp.sqrt(alpha_next)
            v_next = pulled / alpha_next
        u = p / beta
        rho = jnp.sqrt(rhobar * rhobar + beta * beta)
        cosine = rhobar / rho
        sine = beta / rho
        phi = cosine * phibar
        phibar = sine * phibar
        correction = correction + phi / rho * w
        if not final:
            theta = sine * alpha_next
            rhobar = -cosine * alpha_next
            w = v_next - theta / rho * w
            v = v_next
            alpha = alpha_next
    return first_guess + correction


def solution(mesh):
    in_specs = (
        P("basin", None, None),
        P("basin"),
        P("basin"),
        P(),
        P("basin", "tm"),
        P("basin", "tm"),
    )
    out_specs = P("basin", "tm")
    return jax.shard_map(shards, mesh=mesh, in_specs=in_specs, out_specs=out_specs, check_vma=False)
```

```python
import functools

import jax
import jax.numpy as jnp
from jax import lax
from jax.experimental import pallas as pl
from jax.experimental.pallas import tpu as pltpu
from jax.sharding import PartitionSpec as P

ITERS = 3
CAP = 32
LANES = 128

HIGH = lax.Precision.HIGH
MESH = pl.DeviceIdType.MESH


def from_behind(x, axis, by):
    devices = lax.axis_size(axis)
    pairs = [(i, i + by) for i in range(devices) if 0 <= i + by < devices]
    return lax.ppermute(x, axis, pairs)


def lag_table(kernels, lag):
    classes, taps = kernels.shape
    rows, hours = lag.shape
    onehot = (lag.T[None, :, :] == jnp.arange(taps)[:, None, None]).astype(jnp.float32)
    picked = jnp.dot(kernels, onehot.reshape(taps, hours * rows), precision=HIGH)
    return picked.reshape(classes, hours, rows)


def class_mix(extended, table, selector):
    spread = lax.dot_general(extended, table, (((1,), (2,)), ((), ())), precision=lax.Precision.HIGH)
    return jnp.sum(spread * selector[:, :, None], axis=1)


def squared(values):
    return jnp.sum(values * values)


def _total_body(x_ref, o_ref, tm_rows, all_rows, own_sem, tsend, trecv, bsend, brecv, *, nb, nt):
    me = lax.axis_index("basin")
    hb = lax.axis_index("tm")
    barrier = pltpu.get_barrier_semaphore()
    for j in range(1, nt):
        pl.semaphore_signal(barrier, inc=1, device_id=(me, lax.rem(hb + j, nt)), device_id_type=MESH)
    for k in range(1, nb):
        pl.semaphore_signal(barrier, inc=1, device_id=(lax.rem(me + k, nb), hb), device_id_type=MESH)
    pl.semaphore_wait(barrier, nt - 1 + nb - 1)

    own = pltpu.make_async_copy(x_ref, tm_rows.at[pl.ds(hb, 1)], own_sem.at[0])
    own.start()
    sends = []
    for j in range(1, nt):
        copy = pltpu.make_async_remote_copy(
            src_ref=x_ref, dst_ref=tm_rows.at[pl.ds(hb, 1)], send_sem=tsend.at[j], recv_sem=trecv.at[j],
            device_id=(me, lax.rem(hb + j, nt)), device_id_type=MESH,
        )
        copy.start()
        sends.append(copy)
    own.wait()
    for j in range(1, nt):
        sends[j - 1].wait_send()
        origin = lax.rem(hb + nt - j, nt)
        pltpu.make_async_remote_copy(
            src_ref=x_ref, dst_ref=tm_rows.at[pl.ds(origin, 1)], send_sem=tsend.at[j], recv_sem=trecv.at[j],
            device_id=(me, origin), device_id_type=MESH,
        ).wait_recv()

    own_block = pltpu.make_async_copy(tm_rows, all_rows.at[me], own_sem.at[1])
    own_block.start()
    blocks = []
    for k in range(1, nb):
        copy = pltpu.make_async_remote_copy(
            src_ref=tm_rows, dst_ref=all_rows.at[me], send_sem=bsend.at[k], recv_sem=brecv.at[k],
            device_id=(lax.rem(me + k, nb), hb), device_id_type=MESH,
        )
        copy.start()
        blocks.append(copy)
    own_block.wait()
    for k in range(1, nb):
        blocks[k - 1].wait_send()
        source = lax.rem(me + nb - k, nb)
        pltpu.make_async_remote_copy(
            src_ref=tm_rows, dst_ref=all_rows.at[source], send_sem=bsend.at[k], recv_sem=brecv.at[k],
            device_id=(source, hb), device_id_type=MESH,
        ).wait_recv()
    o_ref[...] = jnp.sum(all_rows[...].reshape(nb * nt, LANES), axis=0, keepdims=True)


def global_total(value):
    nb = lax.axis_size("basin")
    nt = lax.axis_size("tm")
    out = pl.pallas_call(
        functools.partial(_total_body, nb=nb, nt=nt),
        out_shape=jax.ShapeDtypeStruct((1, LANES), jnp.float32),
        in_specs=[pl.BlockSpec(memory_space=pltpu.VMEM)],
        out_specs=pl.BlockSpec(memory_space=pltpu.VMEM),
        scratch_shapes=[
            pltpu.VMEM((nt, LANES), jnp.float32),
            pltpu.VMEM((nb, nt, LANES), jnp.float32),
            pltpu.SemaphoreType.DMA((2,)),
            pltpu.SemaphoreType.DMA((nt,)),
            pltpu.SemaphoreType.DMA((nt,)),
            pltpu.SemaphoreType.DMA((nb,)),
            pltpu.SemaphoreType.DMA((nb,)),
        ],
        compiler_params=pltpu.CompilerParams(collective_id=0, has_side_effects=True),
    )(as_row(value))
    return out[0, 0]


def _exchange_body(x_ref, c_ref, o_ref, t_ref, landed, carried, own_sem, send_sem, recv_sem, csend, crecv, *, nb):
    me = lax.axis_index("basin")
    hour_block = lax.axis_index("tm")
    barrier = pltpu.get_barrier_semaphore()
    for k in range(1, nb):
        pl.semaphore_signal(
            barrier, inc=1, device_id=(lax.rem(me + k, nb), hour_block), device_id_type=MESH
        )
    pl.semaphore_wait(barrier, nb - 1)
    own = pltpu.make_async_copy(x_ref.at[me], landed.at[me], own_sem.at[0])
    own.start()
    own_carry = pltpu.make_async_copy(c_ref, carried.at[pl.ds(me, 1)], own_sem.at[1])
    own_carry.start()
    copies = []
    for k in range(1, nb):
        peer = lax.rem(me + k, nb)
        copy = pltpu.make_async_remote_copy(
            src_ref=x_ref.at[peer],
            dst_ref=landed.at[me],
            send_sem=send_sem.at[k],
            recv_sem=recv_sem.at[k],
            device_id=(peer, hour_block),
            device_id_type=MESH,
        )
        copy.start()
        carry = pltpu.make_async_remote_copy(
            src_ref=c_ref,
            dst_ref=carried.at[pl.ds(me, 1)],
            send_sem=csend.at[k],
            recv_sem=crecv.at[k],
            device_id=(peer, hour_block),
            device_id_type=MESH,
        )
        carry.start()
        copies.append((copy, carry))
    own.wait()
    own_carry.wait()
    for k in range(1, nb):
        copies[k - 1][0].wait_send()
        copies[k - 1][1].wait_send()
        source = lax.rem(me + nb - k, nb)
        pltpu.make_async_remote_copy(
            src_ref=x_ref.at[source],
            dst_ref=landed.at[source],
            send_sem=send_sem.at[k],
            recv_sem=recv_sem.at[k],
            device_id=(source, hour_block),
            device_id_type=MESH,
        ).wait_recv()
        pltpu.make_async_remote_copy(
            src_ref=c_ref,
            dst_ref=carried.at[pl.ds(source, 1)],
            send_sem=csend.at[k],
            recv_sem=crecv.at[k],
            device_id=(source, hour_block),
            device_id_type=MESH,
        ).wait_recv()
    o_ref[...] = landed[...]
    t_ref[...] = jnp.sum(carried[...], axis=0, keepdims=True)


def as_row(value):
    if value.ndim == 2:
        return value
    return jnp.broadcast_to(value.astype(jnp.float32), (1, LANES))


def basin_exchange(x, carry):
    nb = lax.axis_size("basin")
    total, hours = x.shape
    shaped = x.reshape(nb, total // nb, hours)
    out, summed = pl.pallas_call(
        functools.partial(_exchange_body, nb=nb),
        out_shape=(
            jax.ShapeDtypeStruct(shaped.shape, jnp.float32),
            jax.ShapeDtypeStruct((1, LANES), jnp.float32),
        ),
        in_specs=[pl.BlockSpec(memory_space=pltpu.VMEM)] * 2,
        out_specs=(pl.BlockSpec(memory_space=pltpu.VMEM),) * 2,
        scratch_shapes=[
            pltpu.VMEM(shaped.shape, jnp.float32),
            pltpu.VMEM((nb, LANES), jnp.float32),
            pltpu.SemaphoreType.DMA((2,)),
            pltpu.SemaphoreType.DMA((nb,)),
            pltpu.SemaphoreType.DMA((nb,)),
            pltpu.SemaphoreType.DMA((nb,)),
            pltpu.SemaphoreType.DMA((nb,)),
        ],
        compiler_params=pltpu.CompilerParams(collective_id=1, has_side_effects=True),
    )(shaped, as_row(carry))
    return out.reshape(total, hours), summed


def _shift_body(x_ref, c_ref, o_ref, t_ref, held, carried, own_sem, dsend, drecv, csend, crecv, *, nt, by):
    basin = lax.axis_index("basin")
    me = lax.axis_index("tm")
    barrier = pltpu.get_barrier_semaphore()
    for k in range(1, nt):
        pl.semaphore_signal(
            barrier, inc=1, device_id=(basin, lax.rem(me + k, nt)), device_id_type=MESH
        )
    pl.semaphore_wait(barrier, nt - 1)

    target = me + by
    source = me - by
    has_target = jnp.logical_and(target >= 0, target < nt)
    has_source = jnp.logical_and(source >= 0, source < nt)
    data = pltpu.make_async_remote_copy(
        src_ref=x_ref,
        dst_ref=held,
        send_sem=dsend,
        recv_sem=drecv,
        device_id=(basin, lax.rem(target + nt, nt)),
        device_id_type=MESH,
    )

    @pl.when(has_target)
    def _():
        data.start()

    own = pltpu.make_async_copy(c_ref, carried.at[pl.ds(me, 1)], own_sem)
    own.start()
    copies = []
    for k in range(1, nt):
        copy = pltpu.make_async_remote_copy(
            src_ref=c_ref,
            dst_ref=carried.at[pl.ds(me, 1)],
            send_sem=csend.at[k],
            recv_sem=crecv.at[k],
            device_id=(basin, lax.rem(me + k, nt)),
            device_id_type=MESH,
        )
        copy.start()
        copies.append(copy)
    own.wait()
    for k in range(1, nt):
        copies[k - 1].wait_send()
        origin = lax.rem(me + nt - k, nt)
        pltpu.make_async_remote_copy(
            src_ref=c_ref,
            dst_ref=carried.at[pl.ds(origin, 1)],
            send_sem=csend.at[k],
            recv_sem=crecv.at[k],
            device_id=(basin, origin),
            device_id_type=MESH,
        ).wait_recv()
    t_ref[...] = jnp.sum(carried[...], axis=0, keepdims=True)

    @pl.when(has_target)
    def _():
        data.wait_send()

    @pl.when(has_source)
    def _():
        data.wait_recv()
        o_ref[...] = held[...]

    @pl.when(jnp.logical_not(has_source))
    def _():
        o_ref[...] = jnp.zeros(o_ref.shape, o_ref.dtype)


def tm_shift(x, carry, by, ident):
    nt = lax.axis_size("tm")
    c = as_row(carry)
    out, summed = pl.pallas_call(
        functools.partial(_shift_body, nt=nt, by=by),
        out_shape=(
            jax.ShapeDtypeStruct(x.shape, jnp.float32),
            jax.ShapeDtypeStruct((1, LANES), jnp.float32),
        ),
        in_specs=[pl.BlockSpec(memory_space=pltpu.VMEM)] * 2,
        out_specs=(pl.BlockSpec(memory_space=pltpu.VMEM),) * 2,
        scratch_shapes=[
            pltpu.VMEM(x.shape, jnp.float32),
            pltpu.VMEM((nt, LANES), jnp.float32),
            pltpu.SemaphoreType.DMA(()),
            pltpu.SemaphoreType.DMA(()),
            pltpu.SemaphoreType.DMA(()),
            pltpu.SemaphoreType.DMA((nt,)),
            pltpu.SemaphoreType.DMA((nt,)),
        ],
        compiler_params=pltpu.CompilerParams(collective_id=ident, has_side_effects=True),
    )(x, c)
    return out, summed


def shards(incidence, row_gauge, gauge_kernel, kernels, observed, first_guess):
    weights = incidence.astype(jnp.float32)
    blocks, slots, width = weights.shape
    gauges_here, hours = observed.shape
    owners = lax.axis_size("basin")
    classes = kernels.shape[0]
    partials = blocks * slots
    outer = jnp.arange(2 * hours)[:, None]
    inner = jnp.arange(hours)[None, :]
    table_fwd = lag_table(kernels, inner + hours - outer)
    table_bwd = lag_table(kernels, outer - inner)
    selector = (gauge_kernel[:, None] == jnp.arange(classes)[None, :]).astype(jnp.float32)

    owner = row_gauge // gauges_here
    local = row_gauge % gauges_here
    hit = owner[:, None] == jnp.arange(owners)[None, :]
    rank = jnp.cumsum(hit.astype(jnp.int32), axis=0) - 1
    dest = owner * CAP + jnp.sum(jnp.where(hit, rank, 0), axis=1)
    entries = owners * CAP
    place = (jnp.arange(entries)[:, None] == dest[None, :]).astype(jnp.float32)
    sent_ids = jnp.full((entries,), -1, jnp.int32).at[dest].set(local)
    got_ids = lax.all_to_all(sent_ids, "basin", 0, 0, tiled=True)
    gather = (jnp.arange(gauges_here)[:, None] == got_ids[None, :]).astype(jnp.float32)

    def forward(field):
        partial_value = jnp.einsum(
            "bjr,brt->bjt", weights, field.reshape(blocks, width, hours), precision=HIGH
        )
        outgoing = jnp.dot(place, partial_value.reshape(partials, hours), precision=HIGH)
        incoming, basin_sq = basin_exchange(outgoing, squared(field))
        sums = jnp.dot(gather, incoming, precision=HIGH)
        earlier, total_sq = tm_shift(sums, basin_sq, 1, 2)
        return class_mix(jnp.concatenate([earlier, sums], axis=1), table_fwd, selector), total_sq[0, 0]

    def backward(series):
        later, tm_sq = tm_shift(series, squared(series), -1, 3)
        upstream = class_mix(jnp.concatenate([series, later], axis=1), table_bwd, selector)
        outgoing = jnp.dot(gather.T, upstream, precision=lax.Precision.HIGH)
        incoming, total_sq = basin_exchange(outgoing, tm_sq)
        rows = jnp.dot(place.T, incoming, precision=lax.Precision.HIGH)
        spread = jnp.einsum(
            "bjr,bjt->brt", weights, rows.reshape(blocks, slots, hours), precision=lax.Precision.HIGH
        )
        return spread.reshape(blocks * width, hours), total_sq[0, 0]

    start = observed - forward(first_guess)[0]
    pulled_start, beta_sq = backward(start)
    beta = jnp.sqrt(beta_sq)
    u = start / beta
    pulled = pulled_start / beta
    forward_pulled, alpha_sq = forward(pulled)
    alpha = jnp.sqrt(alpha_sq)
    v = pulled / alpha
    w = v
    correction = jnp.zeros(first_guess.shape, jnp.float32)
    phibar = beta
    rhobar = alpha
    for step in range(ITERS):
        final = step == ITERS - 1
        p = forward_pulled / alpha - alpha * u
        if final:
            beta = jnp.sqrt(global_total(squared(p)))
        else:
            pulled_p, beta_sq = backward(p)
            beta = jnp.sqrt(beta_sq)
            pulled = pulled_p / beta - beta * v
            forward_pulled, alpha_next = forward(pulled)
            alpha_next = jnp.sqrt(alpha_next)
            v_next = pulled / alpha_next
        u = p / beta
        rho = jnp.sqrt(rhobar * rhobar + beta * beta)
        cosine = rhobar / rho
        sine = beta / rho
        phi = cosine * phibar
        phibar = sine * phibar
        correction = correction + phi / rho * w
        if not final:
            theta = sine * alpha_next
            rhobar = -cosine * alpha_next
            w = v_next - theta / rho * w
            v = v_next
            alpha = alpha_next
    return first_guess + correction


def solution(mesh):
    in_specs = (
        P("basin", None, None),
        P("basin"),
        P("basin"),
        P(),
        P("basin", "tm"),
        P("basin", "tm"),
    )
    out_specs = P("basin", "tm")
    return jax.shard_map(shards, mesh=mesh, in_specs=in_specs, out_specs=out_specs, check_vma=False)
```

```python
import functools

import jax
import jax.numpy as jnp
from jax import lax
from jax.experimental import pallas as pl
from jax.experimental.pallas import tpu as pltpu
from jax.sharding import PartitionSpec as P

ITERS = 3
CAP = 32
LANES = 128

HIGH = lax.Precision.HIGH
MESH = pl.DeviceIdType.MESH


def from_behind(x, axis, by):
    devices = lax.axis_size(axis)
    pairs = [(i, i + by) for i in range(devices) if 0 <= i + by < devices]
    return lax.ppermute(x, axis, pairs)


def lag_table(kernels, lag):
    classes, taps = kernels.shape
    rows, hours = lag.shape
    onehot = (lag.T[None, :, :] == jnp.arange(taps)[:, None, None]).astype(jnp.float32)
    picked = jnp.dot(kernels, onehot.reshape(taps, hours * rows), precision=HIGH)
    return picked.reshape(classes, hours, rows)


def class_mix(extended, table, selector):
    spread = lax.dot_general(extended, table, (((1,), (2,)), ((), ())), precision=lax.Precision.HIGH)
    return jnp.sum(spread * selector[:, :, None], axis=1)


def squared(values):
    return jnp.sum(values * values)


def _total_body(x_ref, o_ref, tm_rows, all_rows, own_sem, tsend, trecv, bsend, brecv, *, nb, nt):
    me = lax.axis_index("basin")
    hb = lax.axis_index("tm")
    barrier = pltpu.get_barrier_semaphore()
    for j in range(1, nt):
        pl.semaphore_signal(barrier, inc=1, device_id=(me, lax.rem(hb + j, nt)), device_id_type=MESH)
    for k in range(1, nb):
        pl.semaphore_signal(barrier, inc=1, device_id=(lax.rem(me + k, nb), hb), device_id_type=MESH)
    pl.semaphore_wait(barrier, nt - 1 + nb - 1)

    own = pltpu.make_async_copy(x_ref, tm_rows.at[pl.ds(hb, 1)], own_sem.at[0])
    own.start()
    sends = []
    for j in range(1, nt):
        copy = pltpu.make_async_remote_copy(
            src_ref=x_ref, dst_ref=tm_rows.at[pl.ds(hb, 1)], send_sem=tsend.at[j], recv_sem=trecv.at[j],
            device_id=(me, lax.rem(hb + j, nt)), device_id_type=MESH,
        )
        copy.start()
        sends.append(copy)
    own.wait()
    for j in range(1, nt):
        sends[j - 1].wait_send()
        origin = lax.rem(hb + nt - j, nt)
        pltpu.make_async_remote_copy(
            src_ref=x_ref, dst_ref=tm_rows.at[pl.ds(origin, 1)], send_sem=tsend.at[j], recv_sem=trecv.at[j],
            device_id=(me, origin), device_id_type=MESH,
        ).wait_recv()

    own_block = pltpu.make_async_copy(tm_rows, all_rows.at[me], own_sem.at[1])
    own_block.start()
    blocks = []
    for k in range(1, nb):
        copy = pltpu.make_async_remote_copy(
            src_ref=tm_rows, dst_ref=all_rows.at[me], send_sem=bsend.at[k], recv_sem=brecv.at[k],
            device_id=(lax.rem(me + k, nb), hb), device_id_type=MESH,
        )
        copy.start()
        blocks.append(copy)
    own_block.wait()
    for k in range(1, nb):
        blocks[k - 1].wait_send()
        source = lax.rem(me + nb - k, nb)
        pltpu.make_async_remote_copy(
            src_ref=tm_rows, dst_ref=all_rows.at[source], send_sem=bsend.at[k], recv_sem=brecv.at[k],
            device_id=(source, hb), device_id_type=MESH,
        ).wait_recv()
    o_ref[...] = jnp.sum(all_rows[...].reshape(nb * nt, LANES), axis=0, keepdims=True)


def global_total(value):
    nb = lax.axis_size("basin")
    nt = lax.axis_size("tm")
    out = pl.pallas_call(
        functools.partial(_total_body, nb=nb, nt=nt),
        out_shape=jax.ShapeDtypeStruct((1, LANES), jnp.float32),
        in_specs=[pl.BlockSpec(memory_space=pltpu.VMEM)],
        out_specs=pl.BlockSpec(memory_space=pltpu.VMEM),
        scratch_shapes=[
            pltpu.VMEM((nt, LANES), jnp.float32),
            pltpu.VMEM((nb, nt, LANES), jnp.float32),
            pltpu.SemaphoreType.DMA((2,)),
            pltpu.SemaphoreType.DMA((nt,)),
            pltpu.SemaphoreType.DMA((nt,)),
            pltpu.SemaphoreType.DMA((nb,)),
            pltpu.SemaphoreType.DMA((nb,)),
        ],
        compiler_params=pltpu.CompilerParams(collective_id=0, has_side_effects=True),
    )(as_row(value))
    return out[0, 0]


def _exchange_body(x_ref, c_ref, o_ref, t_ref, landed, carried, own_sem, send_sem, recv_sem, csend, crecv, *, nb):
    me = lax.axis_index("basin")
    hour_block = lax.axis_index("tm")
    barrier = pltpu.get_barrier_semaphore()
    for k in range(1, nb):
        pl.semaphore_signal(
            barrier, inc=1, device_id=(lax.rem(me + k, nb), hour_block), device_id_type=MESH
        )
    pl.semaphore_wait(barrier, nb - 1)
    own = pltpu.make_async_copy(x_ref.at[me], landed.at[me], own_sem.at[0])
    own.start()
    own_carry = pltpu.make_async_copy(c_ref, carried.at[pl.ds(me, 1)], own_sem.at[1])
    own_carry.start()
    copies = []
    for k in range(1, nb):
        peer = lax.rem(me + k, nb)
        copy = pltpu.make_async_remote_copy(
            src_ref=x_ref.at[peer],
            dst_ref=landed.at[me],
            send_sem=send_sem.at[k],
            recv_sem=recv_sem.at[k],
            device_id=(peer, hour_block),
            device_id_type=MESH,
        )
        copy.start()
        carry = pltpu.make_async_remote_copy(
            src_ref=c_ref,
            dst_ref=carried.at[pl.ds(me, 1)],
            send_sem=csend.at[k],
            recv_sem=crecv.at[k],
            device_id=(peer, hour_block),
            device_id_type=MESH,
        )
        carry.start()
        copies.append((copy, carry))
    own.wait()
    own_carry.wait()
    for k in range(1, nb):
        copies[k - 1][0].wait_send()
        copies[k - 1][1].wait_send()
        source = lax.rem(me + nb - k, nb)
        pltpu.make_async_remote_copy(
            src_ref=x_ref.at[source],
            dst_ref=landed.at[source],
            send_sem=send_sem.at[k],
            recv_sem=recv_sem.at[k],
            device_id=(source, hour_block),
            device_id_type=MESH,
        ).wait_recv()
        pltpu.make_async_remote_copy(
            src_ref=c_ref,
            dst_ref=carried.at[pl.ds(source, 1)],
            send_sem=csend.at[k],
            recv_sem=crecv.at[k],
            device_id=(source, hour_block),
            device_id_type=MESH,
        ).wait_recv()
    o_ref[...] = landed[...]
    t_ref[...] = jnp.sum(carried[...], axis=0, keepdims=True)


def as_row(value):
    if value.ndim == 2:
        return value
    return jnp.broadcast_to(value.astype(jnp.float32), (1, LANES))


def basin_exchange(x, carry, ident=1):
    nb = lax.axis_size("basin")
    total, hours = x.shape
    shaped = x.reshape(nb, total // nb, hours)
    out, summed = pl.pallas_call(
        functools.partial(_exchange_body, nb=nb),
        out_shape=(
            jax.ShapeDtypeStruct(shaped.shape, jnp.float32),
            jax.ShapeDtypeStruct((1, LANES), jnp.float32),
        ),
        in_specs=[pl.BlockSpec(memory_space=pltpu.VMEM)] * 2,
        out_specs=(pl.BlockSpec(memory_space=pltpu.VMEM),) * 2,
        scratch_shapes=[
            pltpu.VMEM(shaped.shape, jnp.float32),
            pltpu.VMEM((nb, LANES), jnp.float32),
            pltpu.SemaphoreType.DMA((2,)),
            pltpu.SemaphoreType.DMA((nb,)),
            pltpu.SemaphoreType.DMA((nb,)),
            pltpu.SemaphoreType.DMA((nb,)),
            pltpu.SemaphoreType.DMA((nb,)),
        ],
        compiler_params=pltpu.CompilerParams(collective_id=ident, has_side_effects=True),
    )(shaped, as_row(carry))
    return out.reshape(total, hours), summed


def _shift_body(x_ref, c_ref, o_ref, t_ref, held, carried, own_sem, dsend, drecv, csend, crecv, *, nt, by):
    basin = lax.axis_index("basin")
    me = lax.axis_index("tm")
    barrier = pltpu.get_barrier_semaphore()
    for k in range(1, nt):
        pl.semaphore_signal(
            barrier, inc=1, device_id=(basin, lax.rem(me + k, nt)), device_id_type=MESH
        )
    pl.semaphore_wait(barrier, nt - 1)

    target = me + by
    source = me - by
    has_target = jnp.logical_and(target >= 0, target < nt)
    has_source = jnp.logical_and(source >= 0, source < nt)
    data = pltpu.make_async_remote_copy(
        src_ref=x_ref,
        dst_ref=held,
        send_sem=dsend,
        recv_sem=drecv,
        device_id=(basin, lax.rem(target + nt, nt)),
        device_id_type=MESH,
    )

    @pl.when(has_target)
    def _():
        data.start()

    own = pltpu.make_async_copy(c_ref, carried.at[pl.ds(me, 1)], own_sem)
    own.start()
    copies = []
    for k in range(1, nt):
        copy = pltpu.make_async_remote_copy(
            src_ref=c_ref,
            dst_ref=carried.at[pl.ds(me, 1)],
            send_sem=csend.at[k],
            recv_sem=crecv.at[k],
            device_id=(basin, lax.rem(me + k, nt)),
            device_id_type=MESH,
        )
        copy.start()
        copies.append(copy)
    own.wait()
    for k in range(1, nt):
        copies[k - 1].wait_send()
        origin = lax.rem(me + nt - k, nt)
        pltpu.make_async_remote_copy(
            src_ref=c_ref,
            dst_ref=carried.at[pl.ds(origin, 1)],
            send_sem=csend.at[k],
            recv_sem=crecv.at[k],
            device_id=(basin, origin),
            device_id_type=MESH,
        ).wait_recv()
    t_ref[...] = jnp.sum(carried[...], axis=0, keepdims=True)

    @pl.when(has_target)
    def _():
        data.wait_send()

    @pl.when(has_source)
    def _():
        data.wait_recv()
        o_ref[...] = held[...]

    @pl.when(jnp.logical_not(has_source))
    def _():
        o_ref[...] = jnp.zeros(o_ref.shape, o_ref.dtype)


def tm_shift(x, carry, by, ident):
    nt = lax.axis_size("tm")
    c = as_row(carry)
    out, summed = pl.pallas_call(
        functools.partial(_shift_body, nt=nt, by=by),
        out_shape=(
            jax.ShapeDtypeStruct(x.shape, jnp.float32),
            jax.ShapeDtypeStruct((1, LANES), jnp.float32),
        ),
        in_specs=[pl.BlockSpec(memory_space=pltpu.VMEM)] * 2,
        out_specs=(pl.BlockSpec(memory_space=pltpu.VMEM),) * 2,
        scratch_shapes=[
            pltpu.VMEM(x.shape, jnp.float32),
            pltpu.VMEM((nt, LANES), jnp.float32),
            pltpu.SemaphoreType.DMA(()),
            pltpu.SemaphoreType.DMA(()),
            pltpu.SemaphoreType.DMA(()),
            pltpu.SemaphoreType.DMA((nt,)),
            pltpu.SemaphoreType.DMA((nt,)),
        ],
        compiler_params=pltpu.CompilerParams(collective_id=ident, has_side_effects=True),
    )(x, c)
    return out, summed


def shards(incidence, row_gauge, gauge_kernel, kernels, observed, first_guess):
    weights = incidence.astype(jnp.float32)
    blocks, slots, width = weights.shape
    gauges_here, hours = observed.shape
    owners = lax.axis_size("basin")
    classes = kernels.shape[0]
    partials = blocks * slots
    outer = jnp.arange(2 * hours)[:, None]
    inner = jnp.arange(hours)[None, :]
    table_fwd = lag_table(kernels, inner + hours - outer)
    table_bwd = lag_table(kernels, outer - inner)
    selector = (gauge_kernel[:, None] == jnp.arange(classes)[None, :]).astype(jnp.float32)

    owner = row_gauge // gauges_here
    local = row_gauge % gauges_here
    hit = owner[:, None] == jnp.arange(owners)[None, :]
    rank = jnp.cumsum(hit.astype(jnp.int32), axis=0) - 1
    dest = owner * CAP + jnp.sum(jnp.where(hit, rank, 0), axis=1)
    entries = owners * CAP
    place = (jnp.arange(entries)[:, None] == dest[None, :]).astype(jnp.float32)
    sent_ids = jnp.full((entries,), -1, jnp.int32).at[dest].set(local)
    id_rows = jnp.zeros((owners, 8, hours), jnp.float32)
    id_rows = id_rows.at[:, 0, :CAP].set(sent_ids.reshape(owners, CAP).astype(jnp.float32))
    routing = {}

    def forward(field):
        partial_value = jnp.einsum(
            "bjr,brt->bjt", weights, field.reshape(blocks, width, hours), precision=HIGH
        )
        outgoing = jnp.dot(place, partial_value.reshape(partials, hours), precision=HIGH)
        if "gather" not in routing:
            packed = jnp.concatenate([outgoing.reshape(owners, CAP, hours), id_rows], axis=1)
            landed, basin_sq = basin_exchange(packed.reshape(owners * (CAP + 8), hours), squared(field), 5)
            landed = landed.reshape(owners, CAP + 8, hours)
            got_ids = landed[:, CAP, :CAP].astype(jnp.int32).reshape(entries)
            routing["gather"] = (jnp.arange(gauges_here)[:, None] == got_ids[None, :]).astype(jnp.float32)
            incoming = landed[:, :CAP, :].reshape(entries, hours)
        else:
            incoming, basin_sq = basin_exchange(outgoing, squared(field))
        gather = routing["gather"]
        sums = jnp.dot(gather, incoming, precision=HIGH)
        earlier, total_sq = tm_shift(sums, basin_sq, 1, 2)
        return class_mix(jnp.concatenate([earlier, sums], axis=1), table_fwd, selector), total_sq[0, 0]

    def backward(series):
        later, tm_sq = tm_shift(series, squared(series), -1, 3)
        upstream = class_mix(jnp.concatenate([series, later], axis=1), table_bwd, selector)
        outgoing = jnp.dot(routing["gather"].T, upstream, precision=lax.Precision.HIGH)
        incoming, total_sq = basin_exchange(outgoing, tm_sq)
        rows = jnp.dot(place.T, incoming, precision=lax.Precision.HIGH)
        spread = jnp.einsum(
            "bjr,bjt->brt", weights, rows.reshape(blocks, slots, hours), precision=lax.Precision.HIGH
        )
        return spread.reshape(blocks * width, hours), total_sq[0, 0]

    start = observed - forward(first_guess)[0]
    pulled_start, beta_sq = backward(start)
    beta = jnp.sqrt(beta_sq)
    u = start / beta
    pulled = pulled_start / beta
    forward_pulled, alpha_sq = forward(pulled)
    alpha = jnp.sqrt(alpha_sq)
    v = pulled / alpha
    w = v
    correction = jnp.zeros(first_guess.shape, jnp.float32)
    phibar = beta
    rhobar = alpha
    for step in range(ITERS):
        final = step == ITERS - 1
        p = forward_pulled / alpha - alpha * u
        if final:
            beta = jnp.sqrt(global_total(squared(p)))
        else:
            pulled_p, beta_sq = backward(p)
            beta = jnp.sqrt(beta_sq)
            pulled = pulled_p / beta - beta * v
            forward_pulled, alpha_next = forward(pulled)
            alpha_next = jnp.sqrt(alpha_next)
            v_next = pulled / alpha_next
        u = p / beta
        rho = jnp.sqrt(rhobar * rhobar + beta * beta)
        cosine = rhobar / rho
        sine = beta / rho
        phi = cosine * phibar
        phibar = sine * phibar
        correction = correction + phi / rho * w
        if not final:
            theta = sine * alpha_next
            rhobar = -cosine * alpha_next
            w = v_next - theta / rho * w
            v = v_next
            alpha = alpha_next
    return first_guess + correction


def solution(mesh):
    in_specs = (
        P("basin", None, None),
        P("basin"),
        P("basin"),
        P(),
        P("basin", "tm"),
        P("basin", "tm"),
    )
    out_specs = P("basin", "tm")
    return jax.shard_map(shards, mesh=mesh, in_specs=in_specs, out_specs=out_specs, check_vma=False)
```

```python
import functools

import jax
import jax.numpy as jnp
from jax import lax
from jax.experimental import pallas as pl
from jax.experimental.pallas import tpu as pltpu
from jax.sharding import PartitionSpec as P

ITERS = 3
CAP = 32
LANES = 128

HIGH = lax.Precision.HIGH
MESH = pl.DeviceIdType.MESH


def from_behind(x, axis, by):
    devices = lax.axis_size(axis)
    pairs = [(i, i + by) for i in range(devices) if 0 <= i + by < devices]
    return lax.ppermute(x, axis, pairs)


def lag_table(kernels, lag):
    classes, taps = kernels.shape
    rows, hours = lag.shape
    onehot = (lag.T[None, :, :] == jnp.arange(taps)[:, None, None]).astype(jnp.float32)
    picked = jnp.dot(kernels, onehot.reshape(taps, hours * rows), precision=HIGH)
    return picked.reshape(classes, hours, rows)


def class_mix(extended, table, selector):
    spread = lax.dot_general(extended, table, (((1,), (2,)), ((), ())), precision=lax.Precision.HIGH)
    return jnp.sum(spread * selector[:, :, None], axis=1)


def squared(values):
    return jnp.sum(values * values)


def _total_body(x_ref, o_ref, tm_rows, all_rows, own_sem, tsend, trecv, bsend, brecv, *, nb, nt):
    me = lax.axis_index("basin")
    hb = lax.axis_index("tm")
    barrier = pltpu.get_barrier_semaphore()
    for j in range(1, nt):
        pl.semaphore_signal(barrier, inc=1, device_id=(me, lax.rem(hb + j, nt)), device_id_type=MESH)
    for k in range(1, nb):
        pl.semaphore_signal(barrier, inc=1, device_id=(lax.rem(me + k, nb), hb), device_id_type=MESH)
    pl.semaphore_wait(barrier, nt - 1 + nb - 1)

    own = pltpu.make_async_copy(x_ref, tm_rows.at[pl.ds(hb, 1)], own_sem.at[0])
    own.start()
    sends = []
    for j in range(1, nt):
        copy = pltpu.make_async_remote_copy(
            src_ref=x_ref, dst_ref=tm_rows.at[pl.ds(hb, 1)], send_sem=tsend.at[j], recv_sem=trecv.at[j],
            device_id=(me, lax.rem(hb + j, nt)), device_id_type=MESH,
        )
        copy.start()
        sends.append(copy)
    own.wait()
    for j in range(1, nt):
        sends[j - 1].wait_send()
        origin = lax.rem(hb + nt - j, nt)
        pltpu.make_async_remote_copy(
            src_ref=x_ref, dst_ref=tm_rows.at[pl.ds(origin, 1)], send_sem=tsend.at[j], recv_sem=trecv.at[j],
            device_id=(me, origin), device_id_type=MESH,
        ).wait_recv()

    own_block = pltpu.make_async_copy(tm_rows, all_rows.at[me], own_sem.at[1])
    own_block.start()
    blocks = []
    for k in range(1, nb):
        copy = pltpu.make_async_remote_copy(
            src_ref=tm_rows, dst_ref=all_rows.at[me], send_sem=bsend.at[k], recv_sem=brecv.at[k],
            device_id=(lax.rem(me + k, nb), hb), device_id_type=MESH,
        )
        copy.start()
        blocks.append(copy)
    own_block.wait()
    for k in range(1, nb):
        blocks[k - 1].wait_send()
        source = lax.rem(me + nb - k, nb)
        pltpu.make_async_remote_copy(
            src_ref=tm_rows, dst_ref=all_rows.at[source], send_sem=bsend.at[k], recv_sem=brecv.at[k],
            device_id=(source, hb), device_id_type=MESH,
        ).wait_recv()
    o_ref[...] = jnp.sum(all_rows[...].reshape(nb * nt, LANES), axis=0, keepdims=True)


def global_total(value):
    nb = lax.axis_size("basin")
    nt = lax.axis_size("tm")
    out = pl.pallas_call(
        functools.partial(_total_body, nb=nb, nt=nt),
        out_shape=jax.ShapeDtypeStruct((1, LANES), jnp.float32),
        in_specs=[pl.BlockSpec(memory_space=pltpu.VMEM)],
        out_specs=pl.BlockSpec(memory_space=pltpu.VMEM),
        scratch_shapes=[
            pltpu.VMEM((nt, LANES), jnp.float32),
            pltpu.VMEM((nb, nt, LANES), jnp.float32),
            pltpu.SemaphoreType.DMA((2,)),
            pltpu.SemaphoreType.DMA((nt,)),
            pltpu.SemaphoreType.DMA((nt,)),
            pltpu.SemaphoreType.DMA((nb,)),
            pltpu.SemaphoreType.DMA((nb,)),
        ],
        compiler_params=pltpu.CompilerParams(collective_id=0, has_side_effects=True),
    )(as_row(value))
    return out[0, 0]


def _exchange_body(x_ref, c_ref, o_ref, t_ref, landed, carried, own_sem, send_sem, recv_sem, csend, crecv, *, nb):
    me = lax.axis_index("basin")
    hour_block = lax.axis_index("tm")
    barrier = pltpu.get_barrier_semaphore()
    for k in range(1, nb):
        pl.semaphore_signal(
            barrier, inc=1, device_id=(lax.rem(me + k, nb), hour_block), device_id_type=MESH
        )
    pl.semaphore_wait(barrier, nb - 1)
    own = pltpu.make_async_copy(x_ref.at[me], landed.at[me], own_sem.at[0])
    own.start()
    own_carry = pltpu.make_async_copy(c_ref, carried.at[pl.ds(me, 1)], own_sem.at[1])
    own_carry.start()
    copies = []
    for k in range(1, nb):
        peer = lax.rem(me + k, nb)
        copy = pltpu.make_async_remote_copy(
            src_ref=x_ref.at[peer],
            dst_ref=landed.at[me],
            send_sem=send_sem.at[k],
            recv_sem=recv_sem.at[k],
            device_id=(peer, hour_block),
            device_id_type=MESH,
        )
        copy.start()
        carry = pltpu.make_async_remote_copy(
            src_ref=c_ref,
            dst_ref=carried.at[pl.ds(me, 1)],
            send_sem=csend.at[k],
            recv_sem=crecv.at[k],
            device_id=(peer, hour_block),
            device_id_type=MESH,
        )
        carry.start()
        copies.append((copy, carry))
    own.wait()
    own_carry.wait()
    for k in range(1, nb):
        copies[k - 1][0].wait_send()
        copies[k - 1][1].wait_send()
        source = lax.rem(me + nb - k, nb)
        pltpu.make_async_remote_copy(
            src_ref=x_ref.at[source],
            dst_ref=landed.at[source],
            send_sem=send_sem.at[k],
            recv_sem=recv_sem.at[k],
            device_id=(source, hour_block),
            device_id_type=MESH,
        ).wait_recv()
        pltpu.make_async_remote_copy(
            src_ref=c_ref,
            dst_ref=carried.at[pl.ds(source, 1)],
            send_sem=csend.at[k],
            recv_sem=crecv.at[k],
            device_id=(source, hour_block),
            device_id_type=MESH,
        ).wait_recv()
    o_ref[...] = landed[...]
    t_ref[...] = jnp.sum(carried[...], axis=0, keepdims=True)


def as_row(value):
    if value.ndim == 2:
        return value
    return jnp.broadcast_to(value.astype(jnp.float32), (1, LANES))


def basin_exchange(x, carry, ident=1):
    nb = lax.axis_size("basin")
    total, hours = x.shape
    shaped = x.reshape(nb, total // nb, hours)
    out, summed = pl.pallas_call(
        functools.partial(_exchange_body, nb=nb),
        out_shape=(
            jax.ShapeDtypeStruct(shaped.shape, jnp.float32),
            jax.ShapeDtypeStruct((1, LANES), jnp.float32),
        ),
        in_specs=[pl.BlockSpec(memory_space=pltpu.VMEM)] * 2,
        out_specs=(pl.BlockSpec(memory_space=pltpu.VMEM),) * 2,
        scratch_shapes=[
            pltpu.VMEM(shaped.shape, jnp.float32),
            pltpu.VMEM((nb, LANES), jnp.float32),
            pltpu.SemaphoreType.DMA((2,)),
            pltpu.SemaphoreType.DMA((nb,)),
            pltpu.SemaphoreType.DMA((nb,)),
            pltpu.SemaphoreType.DMA((nb,)),
            pltpu.SemaphoreType.DMA((nb,)),
        ],
        compiler_params=pltpu.CompilerParams(collective_id=ident, has_side_effects=True),
    )(shaped, as_row(carry))
    return out.reshape(total, hours), summed


def _shift_body(x_ref, c_ref, o_ref, t_ref, held, carried, own_sem, dsend, drecv, csend, crecv, *, nt, by):
    basin = lax.axis_index("basin")
    me = lax.axis_index("tm")
    barrier = pltpu.get_barrier_semaphore()
    for k in range(1, nt):
        pl.semaphore_signal(
            barrier, inc=1, device_id=(basin, lax.rem(me + k, nt)), device_id_type=MESH
        )
    pl.semaphore_wait(barrier, nt - 1)

    target = me + by
    source = me - by
    has_target = jnp.logical_and(target >= 0, target < nt)
    has_source = jnp.logical_and(source >= 0, source < nt)
    data = pltpu.make_async_remote_copy(
        src_ref=x_ref,
        dst_ref=held,
        send_sem=dsend,
        recv_sem=drecv,
        device_id=(basin, lax.rem(target + nt, nt)),
        device_id_type=MESH,
    )

    @pl.when(has_target)
    def _():
        data.start()

    own = pltpu.make_async_copy(c_ref, carried.at[pl.ds(me, 1)], own_sem)
    own.start()
    copies = []
    for k in range(1, nt):
        copy = pltpu.make_async_remote_copy(
            src_ref=c_ref,
            dst_ref=carried.at[pl.ds(me, 1)],
            send_sem=csend.at[k],
            recv_sem=crecv.at[k],
            device_id=(basin, lax.rem(me + k, nt)),
            device_id_type=MESH,
        )
        copy.start()
        copies.append(copy)
    own.wait()
    for k in range(1, nt):
        copies[k - 1].wait_send()
        origin = lax.rem(me + nt - k, nt)
        pltpu.make_async_remote_copy(
            src_ref=c_ref,
            dst_ref=carried.at[pl.ds(origin, 1)],
            send_sem=csend.at[k],
            recv_sem=crecv.at[k],
            device_id=(basin, origin),
            device_id_type=MESH,
        ).wait_recv()
    t_ref[...] = jnp.sum(carried[...], axis=0, keepdims=True)

    @pl.when(has_target)
    def _():
        data.wait_send()

    @pl.when(has_source)
    def _():
        data.wait_recv()
        o_ref[...] = held[...]

    @pl.when(jnp.logical_not(has_source))
    def _():
        o_ref[...] = jnp.zeros(o_ref.shape, o_ref.dtype)


def tm_shift(x, carry, by, ident):
    nt = lax.axis_size("tm")
    c = as_row(carry)
    out, summed = pl.pallas_call(
        functools.partial(_shift_body, nt=nt, by=by),
        out_shape=(
            jax.ShapeDtypeStruct(x.shape, jnp.float32),
            jax.ShapeDtypeStruct((1, LANES), jnp.float32),
        ),
        in_specs=[pl.BlockSpec(memory_space=pltpu.VMEM)] * 2,
        out_specs=(pl.BlockSpec(memory_space=pltpu.VMEM),) * 2,
        scratch_shapes=[
            pltpu.VMEM(x.shape, jnp.float32),
            pltpu.VMEM((nt, LANES), jnp.float32),
            pltpu.SemaphoreType.DMA(()),
            pltpu.SemaphoreType.DMA(()),
            pltpu.SemaphoreType.DMA(()),
            pltpu.SemaphoreType.DMA((nt,)),
            pltpu.SemaphoreType.DMA((nt,)),
        ],
        compiler_params=pltpu.CompilerParams(collective_id=ident, has_side_effects=True),
    )(x, c)
    return out, summed


def shards(incidence, row_gauge, gauge_kernel, kernels, observed, first_guess):
    weights = incidence.astype(jnp.float32)
    blocks, slots, width = weights.shape
    gauges_here, hours = observed.shape
    owners = lax.axis_size("basin")
    classes = kernels.shape[0]
    partials = blocks * slots
    outer = jnp.arange(2 * hours)[:, None]
    inner = jnp.arange(hours)[None, :]
    table_fwd = lag_table(kernels, inner + hours - outer)
    table_bwd = lag_table(kernels, outer - inner)
    selector = (gauge_kernel[:, None] == jnp.arange(classes)[None, :]).astype(jnp.float32)

    owner = row_gauge // gauges_here
    local = row_gauge % gauges_here
    hit = owner[:, None] == jnp.arange(owners)[None, :]
    rank = jnp.cumsum(hit.astype(jnp.int32), axis=0) - 1
    dest = owner * CAP + jnp.sum(jnp.where(hit, rank, 0), axis=1)
    entries = owners * CAP
    place = (jnp.arange(entries)[:, None] == dest[None, :]).astype(jnp.float32)
    sent_ids = jnp.full((entries,), -1, jnp.int32).at[dest].set(local)
    id_rows = jnp.zeros((owners, 8, hours), jnp.float32)
    id_rows = id_rows.at[:, 0, :CAP].set(sent_ids.reshape(owners, CAP).astype(jnp.float32))
    routing = {}

    def forward(field, carry=None):
        partial_value = jnp.einsum(
            "bjr,brt->bjt", weights, field.reshape(blocks, width, hours), precision=HIGH
        )
        outgoing = jnp.dot(place, partial_value.reshape(partials, hours), precision=HIGH)
        if "gather" not in routing:
            packed = jnp.concatenate([outgoing.reshape(owners, CAP, hours), id_rows], axis=1)
            landed, basin_sq = basin_exchange(packed.reshape(owners * (CAP + 8), hours), carry, 5)
            landed = landed.reshape(owners, CAP + 8, hours)
            got_ids = landed[:, CAP, :CAP].astype(jnp.int32).reshape(entries)
            routing["gather"] = (jnp.arange(gauges_here)[:, None] == got_ids[None, :]).astype(jnp.float32)
            incoming = landed[:, :CAP, :].reshape(entries, hours)
        else:
            incoming, basin_sq = basin_exchange(outgoing, squared(field))
        gather = routing["gather"]
        sums = jnp.dot(gather, incoming, precision=HIGH)
        earlier, total_sq = tm_shift(sums, basin_sq, 1, 2)
        return class_mix(jnp.concatenate([earlier, sums], axis=1), table_fwd, selector), total_sq[0, 0]

    def backward(series):
        later, tm_sq = tm_shift(series, squared(series), -1, 3)
        upstream = class_mix(jnp.concatenate([series, later], axis=1), table_bwd, selector)
        outgoing = jnp.dot(routing["gather"].T, upstream, precision=lax.Precision.HIGH)
        incoming, total_sq = basin_exchange(outgoing, tm_sq)
        rows = jnp.dot(place.T, incoming, precision=lax.Precision.HIGH)
        spread = jnp.einsum(
            "bjr,bjt->brt", weights, rows.reshape(blocks, slots, hours), precision=lax.Precision.HIGH
        )
        return spread.reshape(blocks * width, hours), total_sq[0, 0]

    start = observed - forward(first_guess, jnp.zeros((), jnp.float32))[0]
    pulled_start, beta_sq = backward(start)
    beta = jnp.sqrt(beta_sq)
    u = start / beta
    pulled = pulled_start / beta
    forward_pulled, alpha_sq = forward(pulled)
    alpha = jnp.sqrt(alpha_sq)
    v = pulled / alpha
    w = v
    estimate = first_guess
    phibar = beta
    rhobar = alpha
    for step in range(ITERS):
        final = step == ITERS - 1
        p = forward_pulled / alpha - alpha * u
        if final:
            beta = jnp.sqrt(global_total(squared(p)))
        else:
            pulled_p, beta_sq = backward(p)
            beta = jnp.sqrt(beta_sq)
            pulled = pulled_p / beta - beta * v
            forward_pulled, alpha_next = forward(pulled)
            alpha_next = jnp.sqrt(alpha_next)
            v_next = pulled / alpha_next
        u = p / beta
        rho = jnp.sqrt(rhobar * rhobar + beta * beta)
        cosine = rhobar / rho
        sine = beta / rho
        phi = cosine * phibar
        phibar = sine * phibar
        estimate = estimate + phi / rho * w
        if not final:
            theta = sine * alpha_next
            rhobar = -cosine * alpha_next
            w = v_next - theta / rho * w
            v = v_next
            alpha = alpha_next
    return estimate


def solution(mesh):
    in_specs = (
        P("basin", None, None),
        P("basin"),
        P("basin"),
        P(),
        P("basin", "tm"),
        P("basin", "tm"),
    )
    out_specs = P("basin", "tm")
    return jax.shard_map(shards, mesh=mesh, in_specs=in_specs, out_specs=out_specs, check_vma=False)
```

```python
import functools

import jax
import jax.numpy as jnp
from jax import lax
from jax.experimental import pallas as pl
from jax.experimental.pallas import tpu as pltpu
from jax.sharding import PartitionSpec as P

ITERS = 3
CAP = 32
LANES = 128

HIGH = lax.Precision.HIGH
MESH = pl.DeviceIdType.MESH


def from_behind(x, axis, by):
    devices = lax.axis_size(axis)
    pairs = [(i, i + by) for i in range(devices) if 0 <= i + by < devices]
    return lax.ppermute(x, axis, pairs)


def lag_table(kernels, lag):
    classes, taps = kernels.shape
    rows, hours = lag.shape
    onehot = (lag.T[None, :, :] == jnp.arange(taps)[:, None, None]).astype(jnp.float32)
    picked = jnp.dot(kernels, onehot.reshape(taps, hours * rows), precision=HIGH)
    return picked.reshape(classes, hours, rows)


def class_mix(extended, table, selector):
    spread = lax.dot_general(extended, table, (((1,), (2,)), ((), ())), precision=lax.Precision.HIGH)
    return jnp.sum(spread * selector[:, :, None], axis=1)


def squared(values):
    return jnp.sum(values * values)


def squared_row(values):
    if values.shape[-1] == LANES:
        return jnp.sum(values * values, axis=0, keepdims=True)
    return as_row(squared(values))


def _total_body(x_ref, o_ref, tm_rows, all_rows, own_sem, tsend, trecv, bsend, brecv, *, nb, nt):
    me = lax.axis_index("basin")
    hb = lax.axis_index("tm")
    barrier = pltpu.get_barrier_semaphore()
    for j in range(1, nt):
        pl.semaphore_signal(barrier, inc=1, device_id=(me, lax.rem(hb + j, nt)), device_id_type=MESH)
    for k in range(1, nb):
        pl.semaphore_signal(barrier, inc=1, device_id=(lax.rem(me + k, nb), hb), device_id_type=MESH)
    pl.semaphore_wait(barrier, nt - 1 + nb - 1)

    own = pltpu.make_async_copy(x_ref, tm_rows.at[pl.ds(hb, 1)], own_sem.at[0])
    own.start()
    sends = []
    for j in range(1, nt):
        copy = pltpu.make_async_remote_copy(
            src_ref=x_ref, dst_ref=tm_rows.at[pl.ds(hb, 1)], send_sem=tsend.at[j], recv_sem=trecv.at[j],
            device_id=(me, lax.rem(hb + j, nt)), device_id_type=MESH,
        )
        copy.start()
        sends.append(copy)
    own.wait()
    for j in range(1, nt):
        sends[j - 1].wait_send()
        origin = lax.rem(hb + nt - j, nt)
        pltpu.make_async_remote_copy(
            src_ref=x_ref, dst_ref=tm_rows.at[pl.ds(origin, 1)], send_sem=tsend.at[j], recv_sem=trecv.at[j],
            device_id=(me, origin), device_id_type=MESH,
        ).wait_recv()

    own_block = pltpu.make_async_copy(tm_rows, all_rows.at[me], own_sem.at[1])
    own_block.start()
    blocks = []
    for k in range(1, nb):
        copy = pltpu.make_async_remote_copy(
            src_ref=tm_rows, dst_ref=all_rows.at[me], send_sem=bsend.at[k], recv_sem=brecv.at[k],
            device_id=(lax.rem(me + k, nb), hb), device_id_type=MESH,
        )
        copy.start()
        blocks.append(copy)
    own_block.wait()
    for k in range(1, nb):
        blocks[k - 1].wait_send()
        source = lax.rem(me + nb - k, nb)
        pltpu.make_async_remote_copy(
            src_ref=tm_rows, dst_ref=all_rows.at[source], send_sem=bsend.at[k], recv_sem=brecv.at[k],
            device_id=(source, hb), device_id_type=MESH,
        ).wait_recv()
    o_ref[...] = jnp.sum(all_rows[...].reshape(nb * nt, LANES), axis=0, keepdims=True)


def global_total(value):
    nb = lax.axis_size("basin")
    nt = lax.axis_size("tm")
    out = pl.pallas_call(
        functools.partial(_total_body, nb=nb, nt=nt),
        out_shape=jax.ShapeDtypeStruct((1, LANES), jnp.float32),
        in_specs=[pl.BlockSpec(memory_space=pltpu.VMEM)],
        out_specs=pl.BlockSpec(memory_space=pltpu.VMEM),
        scratch_shapes=[
            pltpu.VMEM((nt, LANES), jnp.float32),
            pltpu.VMEM((nb, nt, LANES), jnp.float32),
            pltpu.SemaphoreType.DMA((2,)),
            pltpu.SemaphoreType.DMA((nt,)),
            pltpu.SemaphoreType.DMA((nt,)),
            pltpu.SemaphoreType.DMA((nb,)),
            pltpu.SemaphoreType.DMA((nb,)),
        ],
        compiler_params=pltpu.CompilerParams(collective_id=0, has_side_effects=True),
    )(as_row(value))
    return jnp.sum(out)


def _exchange_body(x_ref, c_ref, o_ref, t_ref, landed, carried, own_sem, send_sem, recv_sem, csend, crecv, *, nb):
    me = lax.axis_index("basin")
    hour_block = lax.axis_index("tm")
    barrier = pltpu.get_barrier_semaphore()
    for k in range(1, nb):
        pl.semaphore_signal(
            barrier, inc=1, device_id=(lax.rem(me + k, nb), hour_block), device_id_type=MESH
        )
    pl.semaphore_wait(barrier, nb - 1)
    own = pltpu.make_async_copy(x_ref.at[me], landed.at[me], own_sem.at[0])
    own.start()
    own_carry = pltpu.make_async_copy(c_ref, carried.at[pl.ds(me, 1)], own_sem.at[1])
    own_carry.start()
    copies = []
    for k in range(1, nb):
        peer = lax.rem(me + k, nb)
        copy = pltpu.make_async_remote_copy(
            src_ref=x_ref.at[peer],
            dst_ref=landed.at[me],
            send_sem=send_sem.at[k],
            recv_sem=recv_sem.at[k],
            device_id=(peer, hour_block),
            device_id_type=MESH,
        )
        copy.start()
        carry = pltpu.make_async_remote_copy(
            src_ref=c_ref,
            dst_ref=carried.at[pl.ds(me, 1)],
            send_sem=csend.at[k],
            recv_sem=crecv.at[k],
            device_id=(peer, hour_block),
            device_id_type=MESH,
        )
        carry.start()
        copies.append((copy, carry))
    own.wait()
    own_carry.wait()
    for k in range(1, nb):
        copies[k - 1][0].wait_send()
        copies[k - 1][1].wait_send()
        source = lax.rem(me + nb - k, nb)
        pltpu.make_async_remote_copy(
            src_ref=x_ref.at[source],
            dst_ref=landed.at[source],
            send_sem=send_sem.at[k],
            recv_sem=recv_sem.at[k],
            device_id=(source, hour_block),
            device_id_type=MESH,
        ).wait_recv()
        pltpu.make_async_remote_copy(
            src_ref=c_ref,
            dst_ref=carried.at[pl.ds(source, 1)],
            send_sem=csend.at[k],
            recv_sem=crecv.at[k],
            device_id=(source, hour_block),
            device_id_type=MESH,
        ).wait_recv()
    o_ref[...] = landed[...]
    t_ref[...] = jnp.sum(carried[...], axis=0, keepdims=True)


def as_row(value):
    if value.ndim == 2:
        return value
    return jnp.broadcast_to(value.astype(jnp.float32), (1, LANES))


def basin_exchange(x, carry, ident=1):
    nb = lax.axis_size("basin")
    total, hours = x.shape
    shaped = x.reshape(nb, total // nb, hours)
    out, summed = pl.pallas_call(
        functools.partial(_exchange_body, nb=nb),
        out_shape=(
            jax.ShapeDtypeStruct(shaped.shape, jnp.float32),
            jax.ShapeDtypeStruct((1, LANES), jnp.float32),
        ),
        in_specs=[pl.BlockSpec(memory_space=pltpu.VMEM)] * 2,
        out_specs=(pl.BlockSpec(memory_space=pltpu.VMEM),) * 2,
        scratch_shapes=[
            pltpu.VMEM(shaped.shape, jnp.float32),
            pltpu.VMEM((nb, LANES), jnp.float32),
            pltpu.SemaphoreType.DMA((2,)),
            pltpu.SemaphoreType.DMA((nb,)),
            pltpu.SemaphoreType.DMA((nb,)),
            pltpu.SemaphoreType.DMA((nb,)),
            pltpu.SemaphoreType.DMA((nb,)),
        ],
        compiler_params=pltpu.CompilerParams(collective_id=ident, has_side_effects=True),
    )(shaped, as_row(carry))
    return out.reshape(total, hours), summed


def _shift_body(x_ref, c_ref, o_ref, t_ref, held, carried, own_sem, dsend, drecv, csend, crecv, *, nt, by):
    basin = lax.axis_index("basin")
    me = lax.axis_index("tm")
    barrier = pltpu.get_barrier_semaphore()
    for k in range(1, nt):
        pl.semaphore_signal(
            barrier, inc=1, device_id=(basin, lax.rem(me + k, nt)), device_id_type=MESH
        )
    pl.semaphore_wait(barrier, nt - 1)

    target = me + by
    source = me - by
    has_target = jnp.logical_and(target >= 0, target < nt)
    has_source = jnp.logical_and(source >= 0, source < nt)
    data = pltpu.make_async_remote_copy(
        src_ref=x_ref,
        dst_ref=held,
        send_sem=dsend,
        recv_sem=drecv,
        device_id=(basin, lax.rem(target + nt, nt)),
        device_id_type=MESH,
    )

    @pl.when(has_target)
    def _():
        data.start()

    own = pltpu.make_async_copy(c_ref, carried.at[pl.ds(me, 1)], own_sem)
    own.start()
    copies = []
    for k in range(1, nt):
        copy = pltpu.make_async_remote_copy(
            src_ref=c_ref,
            dst_ref=carried.at[pl.ds(me, 1)],
            send_sem=csend.at[k],
            recv_sem=crecv.at[k],
            device_id=(basin, lax.rem(me + k, nt)),
            device_id_type=MESH,
        )
        copy.start()
        copies.append(copy)
    own.wait()
    for k in range(1, nt):
        copies[k - 1].wait_send()
        origin = lax.rem(me + nt - k, nt)
        pltpu.make_async_remote_copy(
            src_ref=c_ref,
            dst_ref=carried.at[pl.ds(origin, 1)],
            send_sem=csend.at[k],
            recv_sem=crecv.at[k],
            device_id=(basin, origin),
            device_id_type=MESH,
        ).wait_recv()
    t_ref[...] = jnp.sum(carried[...], axis=0, keepdims=True)

    @pl.when(has_target)
    def _():
        data.wait_send()

    @pl.when(has_source)
    def _():
        data.wait_recv()
        o_ref[...] = held[...]

    @pl.when(jnp.logical_not(has_source))
    def _():
        o_ref[...] = jnp.zeros(o_ref.shape, o_ref.dtype)


def tm_shift(x, carry, by, ident):
    nt = lax.axis_size("tm")
    c = as_row(carry)
    out, summed = pl.pallas_call(
        functools.partial(_shift_body, nt=nt, by=by),
        out_shape=(
            jax.ShapeDtypeStruct(x.shape, jnp.float32),
            jax.ShapeDtypeStruct((1, LANES), jnp.float32),
        ),
        in_specs=[pl.BlockSpec(memory_space=pltpu.VMEM)] * 2,
        out_specs=(pl.BlockSpec(memory_space=pltpu.VMEM),) * 2,
        scratch_shapes=[
            pltpu.VMEM(x.shape, jnp.float32),
            pltpu.VMEM((nt, LANES), jnp.float32),
            pltpu.SemaphoreType.DMA(()),
            pltpu.SemaphoreType.DMA(()),
            pltpu.SemaphoreType.DMA(()),
            pltpu.SemaphoreType.DMA((nt,)),
            pltpu.SemaphoreType.DMA((nt,)),
        ],
        compiler_params=pltpu.CompilerParams(collective_id=ident, has_side_effects=True),
    )(x, c)
    return out, summed


def shards(incidence, row_gauge, gauge_kernel, kernels, observed, first_guess):
    weights = incidence.astype(jnp.float32)
    blocks, slots, width = weights.shape
    gauges_here, hours = observed.shape
    owners = lax.axis_size("basin")
    classes = kernels.shape[0]
    partials = blocks * slots
    outer = jnp.arange(2 * hours)[:, None]
    inner = jnp.arange(hours)[None, :]
    table_fwd = lag_table(kernels, inner + hours - outer)
    table_bwd = lag_table(kernels, outer - inner)
    selector = (gauge_kernel[:, None] == jnp.arange(classes)[None, :]).astype(jnp.float32)

    owner = row_gauge // gauges_here
    local = row_gauge % gauges_here
    hit = owner[:, None] == jnp.arange(owners)[None, :]
    rank = jnp.cumsum(hit.astype(jnp.int32), axis=0) - 1
    dest = owner * CAP + jnp.sum(jnp.where(hit, rank, 0), axis=1)
    entries = owners * CAP
    place = (jnp.arange(entries)[:, None] == dest[None, :]).astype(jnp.float32)
    sent_ids = jnp.full((entries,), -1, jnp.int32).at[dest].set(local)
    id_rows = jnp.zeros((owners, 8, hours), jnp.float32)
    id_rows = id_rows.at[:, 0, :CAP].set(sent_ids.reshape(owners, CAP).astype(jnp.float32))
    routing = {}

    def forward(field, carry=None):
        partial_value = jnp.einsum(
            "bjr,brt->bjt", weights, field.reshape(blocks, width, hours), precision=HIGH
        )
        outgoing = jnp.dot(place, partial_value.reshape(partials, hours), precision=HIGH)
        if "gather" not in routing:
            packed = jnp.concatenate([outgoing.reshape(owners, CAP, hours), id_rows], axis=1)
            landed, basin_sq = basin_exchange(packed.reshape(owners * (CAP + 8), hours), carry, 5)
            landed = landed.reshape(owners, CAP + 8, hours)
            got_ids = landed[:, CAP, :CAP].astype(jnp.int32).reshape(entries)
            routing["gather"] = (jnp.arange(gauges_here)[:, None] == got_ids[None, :]).astype(jnp.float32)
            incoming = landed[:, :CAP, :].reshape(entries, hours)
        else:
            incoming, basin_sq = basin_exchange(outgoing, squared_row(field))
        gather = routing["gather"]
        sums = jnp.dot(gather, incoming, precision=HIGH)
        earlier, total_sq = tm_shift(sums, basin_sq, 1, 2)
        return class_mix(jnp.concatenate([earlier, sums], axis=1), table_fwd, selector), jnp.sum(total_sq)

    def backward(series):
        later, tm_sq = tm_shift(series, squared_row(series), -1, 3)
        upstream = class_mix(jnp.concatenate([series, later], axis=1), table_bwd, selector)
        outgoing = jnp.dot(routing["gather"].T, upstream, precision=lax.Precision.HIGH)
        incoming, total_sq = basin_exchange(outgoing, tm_sq)
        rows = jnp.dot(place.T, incoming, precision=lax.Precision.HIGH)
        spread = jnp.einsum(
            "bjr,bjt->brt", weights, rows.reshape(blocks, slots, hours), precision=lax.Precision.HIGH
        )
        return spread.reshape(blocks * width, hours), jnp.sum(total_sq)

    start = observed - forward(first_guess, jnp.zeros((1, LANES), jnp.float32))[0]
    pulled_start, beta_sq = backward(start)
    beta = jnp.sqrt(beta_sq)
    u = start / beta
    pulled = pulled_start / beta
    forward_pulled, alpha_sq = forward(pulled)
    alpha = jnp.sqrt(alpha_sq)
    v = pulled / alpha
    w = v
    estimate = first_guess
    phibar = beta
    rhobar = alpha
    for step in range(ITERS):
        final = step == ITERS - 1
        p = forward_pulled / alpha - alpha * u
        if final:
            beta = jnp.sqrt(global_total(squared_row(p)))
        else:
            pulled_p, beta_sq = backward(p)
            beta = jnp.sqrt(beta_sq)
            pulled = pulled_p / beta - beta * v
            forward_pulled, alpha_next = forward(pulled)
            alpha_next = jnp.sqrt(alpha_next)
            v_next = pulled / alpha_next
        u = p / beta
        rho = jnp.sqrt(rhobar * rhobar + beta * beta)
        cosine = rhobar / rho
        sine = beta / rho
        phi = cosine * phibar
        phibar = sine * phibar
        estimate = estimate + phi / rho * w
        if not final:
            theta = sine * alpha_next
            rhobar = -cosine * alpha_next
            w = v_next - theta / rho * w
            v = v_next
            alpha = alpha_next
    return estimate


def solution(mesh):
    in_specs = (
        P("basin", None, None),
        P("basin"),
        P("basin"),
        P(),
        P("basin", "tm"),
        P("basin", "tm"),
    )
    out_specs = P("basin", "tm")
    return jax.shard_map(shards, mesh=mesh, in_specs=in_specs, out_specs=out_specs, check_vma=False)
```

```python
import functools

import jax
import jax.numpy as jnp
from jax import lax
from jax.experimental import pallas as pl
from jax.experimental.pallas import tpu as pltpu
from jax.sharding import PartitionSpec as P

ITERS = 3
CAP = 32
LANES = 128

HIGH = lax.Precision.HIGH
MESH = pl.DeviceIdType.MESH


def from_behind(x, axis, by):
    devices = lax.axis_size(axis)
    pairs = [(i, i + by) for i in range(devices) if 0 <= i + by < devices]
    return lax.ppermute(x, axis, pairs)


def lag_table(kernels, lag):
    classes, taps = kernels.shape
    rows, hours = lag.shape
    onehot = (lag.T[None, :, :] == jnp.arange(taps)[:, None, None]).astype(jnp.float32)
    picked = jnp.dot(kernels, onehot.reshape(taps, hours * rows), precision=HIGH)
    return picked.reshape(classes, hours, rows)


def class_mix(extended, table, selector):
    spread = lax.dot_general(extended, table, (((1,), (2,)), ((), ())), precision=lax.Precision.HIGH)
    return jnp.sum(spread * selector[:, :, None], axis=1)


def squared(values):
    return jnp.sum(values * values)


def squared_row(values):
    if values.shape[-1] == LANES:
        return jnp.sum(values * values, axis=0, keepdims=True)
    return as_row(squared(values))


def _total_body(x_ref, o_ref, tm_rows, all_rows, own_sem, tsend, trecv, bsend, brecv, *, nb, nt):
    me = lax.axis_index("basin")
    hb = lax.axis_index("tm")
    barrier = pltpu.get_barrier_semaphore()
    for j in range(1, nt):
        pl.semaphore_signal(barrier, inc=1, device_id=(me, lax.rem(hb + j, nt)), device_id_type=MESH)
    for k in range(1, nb):
        pl.semaphore_signal(barrier, inc=1, device_id=(lax.rem(me + k, nb), hb), device_id_type=MESH)
    pl.semaphore_wait(barrier, nt - 1 + nb - 1)

    own = pltpu.make_async_copy(x_ref, tm_rows.at[pl.ds(hb, 1)], own_sem.at[0])
    own.start()
    sends = []
    for j in range(1, nt):
        copy = pltpu.make_async_remote_copy(
            src_ref=x_ref, dst_ref=tm_rows.at[pl.ds(hb, 1)], send_sem=tsend.at[j], recv_sem=trecv.at[j],
            device_id=(me, lax.rem(hb + j, nt)), device_id_type=MESH,
        )
        copy.start()
        sends.append(copy)
    own.wait()
    for j in range(1, nt):
        sends[j - 1].wait_send()
        origin = lax.rem(hb + nt - j, nt)
        pltpu.make_async_remote_copy(
            src_ref=x_ref, dst_ref=tm_rows.at[pl.ds(origin, 1)], send_sem=tsend.at[j], recv_sem=trecv.at[j],
            device_id=(me, origin), device_id_type=MESH,
        ).wait_recv()

    own_block = pltpu.make_async_copy(tm_rows, all_rows.at[me], own_sem.at[1])
    own_block.start()
    blocks = []
    for k in range(1, nb):
        copy = pltpu.make_async_remote_copy(
            src_ref=tm_rows, dst_ref=all_rows.at[me], send_sem=bsend.at[k], recv_sem=brecv.at[k],
            device_id=(lax.rem(me + k, nb), hb), device_id_type=MESH,
        )
        copy.start()
        blocks.append(copy)
    own_block.wait()
    for k in range(1, nb):
        blocks[k - 1].wait_send()
        source = lax.rem(me + nb - k, nb)
        pltpu.make_async_remote_copy(
            src_ref=tm_rows, dst_ref=all_rows.at[source], send_sem=bsend.at[k], recv_sem=brecv.at[k],
            device_id=(source, hb), device_id_type=MESH,
        ).wait_recv()
    o_ref[...] = jnp.sum(all_rows[...].reshape(nb * nt, LANES), axis=0, keepdims=True)


def global_total(value):
    nb = lax.axis_size("basin")
    nt = lax.axis_size("tm")
    out = pl.pallas_call(
        functools.partial(_total_body, nb=nb, nt=nt),
        out_shape=jax.ShapeDtypeStruct((1, LANES), jnp.float32),
        in_specs=[pl.BlockSpec(memory_space=pltpu.VMEM)],
        out_specs=pl.BlockSpec(memory_space=pltpu.VMEM),
        scratch_shapes=[
            pltpu.VMEM((nt, LANES), jnp.float32),
            pltpu.VMEM((nb, nt, LANES), jnp.float32),
            pltpu.SemaphoreType.DMA((2,)),
            pltpu.SemaphoreType.DMA((nt,)),
            pltpu.SemaphoreType.DMA((nt,)),
            pltpu.SemaphoreType.DMA((nb,)),
            pltpu.SemaphoreType.DMA((nb,)),
        ],
        compiler_params=pltpu.CompilerParams(collective_id=0, has_side_effects=True),
    )(as_row(value))
    return jnp.sum(out)


def _exchange_body(x_ref, c_ref, *rest, nb, mixed):
    if mixed:
        m_ref, o_ref, t_ref, landed, carried, own_sem, send_sem, recv_sem, csend, crecv = rest
    else:
        o_ref, t_ref, landed, carried, own_sem, send_sem, recv_sem, csend, crecv = rest
    me = lax.axis_index("basin")
    hour_block = lax.axis_index("tm")
    barrier = pltpu.get_barrier_semaphore()
    for k in range(1, nb):
        pl.semaphore_signal(
            barrier, inc=1, device_id=(lax.rem(me + k, nb), hour_block), device_id_type=MESH
        )
    pl.semaphore_wait(barrier, nb - 1)
    own = pltpu.make_async_copy(x_ref.at[me], landed.at[me], own_sem.at[0])
    own.start()
    own_carry = pltpu.make_async_copy(c_ref, carried.at[pl.ds(me, 1)], own_sem.at[1])
    own_carry.start()
    copies = []
    for k in range(1, nb):
        peer = lax.rem(me + k, nb)
        copy = pltpu.make_async_remote_copy(
            src_ref=x_ref.at[peer],
            dst_ref=landed.at[me],
            send_sem=send_sem.at[k],
            recv_sem=recv_sem.at[k],
            device_id=(peer, hour_block),
            device_id_type=MESH,
        )
        copy.start()
        carry = pltpu.make_async_remote_copy(
            src_ref=c_ref,
            dst_ref=carried.at[pl.ds(me, 1)],
            send_sem=csend.at[k],
            recv_sem=crecv.at[k],
            device_id=(peer, hour_block),
            device_id_type=MESH,
        )
        carry.start()
        copies.append((copy, carry))
    own.wait()
    own_carry.wait()
    for k in range(1, nb):
        copies[k - 1][0].wait_send()
        copies[k - 1][1].wait_send()
        source = lax.rem(me + nb - k, nb)
        pltpu.make_async_remote_copy(
            src_ref=x_ref.at[source],
            dst_ref=landed.at[source],
            send_sem=send_sem.at[k],
            recv_sem=recv_sem.at[k],
            device_id=(source, hour_block),
            device_id_type=MESH,
        ).wait_recv()
        pltpu.make_async_remote_copy(
            src_ref=c_ref,
            dst_ref=carried.at[pl.ds(source, 1)],
            send_sem=csend.at[k],
            recv_sem=crecv.at[k],
            device_id=(source, hour_block),
            device_id_type=MESH,
        ).wait_recv()
    if mixed:
        o_ref[...] = jnp.dot(
            m_ref[...],
            landed[...].reshape(landed.shape[0] * landed.shape[1], landed.shape[2]),
            precision=lax.Precision.HIGHEST,
            preferred_element_type=jnp.float32,
        )
    else:
        o_ref[...] = landed[...]
    t_ref[...] = jnp.sum(carried[...], axis=0, keepdims=True)


def as_row(value):
    if value.ndim == 2:
        return value
    return jnp.broadcast_to(value.astype(jnp.float32), (1, LANES))


def basin_exchange(x, carry, ident=1, mix=None):
    nb = lax.axis_size("basin")
    total, hours = x.shape
    shaped = x.reshape(nb, total // nb, hours)
    operands = [shaped, as_row(carry)]
    result = shaped.shape
    if mix is not None:
        operands.append(mix)
        result = (mix.shape[0], hours)
    out, summed = pl.pallas_call(
        functools.partial(_exchange_body, nb=nb, mixed=mix is not None),
        out_shape=(
            jax.ShapeDtypeStruct(result, jnp.float32),
            jax.ShapeDtypeStruct((1, LANES), jnp.float32),
        ),
        in_specs=[pl.BlockSpec(memory_space=pltpu.VMEM)] * len(operands),
        out_specs=(pl.BlockSpec(memory_space=pltpu.VMEM),) * 2,
        scratch_shapes=[
            pltpu.VMEM(shaped.shape, jnp.float32),
            pltpu.VMEM((nb, LANES), jnp.float32),
            pltpu.SemaphoreType.DMA((2,)),
            pltpu.SemaphoreType.DMA((nb,)),
            pltpu.SemaphoreType.DMA((nb,)),
            pltpu.SemaphoreType.DMA((nb,)),
            pltpu.SemaphoreType.DMA((nb,)),
        ],
        compiler_params=pltpu.CompilerParams(collective_id=ident, has_side_effects=True),
    )(*operands)
    if mix is not None:
        return out, summed
    return out.reshape(total, hours), summed


def _shift_body(x_ref, c_ref, o_ref, t_ref, held, carried, own_sem, dsend, drecv, csend, crecv, *, nt, by):
    basin = lax.axis_index("basin")
    me = lax.axis_index("tm")
    barrier = pltpu.get_barrier_semaphore()
    for k in range(1, nt):
        pl.semaphore_signal(
            barrier, inc=1, device_id=(basin, lax.rem(me + k, nt)), device_id_type=MESH
        )
    pl.semaphore_wait(barrier, nt - 1)

    target = me + by
    source = me - by
    has_target = jnp.logical_and(target >= 0, target < nt)
    has_source = jnp.logical_and(source >= 0, source < nt)
    data = pltpu.make_async_remote_copy(
        src_ref=x_ref,
        dst_ref=held,
        send_sem=dsend,
        recv_sem=drecv,
        device_id=(basin, lax.rem(target + nt, nt)),
        device_id_type=MESH,
    )

    @pl.when(has_target)
    def _():
        data.start()

    own = pltpu.make_async_copy(c_ref, carried.at[pl.ds(me, 1)], own_sem)
    own.start()
    copies = []
    for k in range(1, nt):
        copy = pltpu.make_async_remote_copy(
            src_ref=c_ref,
            dst_ref=carried.at[pl.ds(me, 1)],
            send_sem=csend.at[k],
            recv_sem=crecv.at[k],
            device_id=(basin, lax.rem(me + k, nt)),
            device_id_type=MESH,
        )
        copy.start()
        copies.append(copy)
    own.wait()
    for k in range(1, nt):
        copies[k - 1].wait_send()
        origin = lax.rem(me + nt - k, nt)
        pltpu.make_async_remote_copy(
            src_ref=c_ref,
            dst_ref=carried.at[pl.ds(origin, 1)],
            send_sem=csend.at[k],
            recv_sem=crecv.at[k],
            device_id=(basin, origin),
            device_id_type=MESH,
        ).wait_recv()
    t_ref[...] = jnp.sum(carried[...], axis=0, keepdims=True)

    @pl.when(has_target)
    def _():
        data.wait_send()

    @pl.when(has_source)
    def _():
        data.wait_recv()
        o_ref[...] = held[...]

    @pl.when(jnp.logical_not(has_source))
    def _():
        o_ref[...] = jnp.zeros(o_ref.shape, o_ref.dtype)


def tm_shift(x, carry, by, ident):
    nt = lax.axis_size("tm")
    c = as_row(carry)
    out, summed = pl.pallas_call(
        functools.partial(_shift_body, nt=nt, by=by),
        out_shape=(
            jax.ShapeDtypeStruct(x.shape, jnp.float32),
            jax.ShapeDtypeStruct((1, LANES), jnp.float32),
        ),
        in_specs=[pl.BlockSpec(memory_space=pltpu.VMEM)] * 2,
        out_specs=(pl.BlockSpec(memory_space=pltpu.VMEM),) * 2,
        scratch_shapes=[
            pltpu.VMEM(x.shape, jnp.float32),
            pltpu.VMEM((nt, LANES), jnp.float32),
            pltpu.SemaphoreType.DMA(()),
            pltpu.SemaphoreType.DMA(()),
            pltpu.SemaphoreType.DMA(()),
            pltpu.SemaphoreType.DMA((nt,)),
            pltpu.SemaphoreType.DMA((nt,)),
        ],
        compiler_params=pltpu.CompilerParams(collective_id=ident, has_side_effects=True),
    )(x, c)
    return out, summed


def shards(incidence, row_gauge, gauge_kernel, kernels, observed, first_guess):
    weights = incidence.astype(jnp.float32)
    blocks, slots, width = weights.shape
    gauges_here, hours = observed.shape
    owners = lax.axis_size("basin")
    classes = kernels.shape[0]
    partials = blocks * slots
    outer = jnp.arange(2 * hours)[:, None]
    inner = jnp.arange(hours)[None, :]
    table_fwd = lag_table(kernels, inner + hours - outer)
    table_bwd = lag_table(kernels, outer - inner)
    selector = (gauge_kernel[:, None] == jnp.arange(classes)[None, :]).astype(jnp.float32)

    owner = row_gauge // gauges_here
    local = row_gauge % gauges_here
    hit = owner[:, None] == jnp.arange(owners)[None, :]
    rank = jnp.cumsum(hit.astype(jnp.int32), axis=0) - 1
    dest = owner * CAP + jnp.sum(jnp.where(hit, rank, 0), axis=1)
    entries = owners * CAP
    place = (jnp.arange(entries)[:, None] == dest[None, :]).astype(jnp.float32)
    sent_ids = jnp.full((entries,), -1, jnp.int32).at[dest].set(local)
    id_rows = jnp.zeros((owners, 8, hours), jnp.float32)
    id_rows = id_rows.at[:, 0, :CAP].set(sent_ids.reshape(owners, CAP).astype(jnp.float32))
    routing = {}

    def forward(field, carry=None):
        partial_value = jnp.einsum(
            "bjr,brt->bjt", weights, field.reshape(blocks, width, hours), precision=HIGH
        )
        outgoing = jnp.dot(place, partial_value.reshape(partials, hours), precision=HIGH)
        if "gather" not in routing:
            packed = jnp.concatenate([outgoing.reshape(owners, CAP, hours), id_rows], axis=1)
            landed, basin_sq = basin_exchange(packed.reshape(owners * (CAP + 8), hours), carry, 5)
            landed = landed.reshape(owners, CAP + 8, hours)
            got_ids = landed[:, CAP, :CAP].astype(jnp.int32).reshape(entries)
            routing["gather"] = (jnp.arange(gauges_here)[:, None] == got_ids[None, :]).astype(jnp.float32)
            incoming = landed[:, :CAP, :].reshape(entries, hours)
            sums = jnp.dot(routing["gather"], incoming, precision=HIGH)
        else:
            sums, basin_sq = basin_exchange(outgoing, squared_row(field), 1, routing["gather"])
        earlier, total_sq = tm_shift(sums, basin_sq, 1, 2)
        return class_mix(jnp.concatenate([earlier, sums], axis=1), table_fwd, selector), jnp.sum(total_sq)

    def backward(series):
        later, tm_sq = tm_shift(series, squared_row(series), -1, 3)
        upstream = class_mix(jnp.concatenate([series, later], axis=1), table_bwd, selector)
        outgoing = jnp.dot(routing["gather"].T, upstream, precision=lax.Precision.HIGH)
        rows, total_sq = basin_exchange(outgoing, tm_sq, 6, place.T)
        spread = jnp.einsum(
            "bjr,bjt->brt", weights, rows.reshape(blocks, slots, hours), precision=lax.Precision.HIGH
        )
        return spread.reshape(blocks * width, hours), jnp.sum(total_sq)

    start = observed - forward(first_guess, jnp.zeros((1, LANES), jnp.float32))[0]
    pulled_start, beta_sq = backward(start)
    beta = jnp.sqrt(beta_sq)
    u = start / beta
    pulled = pulled_start / beta
    forward_pulled, alpha_sq = forward(pulled)
    alpha = jnp.sqrt(alpha_sq)
    v = pulled / alpha
    w = v
    estimate = first_guess
    phibar = beta
    rhobar = alpha
    for step in range(ITERS):
        final = step == ITERS - 1
        p = forward_pulled / alpha - alpha * u
        if final:
            beta = jnp.sqrt(global_total(squared_row(p)))
        else:
            pulled_p, beta_sq = backward(p)
            beta = jnp.sqrt(beta_sq)
            pulled = pulled_p / beta - beta * v
            forward_pulled, alpha_next = forward(pulled)
            alpha_next = jnp.sqrt(alpha_next)
            v_next = pulled / alpha_next
        u = p / beta
        rho = jnp.sqrt(rhobar * rhobar + beta * beta)
        cosine = rhobar / rho
        sine = beta / rho
        phi = cosine * phibar
        phibar = sine * phibar
        estimate = estimate + phi / rho * w
        if not final:
            theta = sine * alpha_next
            rhobar = -cosine * alpha_next
            w = v_next - theta / rho * w
            v = v_next
            alpha = alpha_next
    return estimate


def solution(mesh):
    in_specs = (
        P("basin", None, None),
        P("basin"),
        P("basin"),
        P(),
        P("basin", "tm"),
        P("basin", "tm"),
    )
    out_specs = P("basin", "tm")
    return jax.shard_map(shards, mesh=mesh, in_specs=in_specs, out_specs=out_specs, check_vma=False)
```

```python
import functools

import jax
import jax.numpy as jnp
from jax import lax
from jax.experimental import pallas as pl
from jax.experimental.pallas import tpu as pltpu
from jax.sharding import PartitionSpec as P

ITERS = 3
CAP = 32
LANES = 128

HIGH = lax.Precision.HIGH
MESH = pl.DeviceIdType.MESH


def from_behind(x, axis, by):
    devices = lax.axis_size(axis)
    pairs = [(i, i + by) for i in range(devices) if 0 <= i + by < devices]
    return lax.ppermute(x, axis, pairs)


def lag_table(kernels, lag):
    classes, taps = kernels.shape
    rows, hours = lag.shape
    onehot = (lag.T[None, :, :] == jnp.arange(taps)[:, None, None]).astype(jnp.float32)
    picked = jnp.dot(kernels, onehot.reshape(taps, hours * rows), precision=HIGH)
    return picked.reshape(classes, hours, rows)


def class_mix(extended, table, selector):
    spread = lax.dot_general(extended, table, (((1,), (2,)), ((), ())), precision=lax.Precision.HIGH)
    return jnp.sum(spread * selector[:, :, None], axis=1)


def squared(values):
    return jnp.sum(values * values)


def squared_row(values):
    if values.shape[-1] == LANES:
        return jnp.sum(values * values, axis=0, keepdims=True)
    return as_row(squared(values))


def _total_body(x_ref, o_ref, tm_rows, all_rows, own_sem, tsend, trecv, bsend, brecv, *, nb, nt):
    me = lax.axis_index("basin")
    hb = lax.axis_index("tm")
    barrier = pltpu.get_barrier_semaphore()
    for j in range(1, nt):
        pl.semaphore_signal(barrier, inc=1, device_id=(me, lax.rem(hb + j, nt)), device_id_type=MESH)
    for k in range(1, nb):
        pl.semaphore_signal(barrier, inc=1, device_id=(lax.rem(me + k, nb), hb), device_id_type=MESH)
    pl.semaphore_wait(barrier, nt - 1 + nb - 1)

    own = pltpu.make_async_copy(x_ref, tm_rows.at[pl.ds(hb, 1)], own_sem.at[0])
    own.start()
    sends = []
    for j in range(1, nt):
        copy = pltpu.make_async_remote_copy(
            src_ref=x_ref, dst_ref=tm_rows.at[pl.ds(hb, 1)], send_sem=tsend.at[j], recv_sem=trecv.at[j],
            device_id=(me, lax.rem(hb + j, nt)), device_id_type=MESH,
        )
        copy.start()
        sends.append(copy)
    own.wait()
    for j in range(1, nt):
        sends[j - 1].wait_send()
        origin = lax.rem(hb + nt - j, nt)
        pltpu.make_async_remote_copy(
            src_ref=x_ref, dst_ref=tm_rows.at[pl.ds(origin, 1)], send_sem=tsend.at[j], recv_sem=trecv.at[j],
            device_id=(me, origin), device_id_type=MESH,
        ).wait_recv()

    own_block = pltpu.make_async_copy(tm_rows, all_rows.at[me], own_sem.at[1])
    own_block.start()
    blocks = []
    for k in range(1, nb):
        copy = pltpu.make_async_remote_copy(
            src_ref=tm_rows, dst_ref=all_rows.at[me], send_sem=bsend.at[k], recv_sem=brecv.at[k],
            device_id=(lax.rem(me + k, nb), hb), device_id_type=MESH,
        )
        copy.start()
        blocks.append(copy)
    own_block.wait()
    for k in range(1, nb):
        blocks[k - 1].wait_send()
        source = lax.rem(me + nb - k, nb)
        pltpu.make_async_remote_copy(
            src_ref=tm_rows, dst_ref=all_rows.at[source], send_sem=bsend.at[k], recv_sem=brecv.at[k],
            device_id=(source, hb), device_id_type=MESH,
        ).wait_recv()
    o_ref[...] = jnp.sum(all_rows[...].reshape(nb * nt, LANES), axis=0, keepdims=True)


def global_total(value):
    nb = lax.axis_size("basin")
    nt = lax.axis_size("tm")
    out = pl.pallas_call(
        functools.partial(_total_body, nb=nb, nt=nt),
        out_shape=jax.ShapeDtypeStruct((1, LANES), jnp.float32),
        in_specs=[pl.BlockSpec(memory_space=pltpu.VMEM)],
        out_specs=pl.BlockSpec(memory_space=pltpu.VMEM),
        scratch_shapes=[
            pltpu.VMEM((nt, LANES), jnp.float32),
            pltpu.VMEM((nb, nt, LANES), jnp.float32),
            pltpu.SemaphoreType.DMA((2,)),
            pltpu.SemaphoreType.DMA((nt,)),
            pltpu.SemaphoreType.DMA((nt,)),
            pltpu.SemaphoreType.DMA((nb,)),
            pltpu.SemaphoreType.DMA((nb,)),
        ],
        compiler_params=pltpu.CompilerParams(collective_id=0, has_side_effects=True),
    )(as_row(value))
    return jnp.sum(out)


def _exchange_body(x_ref, c_ref, landed, t_ref, carried, own_sem, send_sem, recv_sem, csend, crecv, *, nb):
    me = lax.axis_index("basin")
    hour_block = lax.axis_index("tm")
    barrier = pltpu.get_barrier_semaphore()
    for k in range(1, nb):
        pl.semaphore_signal(
            barrier, inc=1, device_id=(lax.rem(me + k, nb), hour_block), device_id_type=MESH
        )
    pl.semaphore_wait(barrier, nb - 1)
    own = pltpu.make_async_copy(x_ref.at[me], landed.at[me], own_sem.at[0])
    own.start()
    own_carry = pltpu.make_async_copy(c_ref, carried.at[pl.ds(me, 1)], own_sem.at[1])
    own_carry.start()
    copies = []
    for k in range(1, nb):
        peer = lax.rem(me + k, nb)
        copy = pltpu.make_async_remote_copy(
            src_ref=x_ref.at[peer],
            dst_ref=landed.at[me],
            send_sem=send_sem.at[k],
            recv_sem=recv_sem.at[k],
            device_id=(peer, hour_block),
            device_id_type=MESH,
        )
        copy.start()
        carry = pltpu.make_async_remote_copy(
            src_ref=c_ref,
            dst_ref=carried.at[pl.ds(me, 1)],
            send_sem=csend.at[k],
            recv_sem=crecv.at[k],
            device_id=(peer, hour_block),
            device_id_type=MESH,
        )
        carry.start()
        copies.append((copy, carry))
    own.wait()
    own_carry.wait()
    for k in range(1, nb):
        copies[k - 1][0].wait_send()
        copies[k - 1][1].wait_send()
        source = lax.rem(me + nb - k, nb)
        pltpu.make_async_remote_copy(
            src_ref=x_ref.at[source],
            dst_ref=landed.at[source],
            send_sem=send_sem.at[k],
            recv_sem=recv_sem.at[k],
            device_id=(source, hour_block),
            device_id_type=MESH,
        ).wait_recv()
        pltpu.make_async_remote_copy(
            src_ref=c_ref,
            dst_ref=carried.at[pl.ds(source, 1)],
            send_sem=csend.at[k],
            recv_sem=crecv.at[k],
            device_id=(source, hour_block),
            device_id_type=MESH,
        ).wait_recv()
    t_ref[...] = jnp.sum(carried[...], axis=0, keepdims=True)


def as_row(value):
    if value.ndim == 2:
        return value
    return jnp.broadcast_to(value.astype(jnp.float32), (1, LANES))


def basin_exchange(x, carry, ident=1):
    nb = lax.axis_size("basin")
    total, hours = x.shape
    shaped = x.reshape(nb, total // nb, hours)
    out, summed = pl.pallas_call(
        functools.partial(_exchange_body, nb=nb),
        out_shape=(
            jax.ShapeDtypeStruct(shaped.shape, jnp.float32),
            jax.ShapeDtypeStruct((1, LANES), jnp.float32),
        ),
        in_specs=[pl.BlockSpec(memory_space=pltpu.VMEM)] * 2,
        out_specs=(pl.BlockSpec(memory_space=pltpu.VMEM),) * 2,
        scratch_shapes=[
            pltpu.VMEM((nb, LANES), jnp.float32),
            pltpu.SemaphoreType.DMA((2,)),
            pltpu.SemaphoreType.DMA((nb,)),
            pltpu.SemaphoreType.DMA((nb,)),
            pltpu.SemaphoreType.DMA((nb,)),
            pltpu.SemaphoreType.DMA((nb,)),
        ],
        compiler_params=pltpu.CompilerParams(collective_id=ident, has_side_effects=True),
    )(shaped, as_row(carry))
    return out.reshape(total, hours), summed


def _shift_body(x_ref, c_ref, o_ref, t_ref, carried, own_sem, dsend, drecv, csend, crecv, *, nt, by):
    basin = lax.axis_index("basin")
    me = lax.axis_index("tm")
    barrier = pltpu.get_barrier_semaphore()
    for k in range(1, nt):
        pl.semaphore_signal(
            barrier, inc=1, device_id=(basin, lax.rem(me + k, nt)), device_id_type=MESH
        )
    pl.semaphore_wait(barrier, nt - 1)

    target = me + by
    source = me - by
    has_target = jnp.logical_and(target >= 0, target < nt)
    has_source = jnp.logical_and(source >= 0, source < nt)
    data = pltpu.make_async_remote_copy(
        src_ref=x_ref,
        dst_ref=o_ref,
        send_sem=dsend,
        recv_sem=drecv,
        device_id=(basin, lax.rem(target + nt, nt)),
        device_id_type=MESH,
    )

    @pl.when(has_target)
    def _():
        data.start()

    own = pltpu.make_async_copy(c_ref, carried.at[pl.ds(me, 1)], own_sem)
    own.start()
    copies = []
    for k in range(1, nt):
        copy = pltpu.make_async_remote_copy(
            src_ref=c_ref,
            dst_ref=carried.at[pl.ds(me, 1)],
            send_sem=csend.at[k],
            recv_sem=crecv.at[k],
            device_id=(basin, lax.rem(me + k, nt)),
            device_id_type=MESH,
        )
        copy.start()
        copies.append(copy)
    own.wait()
    for k in range(1, nt):
        copies[k - 1].wait_send()
        origin = lax.rem(me + nt - k, nt)
        pltpu.make_async_remote_copy(
            src_ref=c_ref,
            dst_ref=carried.at[pl.ds(origin, 1)],
            send_sem=csend.at[k],
            recv_sem=crecv.at[k],
            device_id=(basin, origin),
            device_id_type=MESH,
        ).wait_recv()
    t_ref[...] = jnp.sum(carried[...], axis=0, keepdims=True)

    @pl.when(has_target)
    def _():
        data.wait_send()

    @pl.when(has_source)
    def _():
        data.wait_recv()

    @pl.when(jnp.logical_not(has_source))
    def _():
        o_ref[...] = jnp.zeros(o_ref.shape, o_ref.dtype)


def tm_shift(x, carry, by, ident):
    nt = lax.axis_size("tm")
    c = as_row(carry)
    out, summed = pl.pallas_call(
        functools.partial(_shift_body, nt=nt, by=by),
        out_shape=(
            jax.ShapeDtypeStruct(x.shape, jnp.float32),
            jax.ShapeDtypeStruct((1, LANES), jnp.float32),
        ),
        in_specs=[pl.BlockSpec(memory_space=pltpu.VMEM)] * 2,
        out_specs=(pl.BlockSpec(memory_space=pltpu.VMEM),) * 2,
        scratch_shapes=[
            pltpu.VMEM((nt, LANES), jnp.float32),
            pltpu.SemaphoreType.DMA(()),
            pltpu.SemaphoreType.DMA(()),
            pltpu.SemaphoreType.DMA(()),
            pltpu.SemaphoreType.DMA((nt,)),
            pltpu.SemaphoreType.DMA((nt,)),
        ],
        compiler_params=pltpu.CompilerParams(collective_id=ident, has_side_effects=True),
    )(x, c)
    return out, summed


def shards(incidence, row_gauge, gauge_kernel, kernels, observed, first_guess):
    weights = incidence.astype(jnp.float32)
    blocks, slots, width = weights.shape
    gauges_here, hours = observed.shape
    owners = lax.axis_size("basin")
    classes = kernels.shape[0]
    partials = blocks * slots
    outer = jnp.arange(2 * hours)[:, None]
    inner = jnp.arange(hours)[None, :]
    table_fwd = lag_table(kernels, inner + hours - outer)
    table_bwd = lag_table(kernels, outer - inner)
    selector = (gauge_kernel[:, None] == jnp.arange(classes)[None, :]).astype(jnp.float32)

    owner = row_gauge // gauges_here
    local = row_gauge % gauges_here
    hit = owner[:, None] == jnp.arange(owners)[None, :]
    rank = jnp.cumsum(hit.astype(jnp.int32), axis=0) - 1
    dest = owner * CAP + jnp.sum(jnp.where(hit, rank, 0), axis=1)
    entries = owners * CAP
    place = (jnp.arange(entries)[:, None] == dest[None, :]).astype(jnp.float32)
    sent_ids = jnp.full((entries,), -1, jnp.int32).at[dest].set(local)
    id_rows = jnp.zeros((owners, 8, hours), jnp.float32)
    id_rows = id_rows.at[:, 0, :CAP].set(sent_ids.reshape(owners, CAP).astype(jnp.float32))
    routing = {}

    def forward(field, carry=None):
        partial_value = jnp.einsum(
            "bjr,brt->bjt", weights, field.reshape(blocks, width, hours), precision=HIGH
        )
        outgoing = jnp.dot(place, partial_value.reshape(partials, hours), precision=HIGH)
        if "gather" not in routing:
            packed = jnp.concatenate([outgoing.reshape(owners, CAP, hours), id_rows], axis=1)
            landed, basin_sq = basin_exchange(packed.reshape(owners * (CAP + 8), hours), carry, 5)
            landed = landed.reshape(owners, CAP + 8, hours)
            got_ids = landed[:, CAP, :CAP].astype(jnp.int32).reshape(entries)
            routing["gather"] = (jnp.arange(gauges_here)[:, None] == got_ids[None, :]).astype(jnp.float32)
            incoming = landed[:, :CAP, :].reshape(entries, hours)
        else:
            incoming, basin_sq = basin_exchange(outgoing, squared_row(field))
        gather = routing["gather"]
        sums = jnp.dot(gather, incoming, precision=HIGH)
        earlier, total_sq = tm_shift(sums, basin_sq, 1, 2)
        return class_mix(jnp.concatenate([earlier, sums], axis=1), table_fwd, selector), jnp.sum(total_sq)

    def backward(series):
        later, tm_sq = tm_shift(series, squared_row(series), -1, 3)
        upstream = class_mix(jnp.concatenate([series, later], axis=1), table_bwd, selector)
        outgoing = jnp.dot(routing["gather"].T, upstream, precision=lax.Precision.HIGH)
        incoming, total_sq = basin_exchange(outgoing, tm_sq)
        rows = jnp.dot(place.T, incoming, precision=lax.Precision.HIGH)
        spread = jnp.einsum(
            "bjr,bjt->brt", weights, rows.reshape(blocks, slots, hours), precision=lax.Precision.HIGH
        )
        return spread.reshape(blocks * width, hours), jnp.sum(total_sq)

    start = observed - forward(first_guess, jnp.zeros((1, LANES), jnp.float32))[0]
    pulled_start, beta_sq = backward(start)
    beta = jnp.sqrt(beta_sq)
    u = start / beta
    pulled = pulled_start / beta
    forward_pulled, alpha_sq = forward(pulled)
    alpha = jnp.sqrt(alpha_sq)
    v = pulled / alpha
    w = v
    estimate = first_guess
    phibar = beta
    rhobar = alpha
    for step in range(ITERS):
        final = step == ITERS - 1
        p = forward_pulled / alpha - alpha * u
        if final:
            beta = jnp.sqrt(global_total(squared_row(p)))
        else:
            pulled_p, beta_sq = backward(p)
            beta = jnp.sqrt(beta_sq)
            pulled = pulled_p / beta - beta * v
            forward_pulled, alpha_next = forward(pulled)
            alpha_next = jnp.sqrt(alpha_next)
            v_next = pulled / alpha_next
        u = p / beta
        rho = jnp.sqrt(rhobar * rhobar + beta * beta)
        cosine = rhobar / rho
        sine = beta / rho
        phi = cosine * phibar
        phibar = sine * phibar
        estimate = estimate + phi / rho * w
        if not final:
            theta = sine * alpha_next
            rhobar = -cosine * alpha_next
            w = v_next - theta / rho * w
            v = v_next
            alpha = alpha_next
    return estimate


def solution(mesh):
    in_specs = (
        P("basin", None, None),
        P("basin"),
        P("basin"),
        P(),
        P("basin", "tm"),
        P("basin", "tm"),
    )
    out_specs = P("basin", "tm")
    return jax.shard_map(shards, mesh=mesh, in_specs=in_specs, out_specs=out_specs, check_vma=False)
```

```python
import functools

import jax
import jax.numpy as jnp
from jax import lax
from jax.experimental import pallas as pl
from jax.experimental.pallas import tpu as pltpu
from jax.sharding import PartitionSpec as P

ITERS = 3
CAP = 32
LANES = 128

HIGH = lax.Precision.HIGH
MESH = pl.DeviceIdType.MESH


def from_behind(x, axis, by):
    devices = lax.axis_size(axis)
    pairs = [(i, i + by) for i in range(devices) if 0 <= i + by < devices]
    return lax.ppermute(x, axis, pairs)


def lag_table(kernels, lag):
    classes, taps = kernels.shape
    rows, hours = lag.shape
    onehot = (lag.T[None, :, :] == jnp.arange(taps)[:, None, None]).astype(jnp.float32)
    picked = jnp.dot(kernels, onehot.reshape(taps, hours * rows), precision=HIGH)
    return picked.reshape(classes, hours, rows)


def class_mix(extended, table, selector):
    spread = lax.dot_general(extended, table, (((1,), (2,)), ((), ())), precision=lax.Precision.HIGH)
    return jnp.sum(spread * selector[:, :, None], axis=1)


def squared(values):
    return jnp.sum(values * values)


def squared_row(values):
    if values.shape[-1] == LANES:
        return jnp.sum(values * values, axis=0, keepdims=True)
    return as_row(squared(values))


def _total_body(x_ref, o_ref, tm_rows, all_rows, own_sem, tsend, trecv, bsend, brecv, *, nb, nt):
    me = lax.axis_index("basin")
    hb = lax.axis_index("tm")
    barrier = pltpu.get_barrier_semaphore()
    for j in range(1, nt):
        pl.semaphore_signal(barrier, inc=1, device_id=(me, lax.rem(hb + j, nt)), device_id_type=MESH)

    def greet(k, state):
        pl.semaphore_signal(barrier, inc=1, device_id=(lax.rem(me + k, nb), hb), device_id_type=MESH)
        return state

    lax.fori_loop(1, nb, greet, 0)
    pl.semaphore_wait(barrier, nt - 1 + nb - 1)

    own = pltpu.make_async_copy(x_ref, tm_rows.at[pl.ds(hb, 1)], own_sem.at[0])
    own.start()
    sends = []
    for j in range(1, nt):
        copy = pltpu.make_async_remote_copy(
            src_ref=x_ref, dst_ref=tm_rows.at[pl.ds(hb, 1)], send_sem=tsend.at[j], recv_sem=trecv.at[j],
            device_id=(me, lax.rem(hb + j, nt)), device_id_type=MESH,
        )
        copy.start()
        sends.append(copy)
    own.wait()
    for j in range(1, nt):
        sends[j - 1].wait_send()
        origin = lax.rem(hb + nt - j, nt)
        pltpu.make_async_remote_copy(
            src_ref=x_ref, dst_ref=tm_rows.at[pl.ds(origin, 1)], send_sem=tsend.at[j], recv_sem=trecv.at[j],
            device_id=(me, origin), device_id_type=MESH,
        ).wait_recv()

    def block_copy(k, source, target):
        return pltpu.make_async_remote_copy(
            src_ref=tm_rows, dst_ref=all_rows.at[source], send_sem=bsend.at[k], recv_sem=brecv.at[k],
            device_id=(target, hb), device_id_type=MESH,
        )

    own_block = pltpu.make_async_copy(tm_rows, all_rows.at[me], own_sem.at[1])
    own_block.start()

    def send(k, state):
        block_copy(k, me, lax.rem(me + k, nb)).start()
        return state

    lax.fori_loop(1, nb, send, 0)
    own_block.wait()

    def settle(k, state):
        block_copy(k, me, lax.rem(me + k, nb)).wait_send()
        source = lax.rem(me + nb - k, nb)
        block_copy(k, source, source).wait_recv()
        return state

    lax.fori_loop(1, nb, settle, 0)
    o_ref[...] = jnp.sum(all_rows[...].reshape(nb * nt, LANES), axis=0, keepdims=True)


def global_total(value):
    nb = lax.axis_size("basin")
    nt = lax.axis_size("tm")
    out = pl.pallas_call(
        functools.partial(_total_body, nb=nb, nt=nt),
        out_shape=jax.ShapeDtypeStruct((1, LANES), jnp.float32),
        in_specs=[pl.BlockSpec(memory_space=pltpu.VMEM)],
        out_specs=pl.BlockSpec(memory_space=pltpu.VMEM),
        scratch_shapes=[
            pltpu.VMEM((nt, LANES), jnp.float32),
            pltpu.VMEM((nb, nt, LANES), jnp.float32),
            pltpu.SemaphoreType.DMA((2,)),
            pltpu.SemaphoreType.DMA((nt,)),
            pltpu.SemaphoreType.DMA((nt,)),
            pltpu.SemaphoreType.DMA((nb,)),
            pltpu.SemaphoreType.DMA((nb,)),
        ],
        compiler_params=pltpu.CompilerParams(collective_id=0, has_side_effects=True),
    )(as_row(value))
    return jnp.sum(out)


def _exchange_body(x_ref, c_ref, landed, t_ref, carried, own_sem, send_sem, recv_sem, csend, crecv, *, nb):
    me = lax.axis_index("basin")
    hour_block = lax.axis_index("tm")

    def data_copy(k, source, target):
        return pltpu.make_async_remote_copy(
            src_ref=x_ref.at[target],
            dst_ref=landed.at[source],
            send_sem=send_sem.at[k],
            recv_sem=recv_sem.at[k],
            device_id=(target, hour_block),
            device_id_type=MESH,
        )

    def carry_copy(k, source, target):
        return pltpu.make_async_remote_copy(
            src_ref=c_ref,
            dst_ref=carried.at[pl.ds(source, 1)],
            send_sem=csend.at[k],
            recv_sem=crecv.at[k],
            device_id=(target, hour_block),
            device_id_type=MESH,
        )

    barrier = pltpu.get_barrier_semaphore()

    def greet(k, state):
        pl.semaphore_signal(
            barrier, inc=1, device_id=(lax.rem(me + k, nb), hour_block), device_id_type=MESH
        )
        return state

    lax.fori_loop(1, nb, greet, 0)
    pl.semaphore_wait(barrier, nb - 1)
    own = pltpu.make_async_copy(x_ref.at[me], landed.at[me], own_sem.at[0])
    own.start()
    own_carry = pltpu.make_async_copy(c_ref, carried.at[pl.ds(me, 1)], own_sem.at[1])
    own_carry.start()

    def send(k, state):
        peer = lax.rem(me + k, nb)
        data_copy(k, me, peer).start()
        carry_copy(k, me, peer).start()
        return state

    lax.fori_loop(1, nb, send, 0)
    own.wait()
    own_carry.wait()

    def settle(k, state):
        peer = lax.rem(me + k, nb)
        source = lax.rem(me + nb - k, nb)
        data_copy(k, me, peer).wait_send()
        carry_copy(k, me, peer).wait_send()
        data_copy(k, source, source).wait_recv()
        carry_copy(k, source, source).wait_recv()
        return state

    lax.fori_loop(1, nb, settle, 0)
    t_ref[...] = jnp.sum(carried[...], axis=0, keepdims=True)


def as_row(value):
    if value.ndim == 2:
        return value
    return jnp.broadcast_to(value.astype(jnp.float32), (1, LANES))


def basin_exchange(x, carry, ident=1):
    nb = lax.axis_size("basin")
    total, hours = x.shape
    shaped = x.reshape(nb, total // nb, hours)
    out, summed = pl.pallas_call(
        functools.partial(_exchange_body, nb=nb),
        out_shape=(
            jax.ShapeDtypeStruct(shaped.shape, jnp.float32),
            jax.ShapeDtypeStruct((1, LANES), jnp.float32),
        ),
        in_specs=[pl.BlockSpec(memory_space=pltpu.VMEM)] * 2,
        out_specs=(pl.BlockSpec(memory_space=pltpu.VMEM),) * 2,
        scratch_shapes=[
            pltpu.VMEM((nb, LANES), jnp.float32),
            pltpu.SemaphoreType.DMA((2,)),
            pltpu.SemaphoreType.DMA((nb,)),
            pltpu.SemaphoreType.DMA((nb,)),
            pltpu.SemaphoreType.DMA((nb,)),
            pltpu.SemaphoreType.DMA((nb,)),
        ],
        compiler_params=pltpu.CompilerParams(collective_id=ident, has_side_effects=True),
    )(shaped, as_row(carry))
    return out.reshape(total, hours), summed


def _shift_body(x_ref, c_ref, o_ref, t_ref, carried, own_sem, dsend, drecv, csend, crecv, *, nt, by):
    basin = lax.axis_index("basin")
    me = lax.axis_index("tm")
    barrier = pltpu.get_barrier_semaphore()
    for k in range(1, nt):
        pl.semaphore_signal(
            barrier, inc=1, device_id=(basin, lax.rem(me + k, nt)), device_id_type=MESH
        )
    pl.semaphore_wait(barrier, nt - 1)

    target = me + by
    source = me - by
    has_target = jnp.logical_and(target >= 0, target < nt)
    has_source = jnp.logical_and(source >= 0, source < nt)
    data = pltpu.make_async_remote_copy(
        src_ref=x_ref,
        dst_ref=o_ref,
        send_sem=dsend,
        recv_sem=drecv,
        device_id=(basin, lax.rem(target + nt, nt)),
        device_id_type=MESH,
    )

    @pl.when(has_target)
    def _():
        data.start()

    own = pltpu.make_async_copy(c_ref, carried.at[pl.ds(me, 1)], own_sem)
    own.start()
    copies = []
    for k in range(1, nt):
        copy = pltpu.make_async_remote_copy(
            src_ref=c_ref,
            dst_ref=carried.at[pl.ds(me, 1)],
            send_sem=csend.at[k],
            recv_sem=crecv.at[k],
            device_id=(basin, lax.rem(me + k, nt)),
            device_id_type=MESH,
        )
        copy.start()
        copies.append(copy)
    own.wait()
    for k in range(1, nt):
        copies[k - 1].wait_send()
        origin = lax.rem(me + nt - k, nt)
        pltpu.make_async_remote_copy(
            src_ref=c_ref,
            dst_ref=carried.at[pl.ds(origin, 1)],
            send_sem=csend.at[k],
            recv_sem=crecv.at[k],
            device_id=(basin, origin),
            device_id_type=MESH,
        ).wait_recv()
    t_ref[...] = jnp.sum(carried[...], axis=0, keepdims=True)

    @pl.when(has_target)
    def _():
        data.wait_send()

    @pl.when(has_source)
    def _():
        data.wait_recv()

    @pl.when(jnp.logical_not(has_source))
    def _():
        o_ref[...] = jnp.zeros(o_ref.shape, o_ref.dtype)


def tm_shift(x, carry, by, ident):
    nt = lax.axis_size("tm")
    c = as_row(carry)
    out, summed = pl.pallas_call(
        functools.partial(_shift_body, nt=nt, by=by),
        out_shape=(
            jax.ShapeDtypeStruct(x.shape, jnp.float32),
            jax.ShapeDtypeStruct((1, LANES), jnp.float32),
        ),
        in_specs=[pl.BlockSpec(memory_space=pltpu.VMEM)] * 2,
        out_specs=(pl.BlockSpec(memory_space=pltpu.VMEM),) * 2,
        scratch_shapes=[
            pltpu.VMEM((nt, LANES), jnp.float32),
            pltpu.SemaphoreType.DMA(()),
            pltpu.SemaphoreType.DMA(()),
            pltpu.SemaphoreType.DMA(()),
            pltpu.SemaphoreType.DMA((nt,)),
            pltpu.SemaphoreType.DMA((nt,)),
        ],
        compiler_params=pltpu.CompilerParams(collective_id=ident, has_side_effects=True),
    )(x, c)
    return out, summed


def shards(incidence, row_gauge, gauge_kernel, kernels, observed, first_guess):
    weights = incidence.astype(jnp.float32)
    blocks, slots, width = weights.shape
    gauges_here, hours = observed.shape
    owners = lax.axis_size("basin")
    classes = kernels.shape[0]
    partials = blocks * slots
    outer = jnp.arange(2 * hours)[:, None]
    inner = jnp.arange(hours)[None, :]
    table_fwd = lag_table(kernels, inner + hours - outer)
    table_bwd = lag_table(kernels, outer - inner)
    selector = (gauge_kernel[:, None] == jnp.arange(classes)[None, :]).astype(jnp.float32)

    owner = row_gauge // gauges_here
    local = row_gauge % gauges_here
    hit = owner[:, None] == jnp.arange(owners)[None, :]
    rank = jnp.cumsum(hit.astype(jnp.int32), axis=0) - 1
    dest = owner * CAP + jnp.sum(jnp.where(hit, rank, 0), axis=1)
    entries = owners * CAP
    place = (jnp.arange(entries)[:, None] == dest[None, :]).astype(jnp.float32)
    sent_ids = jnp.full((entries,), -1, jnp.int32).at[dest].set(local)
    id_rows = jnp.zeros((owners, 8, hours), jnp.float32)
    id_rows = id_rows.at[:, 0, :CAP].set(sent_ids.reshape(owners, CAP).astype(jnp.float32))
    routing = {}

    def forward(field, carry=None):
        partial_value = jnp.einsum(
            "bjr,brt->bjt", weights, field.reshape(blocks, width, hours), precision=HIGH
        )
        outgoing = jnp.dot(place, partial_value.reshape(partials, hours), precision=HIGH)
        if "gather" not in routing:
            packed = jnp.concatenate([outgoing.reshape(owners, CAP, hours), id_rows], axis=1)
            landed, basin_sq = basin_exchange(packed.reshape(owners * (CAP + 8), hours), carry, 5)
            landed = landed.reshape(owners, CAP + 8, hours)
            got_ids = landed[:, CAP, :CAP].astype(jnp.int32).reshape(entries)
            routing["gather"] = (jnp.arange(gauges_here)[:, None] == got_ids[None, :]).astype(jnp.float32)
            incoming = landed[:, :CAP, :].reshape(entries, hours)
        else:
            incoming, basin_sq = basin_exchange(outgoing, squared_row(field))
        gather = routing["gather"]
        sums = jnp.dot(gather, incoming, precision=HIGH)
        earlier, total_sq = tm_shift(sums, basin_sq, 1, 2)
        return class_mix(jnp.concatenate([earlier, sums], axis=1), table_fwd, selector), jnp.sum(total_sq)

    def backward(series):
        later, tm_sq = tm_shift(series, squared_row(series), -1, 3)
        upstream = class_mix(jnp.concatenate([series, later], axis=1), table_bwd, selector)
        outgoing = jnp.dot(routing["gather"].T, upstream, precision=lax.Precision.HIGH)
        incoming, total_sq = basin_exchange(outgoing, tm_sq)
        rows = jnp.dot(place.T, incoming, precision=lax.Precision.HIGH)
        spread = jnp.einsum(
            "bjr,bjt->brt", weights, rows.reshape(blocks, slots, hours), precision=lax.Precision.HIGH
        )
        return spread.reshape(blocks * width, hours), jnp.sum(total_sq)

    start = observed - forward(first_guess, jnp.zeros((1, LANES), jnp.float32))[0]
    pulled_start, beta_sq = backward(start)
    beta = jnp.sqrt(beta_sq)
    u = start / beta
    pulled = pulled_start / beta
    forward_pulled, alpha_sq = forward(pulled)
    alpha = jnp.sqrt(alpha_sq)
    v = pulled / alpha
    w = v
    estimate = first_guess
    phibar = beta
    rhobar = alpha
    for step in range(ITERS):
        final = step == ITERS - 1
        p = forward_pulled / alpha - alpha * u
        if final:
            beta = jnp.sqrt(global_total(squared_row(p)))
        else:
            pulled_p, beta_sq = backward(p)
            beta = jnp.sqrt(beta_sq)
            pulled = pulled_p / beta - beta * v
            forward_pulled, alpha_next = forward(pulled)
            alpha_next = jnp.sqrt(alpha_next)
            v_next = pulled / alpha_next
        u = p / beta
        rho = jnp.sqrt(rhobar * rhobar + beta * beta)
        cosine = rhobar / rho
        sine = beta / rho
        phi = cosine * phibar
        phibar = sine * phibar
        estimate = estimate + phi / rho * w
        if not final:
            theta = sine * alpha_next
            rhobar = -cosine * alpha_next
            w = v_next - theta / rho * w
            v = v_next
            alpha = alpha_next
    return estimate


def solution(mesh):
    in_specs = (
        P("basin", None, None),
        P("basin"),
        P("basin"),
        P(),
        P("basin", "tm"),
        P("basin", "tm"),
    )
    out_specs = P("basin", "tm")
    return jax.shard_map(shards, mesh=mesh, in_specs=in_specs, out_specs=out_specs, check_vma=False)
```

```python
import functools

import jax
import jax.numpy as jnp
from jax import lax
from jax.experimental import pallas as pl
from jax.experimental.pallas import tpu as pltpu
from jax.sharding import PartitionSpec as P

ITERS = 3
CAP = 32
LANES = 128

HIGH = lax.Precision.HIGH
MESH = pl.DeviceIdType.MESH


def from_behind(x, axis, by):
    devices = lax.axis_size(axis)
    pairs = [(i, i + by) for i in range(devices) if 0 <= i + by < devices]
    return lax.ppermute(x, axis, pairs)


def lag_table(kernels, lag):
    classes, taps = kernels.shape
    rows, hours = lag.shape
    onehot = (lag.T[None, :, :] == jnp.arange(taps)[:, None, None]).astype(jnp.float32)
    picked = jnp.dot(kernels, onehot.reshape(taps, hours * rows), precision=HIGH)
    return picked.reshape(classes, hours, rows)


def class_mix(extended, table, selector):
    spread = lax.dot_general(extended, table, (((1,), (2,)), ((), ())), precision=lax.Precision.HIGH)
    return jnp.sum(spread * selector[:, :, None], axis=1)


def squared(values):
    return jnp.sum(values * values)


def squared_row(values):
    if values.shape[-1] == LANES:
        return jnp.sum(values * values, axis=0, keepdims=True)
    return as_row(squared(values))


def _total_body(x_ref, o_ref, tm_rows, all_rows, own_sem, tsend, trecv, bsend, brecv, *, nb, nt):
    me = lax.axis_index("basin")
    hb = lax.axis_index("tm")
    barrier = pltpu.get_barrier_semaphore()
    for j in range(1, nt):
        pl.semaphore_signal(barrier, inc=1, device_id=(me, lax.rem(hb + j, nt)), device_id_type=MESH)
    for k in range(1, nb):
        pl.semaphore_signal(barrier, inc=1, device_id=(lax.rem(me + k, nb), hb), device_id_type=MESH)
    pl.semaphore_wait(barrier, nt - 1 + nb - 1)

    own = pltpu.make_async_copy(x_ref, tm_rows.at[pl.ds(hb, 1)], own_sem.at[0])
    own.start()
    sends = []
    for j in range(1, nt):
        copy = pltpu.make_async_remote_copy(
            src_ref=x_ref, dst_ref=tm_rows.at[pl.ds(hb, 1)], send_sem=tsend.at[j], recv_sem=trecv.at[j],
            device_id=(me, lax.rem(hb + j, nt)), device_id_type=MESH,
        )
        copy.start()
        sends.append(copy)
    own.wait()
    for j in range(1, nt):
        sends[j - 1].wait_send()
        origin = lax.rem(hb + nt - j, nt)
        pltpu.make_async_remote_copy(
            src_ref=x_ref, dst_ref=tm_rows.at[pl.ds(origin, 1)], send_sem=tsend.at[j], recv_sem=trecv.at[j],
            device_id=(me, origin), device_id_type=MESH,
        ).wait_recv()

    own_block = pltpu.make_async_copy(tm_rows, all_rows.at[me], own_sem.at[1])
    own_block.start()
    blocks = []
    for k in range(1, nb):
        copy = pltpu.make_async_remote_copy(
            src_ref=tm_rows, dst_ref=all_rows.at[me], send_sem=bsend.at[k], recv_sem=brecv.at[k],
            device_id=(lax.rem(me + k, nb), hb), device_id_type=MESH,
        )
        copy.start()
        blocks.append(copy)
    own_block.wait()
    for k in range(1, nb):
        blocks[k - 1].wait_send()
        source = lax.rem(me + nb - k, nb)
        pltpu.make_async_remote_copy(
            src_ref=tm_rows, dst_ref=all_rows.at[source], send_sem=bsend.at[k], recv_sem=brecv.at[k],
            device_id=(source, hb), device_id_type=MESH,
        ).wait_recv()
    o_ref[...] = jnp.sum(all_rows[...].reshape(nb * nt, LANES), axis=0, keepdims=True)


def global_total(value):
    nb = lax.axis_size("basin")
    nt = lax.axis_size("tm")
    out = pl.pallas_call(
        functools.partial(_total_body, nb=nb, nt=nt),
        out_shape=jax.ShapeDtypeStruct((1, LANES), jnp.float32),
        in_specs=[pl.BlockSpec(memory_space=pltpu.VMEM)],
        out_specs=pl.BlockSpec(memory_space=pltpu.VMEM),
        scratch_shapes=[
            pltpu.VMEM((nt, LANES), jnp.float32),
            pltpu.VMEM((nb, nt, LANES), jnp.float32),
            pltpu.SemaphoreType.DMA((2,)),
            pltpu.SemaphoreType.DMA((nt,)),
            pltpu.SemaphoreType.DMA((nt,)),
            pltpu.SemaphoreType.DMA((nb,)),
            pltpu.SemaphoreType.DMA((nb,)),
        ],
        compiler_params=pltpu.CompilerParams(collective_id=0, has_side_effects=True),
    )(as_row(value))
    return jnp.sum(out)


def _peer_order(nb):
    if nb != 32:
        return None
    offsets = [(dz, dx, dc) for dz in range(4) for dx in range(4) for dc in range(2) if (dz, dx, dc) != (0, 0, 0)]
    return sorted(offsets, key=lambda o: (-(min(o[0], 4 - o[0]) + min(o[1], 4 - o[1])), o))


def _peer(me, offset, sign):
    if len(offset) == 1:
        return lax.rem(me + sign * offset[0] + 32 * 64, 32 * 64) % 32
    dz, dx, dc = offset
    z, x, c = me // 8, (me // 2) % 4, me % 2
    return ((z + sign * dz + 4) % 4) * 8 + ((x + sign * dx + 4) % 4) * 2 + (c + sign * dc + 2) % 2


def _exchange_body(x_ref, c_ref, landed, t_ref, carried, own_sem, send_sem, recv_sem, csend, crecv, *, nb):
    me = lax.axis_index("basin")
    hour_block = lax.axis_index("tm")
    order = _peer_order(nb)
    if order is None:
        order = [(k,) for k in range(1, nb)]
        targets = [lax.rem(me + k, nb) for k in range(1, nb)]
        sources = [lax.rem(me + nb - k, nb) for k in range(1, nb)]
    else:
        targets = [_peer(me, o, 1) for o in order]
        sources = [_peer(me, o, -1) for o in order]
    barrier = pltpu.get_barrier_semaphore()
    for target in targets:
        pl.semaphore_signal(barrier, inc=1, device_id=(target, hour_block), device_id_type=MESH)
    pl.semaphore_wait(barrier, nb - 1)
    own = pltpu.make_async_copy(x_ref.at[me], landed.at[me], own_sem.at[0])
    own.start()
    own_carry = pltpu.make_async_copy(c_ref, carried.at[pl.ds(me, 1)], own_sem.at[1])
    own_carry.start()
    copies = []
    for i, peer in enumerate(targets):
        copy = pltpu.make_async_remote_copy(
            src_ref=x_ref.at[peer],
            dst_ref=landed.at[me],
            send_sem=send_sem.at[i],
            recv_sem=recv_sem.at[i],
            device_id=(peer, hour_block),
            device_id_type=MESH,
        )
        copy.start()
        carry = pltpu.make_async_remote_copy(
            src_ref=c_ref,
            dst_ref=carried.at[pl.ds(me, 1)],
            send_sem=csend.at[i],
            recv_sem=crecv.at[i],
            device_id=(peer, hour_block),
            device_id_type=MESH,
        )
        carry.start()
        copies.append((copy, carry))
    own.wait()
    own_carry.wait()
    for i, source in enumerate(sources):
        copies[i][0].wait_send()
        copies[i][1].wait_send()
        pltpu.make_async_remote_copy(
            src_ref=x_ref.at[source],
            dst_ref=landed.at[source],
            send_sem=send_sem.at[i],
            recv_sem=recv_sem.at[i],
            device_id=(source, hour_block),
            device_id_type=MESH,
        ).wait_recv()
        pltpu.make_async_remote_copy(
            src_ref=c_ref,
            dst_ref=carried.at[pl.ds(source, 1)],
            send_sem=csend.at[i],
            recv_sem=crecv.at[i],
            device_id=(source, hour_block),
            device_id_type=MESH,
        ).wait_recv()
    t_ref[...] = jnp.sum(carried[...], axis=0, keepdims=True)


def as_row(value):
    if value.ndim == 2:
        return value
    return jnp.broadcast_to(value.astype(jnp.float32), (1, LANES))


def basin_exchange(x, carry, ident=1):
    nb = lax.axis_size("basin")
    total, hours = x.shape
    shaped = x.reshape(nb, total // nb, hours)
    out, summed = pl.pallas_call(
        functools.partial(_exchange_body, nb=nb),
        out_shape=(
            jax.ShapeDtypeStruct(shaped.shape, jnp.float32),
            jax.ShapeDtypeStruct((1, LANES), jnp.float32),
        ),
        in_specs=[pl.BlockSpec(memory_space=pltpu.VMEM)] * 2,
        out_specs=(pl.BlockSpec(memory_space=pltpu.VMEM),) * 2,
        scratch_shapes=[
            pltpu.VMEM((nb, LANES), jnp.float32),
            pltpu.SemaphoreType.DMA((2,)),
            pltpu.SemaphoreType.DMA((nb,)),
            pltpu.SemaphoreType.DMA((nb,)),
            pltpu.SemaphoreType.DMA((nb,)),
            pltpu.SemaphoreType.DMA((nb,)),
        ],
        compiler_params=pltpu.CompilerParams(collective_id=ident, has_side_effects=True),
    )(shaped, as_row(carry))
    return out.reshape(total, hours), summed


def _shift_body(x_ref, c_ref, o_ref, t_ref, carried, own_sem, dsend, drecv, csend, crecv, *, nt, by):
    basin = lax.axis_index("basin")
    me = lax.axis_index("tm")
    barrier = pltpu.get_barrier_semaphore()
    for k in range(1, nt):
        pl.semaphore_signal(
            barrier, inc=1, device_id=(basin, lax.rem(me + k, nt)), device_id_type=MESH
        )
    pl.semaphore_wait(barrier, nt - 1)

    target = me + by
    source = me - by
    has_target = jnp.logical_and(target >= 0, target < nt)
    has_source = jnp.logical_and(source >= 0, source < nt)
    data = pltpu.make_async_remote_copy(
        src_ref=x_ref,
        dst_ref=o_ref,
        send_sem=dsend,
        recv_sem=drecv,
        device_id=(basin, lax.rem(target + nt, nt)),
        device_id_type=MESH,
    )

    @pl.when(has_target)
    def _():
        data.start()

    own = pltpu.make_async_copy(c_ref, carried.at[pl.ds(me, 1)], own_sem)
    own.start()
    copies = []
    for k in range(1, nt):
        copy = pltpu.make_async_remote_copy(
            src_ref=c_ref,
            dst_ref=carried.at[pl.ds(me, 1)],
            send_sem=csend.at[k],
            recv_sem=crecv.at[k],
            device_id=(basin, lax.rem(me + k, nt)),
            device_id_type=MESH,
        )
        copy.start()
        copies.append(copy)
    own.wait()
    for k in range(1, nt):
        copies[k - 1].wait_send()
        origin = lax.rem(me + nt - k, nt)
        pltpu.make_async_remote_copy(
            src_ref=c_ref,
            dst_ref=carried.at[pl.ds(origin, 1)],
            send_sem=csend.at[k],
            recv_sem=crecv.at[k],
            device_id=(basin, origin),
            device_id_type=MESH,
        ).wait_recv()
    t_ref[...] = jnp.sum(carried[...], axis=0, keepdims=True)

    @pl.when(has_target)
    def _():
        data.wait_send()

    @pl.when(has_source)
    def _():
        data.wait_recv()

    @pl.when(jnp.logical_not(has_source))
    def _():
        o_ref[...] = jnp.zeros(o_ref.shape, o_ref.dtype)


def tm_shift(x, carry, by, ident):
    nt = lax.axis_size("tm")
    c = as_row(carry)
    out, summed = pl.pallas_call(
        functools.partial(_shift_body, nt=nt, by=by),
        out_shape=(
            jax.ShapeDtypeStruct(x.shape, jnp.float32),
            jax.ShapeDtypeStruct((1, LANES), jnp.float32),
        ),
        in_specs=[pl.BlockSpec(memory_space=pltpu.VMEM)] * 2,
        out_specs=(pl.BlockSpec(memory_space=pltpu.VMEM),) * 2,
        scratch_shapes=[
            pltpu.VMEM((nt, LANES), jnp.float32),
            pltpu.SemaphoreType.DMA(()),
            pltpu.SemaphoreType.DMA(()),
            pltpu.SemaphoreType.DMA(()),
            pltpu.SemaphoreType.DMA((nt,)),
            pltpu.SemaphoreType.DMA((nt,)),
        ],
        compiler_params=pltpu.CompilerParams(collective_id=ident, has_side_effects=True),
    )(x, c)
    return out, summed


def shards(incidence, row_gauge, gauge_kernel, kernels, observed, first_guess):
    weights = incidence.astype(jnp.float32)
    blocks, slots, width = weights.shape
    gauges_here, hours = observed.shape
    owners = lax.axis_size("basin")
    classes = kernels.shape[0]
    partials = blocks * slots
    outer = jnp.arange(2 * hours)[:, None]
    inner = jnp.arange(hours)[None, :]
    table_fwd = lag_table(kernels, inner + hours - outer)
    table_bwd = lag_table(kernels, outer - inner)
    selector = (gauge_kernel[:, None] == jnp.arange(classes)[None, :]).astype(jnp.float32)

    owner = row_gauge // gauges_here
    local = row_gauge % gauges_here
    hit = owner[:, None] == jnp.arange(owners)[None, :]
    rank = jnp.cumsum(hit.astype(jnp.int32), axis=0) - 1
    dest = owner * CAP + jnp.sum(jnp.where(hit, rank, 0), axis=1)
    entries = owners * CAP
    place = (jnp.arange(entries)[:, None] == dest[None, :]).astype(jnp.float32)
    sent_ids = jnp.full((entries,), -1, jnp.int32).at[dest].set(local)
    id_rows = jnp.zeros((owners, 8, hours), jnp.float32)
    id_rows = id_rows.at[:, 0, :CAP].set(sent_ids.reshape(owners, CAP).astype(jnp.float32))
    routing = {}

    def forward(field, carry=None):
        partial_value = jnp.einsum(
            "bjr,brt->bjt", weights, field.reshape(blocks, width, hours), precision=HIGH
        )
        outgoing = jnp.dot(place, partial_value.reshape(partials, hours), precision=HIGH)
        if "gather" not in routing:
            packed = jnp.concatenate([outgoing.reshape(owners, CAP, hours), id_rows], axis=1)
            landed, basin_sq = basin_exchange(packed.reshape(owners * (CAP + 8), hours), carry, 5)
            landed = landed.reshape(owners, CAP + 8, hours)
            got_ids = landed[:, CAP, :CAP].astype(jnp.int32).reshape(entries)
            routing["gather"] = (jnp.arange(gauges_here)[:, None] == got_ids[None, :]).astype(jnp.float32)
            incoming = landed[:, :CAP, :].reshape(entries, hours)
        else:
            incoming, basin_sq = basin_exchange(outgoing, squared_row(field))
        gather = routing["gather"]
        sums = jnp.dot(gather, incoming, precision=HIGH)
        earlier, total_sq = tm_shift(sums, basin_sq, 1, 2)
        return class_mix(jnp.concatenate([earlier, sums], axis=1), table_fwd, selector), jnp.sum(total_sq)

    def backward(series):
        later, tm_sq = tm_shift(series, squared_row(series), -1, 3)
        upstream = class_mix(jnp.concatenate([series, later], axis=1), table_bwd, selector)
        outgoing = jnp.dot(routing["gather"].T, upstream, precision=lax.Precision.HIGH)
        incoming, total_sq = basin_exchange(outgoing, tm_sq)
        rows = jnp.dot(place.T, incoming, precision=lax.Precision.HIGH)
        spread = jnp.einsum(
            "bjr,bjt->brt", weights, rows.reshape(blocks, slots, hours), precision=lax.Precision.HIGH
        )
        return spread.reshape(blocks * width, hours), jnp.sum(total_sq)

    start = observed - forward(first_guess, jnp.zeros((1, LANES), jnp.float32))[0]
    pulled_start, beta_sq = backward(start)
    beta = jnp.sqrt(beta_sq)
    u = start / beta
    pulled = pulled_start / beta
    forward_pulled, alpha_sq = forward(pulled)
    alpha = jnp.sqrt(alpha_sq)
    v = pulled / alpha
    w = v
    estimate = first_guess
    phibar = beta
    rhobar = alpha
    for step in range(ITERS):
        final = step == ITERS - 1
        p = forward_pulled / alpha - alpha * u
        if final:
            beta = jnp.sqrt(global_total(squared_row(p)))
        else:
            pulled_p, beta_sq = backward(p)
            beta = jnp.sqrt(beta_sq)
            pulled = pulled_p / beta - beta * v
            forward_pulled, alpha_next = forward(pulled)
            alpha_next = jnp.sqrt(alpha_next)
            v_next = pulled / alpha_next
        u = p / beta
        rho = jnp.sqrt(rhobar * rhobar + beta * beta)
        cosine = rhobar / rho
        sine = beta / rho
        phi = cosine * phibar
        phibar = sine * phibar
        estimate = estimate + phi / rho * w
        if not final:
            theta = sine * alpha_next
            rhobar = -cosine * alpha_next
            w = v_next - theta / rho * w
            v = v_next
            alpha = alpha_next
    return estimate


def solution(mesh):
    in_specs = (
        P("basin", None, None),
        P("basin"),
        P("basin"),
        P(),
        P("basin", "tm"),
        P("basin", "tm"),
    )
    out_specs = P("basin", "tm")
    return jax.shard_map(shards, mesh=mesh, in_specs=in_specs, out_specs=out_specs, check_vma=False)
```

```python
import functools

import jax
import jax.numpy as jnp
from jax import lax
from jax.experimental import pallas as pl
from jax.experimental.pallas import tpu as pltpu
from jax.sharding import PartitionSpec as P

ITERS = 3
CAP = 32
LANES = 128

HIGH = lax.Precision.HIGH
MESH = pl.DeviceIdType.MESH


def from_behind(x, axis, by):
    devices = lax.axis_size(axis)
    pairs = [(i, i + by) for i in range(devices) if 0 <= i + by < devices]
    return lax.ppermute(x, axis, pairs)


def lag_table(kernels, lag):
    classes, taps = kernels.shape
    rows, hours = lag.shape
    onehot = (lag.T[None, :, :] == jnp.arange(taps)[:, None, None]).astype(jnp.float32)
    picked = jnp.dot(kernels, onehot.reshape(taps, hours * rows), precision=HIGH)
    return picked.reshape(classes, hours, rows)


def class_mix(extended, table, selector):
    spread = lax.dot_general(extended, table, (((1,), (2,)), ((), ())), precision=lax.Precision.HIGH)
    return jnp.sum(spread * selector[:, :, None], axis=1)


def squared(values):
    return jnp.sum(values * values)


def squared_row(values):
    if values.shape[-1] == LANES:
        return jnp.sum(values * values, axis=0, keepdims=True)
    return as_row(squared(values))


def _total_body(x_ref, o_ref, tm_rows, all_rows, own_sem, tsend, trecv, bsend, brecv, *, nb, nt):
    me = lax.axis_index("basin")
    hb = lax.axis_index("tm")
    barrier = pltpu.get_barrier_semaphore()
    for j in range(1, nt):
        pl.semaphore_signal(barrier, inc=1, device_id=(me, lax.rem(hb + j, nt)), device_id_type=MESH)
    order = _peer_order(nb)
    if order is None:
        targets = [lax.rem(me + k, nb) for k in range(1, nb)]
        sources = [lax.rem(me + nb - k, nb) for k in range(1, nb)]
    else:
        targets = [_peer(me, o, 1) for o in order]
        sources = [_peer(me, o, -1) for o in order]
    for target in targets:
        pl.semaphore_signal(barrier, inc=1, device_id=(target, hb), device_id_type=MESH)
    pl.semaphore_wait(barrier, nt - 1 + nb - 1)

    own = pltpu.make_async_copy(x_ref, tm_rows.at[pl.ds(hb, 1)], own_sem.at[0])
    own.start()
    sends = []
    for j in range(1, nt):
        copy = pltpu.make_async_remote_copy(
            src_ref=x_ref, dst_ref=tm_rows.at[pl.ds(hb, 1)], send_sem=tsend.at[j], recv_sem=trecv.at[j],
            device_id=(me, lax.rem(hb + j, nt)), device_id_type=MESH,
        )
        copy.start()
        sends.append(copy)
    own.wait()
    for j in range(1, nt):
        sends[j - 1].wait_send()
        origin = lax.rem(hb + nt - j, nt)
        pltpu.make_async_remote_copy(
            src_ref=x_ref, dst_ref=tm_rows.at[pl.ds(origin, 1)], send_sem=tsend.at[j], recv_sem=trecv.at[j],
            device_id=(me, origin), device_id_type=MESH,
        ).wait_recv()

    own_block = pltpu.make_async_copy(tm_rows, all_rows.at[me], own_sem.at[1])
    own_block.start()
    blocks = []
    for i, target in enumerate(targets):
        copy = pltpu.make_async_remote_copy(
            src_ref=tm_rows, dst_ref=all_rows.at[me], send_sem=bsend.at[i], recv_sem=brecv.at[i],
            device_id=(target, hb), device_id_type=MESH,
        )
        copy.start()
        blocks.append(copy)
    own_block.wait()
    for i, source in enumerate(sources):
        blocks[i].wait_send()
        pltpu.make_async_remote_copy(
            src_ref=tm_rows, dst_ref=all_rows.at[source], send_sem=bsend.at[i], recv_sem=brecv.at[i],
            device_id=(source, hb), device_id_type=MESH,
        ).wait_recv()
    o_ref[...] = jnp.sum(all_rows[...].reshape(nb * nt, LANES), axis=0, keepdims=True)


def global_total(value):
    nb = lax.axis_size("basin")
    nt = lax.axis_size("tm")
    out = pl.pallas_call(
        functools.partial(_total_body, nb=nb, nt=nt),
        out_shape=jax.ShapeDtypeStruct((1, LANES), jnp.float32),
        in_specs=[pl.BlockSpec(memory_space=pltpu.VMEM)],
        out_specs=pl.BlockSpec(memory_space=pltpu.VMEM),
        scratch_shapes=[
            pltpu.VMEM((nt, LANES), jnp.float32),
            pltpu.VMEM((nb, nt, LANES), jnp.float32),
            pltpu.SemaphoreType.DMA((2,)),
            pltpu.SemaphoreType.DMA((nt,)),
            pltpu.SemaphoreType.DMA((nt,)),
            pltpu.SemaphoreType.DMA((nb,)),
            pltpu.SemaphoreType.DMA((nb,)),
        ],
        compiler_params=pltpu.CompilerParams(collective_id=0, has_side_effects=True),
    )(as_row(value))
    return jnp.sum(out)


def _peer_order(nb):
    if nb != 32:
        return None
    offsets = [(dz, dx, dc) for dz in range(4) for dx in range(4) for dc in range(2) if (dz, dx, dc) != (0, 0, 0)]
    return sorted(offsets, key=lambda o: (-(min(o[0], 4 - o[0]) + min(o[1], 4 - o[1])), o))


def _peer(me, offset, sign):
    if len(offset) == 1:
        return lax.rem(me + sign * offset[0] + 32 * 64, 32 * 64) % 32
    dz, dx, dc = offset
    z, x, c = me // 8, (me // 2) % 4, me % 2
    return ((z + sign * dz + 4) % 4) * 8 + ((x + sign * dx + 4) % 4) * 2 + (c + sign * dc + 2) % 2


def _exchange_body(x_ref, c_ref, landed, t_ref, carried, own_sem, send_sem, recv_sem, csend, crecv, *, nb):
    me = lax.axis_index("basin")
    hour_block = lax.axis_index("tm")
    order = _peer_order(nb)
    if order is None:
        order = [(k,) for k in range(1, nb)]
        targets = [lax.rem(me + k, nb) for k in range(1, nb)]
        sources = [lax.rem(me + nb - k, nb) for k in range(1, nb)]
    else:
        targets = [_peer(me, o, 1) for o in order]
        sources = [_peer(me, o, -1) for o in order]
    barrier = pltpu.get_barrier_semaphore()
    for target in targets:
        pl.semaphore_signal(barrier, inc=1, device_id=(target, hour_block), device_id_type=MESH)
    pl.semaphore_wait(barrier, nb - 1)
    own = pltpu.make_async_copy(x_ref.at[me], landed.at[me], own_sem.at[0])
    own.start()
    own_carry = pltpu.make_async_copy(c_ref, carried.at[pl.ds(me, 1)], own_sem.at[1])
    own_carry.start()
    copies = []
    for i, peer in enumerate(targets):
        copy = pltpu.make_async_remote_copy(
            src_ref=x_ref.at[peer],
            dst_ref=landed.at[me],
            send_sem=send_sem.at[i],
            recv_sem=recv_sem.at[i],
            device_id=(peer, hour_block),
            device_id_type=MESH,
        )
        copy.start()
        carry = pltpu.make_async_remote_copy(
            src_ref=c_ref,
            dst_ref=carried.at[pl.ds(me, 1)],
            send_sem=csend.at[i],
            recv_sem=crecv.at[i],
            device_id=(peer, hour_block),
            device_id_type=MESH,
        )
        carry.start()
        copies.append((copy, carry))
    own.wait()
    own_carry.wait()
    for i, source in enumerate(sources):
        copies[i][0].wait_send()
        copies[i][1].wait_send()
        pltpu.make_async_remote_copy(
            src_ref=x_ref.at[source],
            dst_ref=landed.at[source],
            send_sem=send_sem.at[i],
            recv_sem=recv_sem.at[i],
            device_id=(source, hour_block),
            device_id_type=MESH,
        ).wait_recv()
        pltpu.make_async_remote_copy(
            src_ref=c_ref,
            dst_ref=carried.at[pl.ds(source, 1)],
            send_sem=csend.at[i],
            recv_sem=crecv.at[i],
            device_id=(source, hour_block),
            device_id_type=MESH,
        ).wait_recv()
    t_ref[...] = jnp.sum(carried[...], axis=0, keepdims=True)


def as_row(value):
    if value.ndim == 2:
        return value
    return jnp.broadcast_to(value.astype(jnp.float32), (1, LANES))


def basin_exchange(x, carry, ident=1):
    nb = lax.axis_size("basin")
    total, hours = x.shape
    shaped = x.reshape(nb, total // nb, hours)
    out, summed = pl.pallas_call(
        functools.partial(_exchange_body, nb=nb),
        out_shape=(
            jax.ShapeDtypeStruct(shaped.shape, jnp.float32),
            jax.ShapeDtypeStruct((1, LANES), jnp.float32),
        ),
        in_specs=[pl.BlockSpec(memory_space=pltpu.VMEM)] * 2,
        out_specs=(pl.BlockSpec(memory_space=pltpu.VMEM),) * 2,
        scratch_shapes=[
            pltpu.VMEM((nb, LANES), jnp.float32),
            pltpu.SemaphoreType.DMA((2,)),
            pltpu.SemaphoreType.DMA((nb,)),
            pltpu.SemaphoreType.DMA((nb,)),
            pltpu.SemaphoreType.DMA((nb,)),
            pltpu.SemaphoreType.DMA((nb,)),
        ],
        compiler_params=pltpu.CompilerParams(collective_id=ident, has_side_effects=True),
    )(shaped, as_row(carry))
    return out.reshape(total, hours), summed


def _shift_body(x_ref, c_ref, o_ref, t_ref, carried, own_sem, dsend, drecv, csend, crecv, *, nt, by):
    basin = lax.axis_index("basin")
    me = lax.axis_index("tm")
    barrier = pltpu.get_barrier_semaphore()
    for k in range(1, nt):
        pl.semaphore_signal(
            barrier, inc=1, device_id=(basin, lax.rem(me + k, nt)), device_id_type=MESH
        )
    pl.semaphore_wait(barrier, nt - 1)

    target = me + by
    source = me - by
    has_target = jnp.logical_and(target >= 0, target < nt)
    has_source = jnp.logical_and(source >= 0, source < nt)
    data = pltpu.make_async_remote_copy(
        src_ref=x_ref,
        dst_ref=o_ref,
        send_sem=dsend,
        recv_sem=drecv,
        device_id=(basin, lax.rem(target + nt, nt)),
        device_id_type=MESH,
    )

    @pl.when(has_target)
    def _():
        data.start()

    own = pltpu.make_async_copy(c_ref, carried.at[pl.ds(me, 1)], own_sem)
    own.start()
    copies = []
    for k in range(1, nt):
        copy = pltpu.make_async_remote_copy(
            src_ref=c_ref,
            dst_ref=carried.at[pl.ds(me, 1)],
            send_sem=csend.at[k],
            recv_sem=crecv.at[k],
            device_id=(basin, lax.rem(me + k, nt)),
            device_id_type=MESH,
        )
        copy.start()
        copies.append(copy)
    own.wait()
    for k in range(1, nt):
        copies[k - 1].wait_send()
        origin = lax.rem(me + nt - k, nt)
        pltpu.make_async_remote_copy(
            src_ref=c_ref,
            dst_ref=carried.at[pl.ds(origin, 1)],
            send_sem=csend.at[k],
            recv_sem=crecv.at[k],
            device_id=(basin, origin),
            device_id_type=MESH,
        ).wait_recv()
    t_ref[...] = jnp.sum(carried[...], axis=0, keepdims=True)

    @pl.when(has_target)
    def _():
        data.wait_send()

    @pl.when(has_source)
    def _():
        data.wait_recv()

    @pl.when(jnp.logical_not(has_source))
    def _():
        o_ref[...] = jnp.zeros(o_ref.shape, o_ref.dtype)


def tm_shift(x, carry, by, ident):
    nt = lax.axis_size("tm")
    c = as_row(carry)
    out, summed = pl.pallas_call(
        functools.partial(_shift_body, nt=nt, by=by),
        out_shape=(
            jax.ShapeDtypeStruct(x.shape, jnp.float32),
            jax.ShapeDtypeStruct((1, LANES), jnp.float32),
        ),
        in_specs=[pl.BlockSpec(memory_space=pltpu.VMEM)] * 2,
        out_specs=(pl.BlockSpec(memory_space=pltpu.VMEM),) * 2,
        scratch_shapes=[
            pltpu.VMEM((nt, LANES), jnp.float32),
            pltpu.SemaphoreType.DMA(()),
            pltpu.SemaphoreType.DMA(()),
            pltpu.SemaphoreType.DMA(()),
            pltpu.SemaphoreType.DMA((nt,)),
            pltpu.SemaphoreType.DMA((nt,)),
        ],
        compiler_params=pltpu.CompilerParams(collective_id=ident, has_side_effects=True),
    )(x, c)
    return out, summed


def shards(incidence, row_gauge, gauge_kernel, kernels, observed, first_guess):
    weights = incidence.astype(jnp.float32)
    blocks, slots, width = weights.shape
    gauges_here, hours = observed.shape
    owners = lax.axis_size("basin")
    classes = kernels.shape[0]
    partials = blocks * slots
    outer = jnp.arange(2 * hours)[:, None]
    inner = jnp.arange(hours)[None, :]
    table_fwd = lag_table(kernels, inner + hours - outer)
    table_bwd = lag_table(kernels, outer - inner)
    selector = (gauge_kernel[:, None] == jnp.arange(classes)[None, :]).astype(jnp.float32)

    owner = row_gauge // gauges_here
    local = row_gauge % gauges_here
    hit = owner[:, None] == jnp.arange(owners)[None, :]
    rank = jnp.cumsum(hit.astype(jnp.int32), axis=0) - 1
    dest = owner * CAP + jnp.sum(jnp.where(hit, rank, 0), axis=1)
    entries = owners * CAP
    place = (jnp.arange(entries)[:, None] == dest[None, :]).astype(jnp.float32)
    sent_ids = jnp.full((entries,), -1, jnp.int32).at[dest].set(local)
    id_rows = jnp.zeros((owners, 8, hours), jnp.float32)
    id_rows = id_rows.at[:, 0, :CAP].set(sent_ids.reshape(owners, CAP).astype(jnp.float32))
    routing = {}

    def forward(field, carry=None):
        partial_value = jnp.einsum(
            "bjr,brt->bjt", weights, field.reshape(blocks, width, hours), precision=HIGH
        )
        outgoing = jnp.dot(place, partial_value.reshape(partials, hours), precision=HIGH)
        if "gather" not in routing:
            packed = jnp.concatenate([outgoing.reshape(owners, CAP, hours), id_rows], axis=1)
            landed, basin_sq = basin_exchange(packed.reshape(owners * (CAP + 8), hours), carry, 5)
            landed = landed.reshape(owners, CAP + 8, hours)
            got_ids = landed[:, CAP, :CAP].astype(jnp.int32).reshape(entries)
            routing["gather"] = (jnp.arange(gauges_here)[:, None] == got_ids[None, :]).astype(jnp.float32)
            incoming = landed[:, :CAP, :].reshape(entries, hours)
        else:
            incoming, basin_sq = basin_exchange(outgoing, squared_row(field))
        gather = routing["gather"]
        sums = jnp.dot(gather, incoming, precision=HIGH)
        earlier, total_sq = tm_shift(sums, basin_sq, 1, 2)
        return class_mix(jnp.concatenate([earlier, sums], axis=1), table_fwd, selector), jnp.sum(total_sq)

    def backward(series):
        later, tm_sq = tm_shift(series, squared_row(series), -1, 3)
        upstream = class_mix(jnp.concatenate([series, later], axis=1), table_bwd, selector)
        outgoing = jnp.dot(routing["gather"].T, upstream, precision=lax.Precision.HIGH)
        incoming, total_sq = basin_exchange(outgoing, tm_sq)
        rows = jnp.dot(place.T, incoming, precision=lax.Precision.HIGH)
        spread = jnp.einsum(
            "bjr,bjt->brt", weights, rows.reshape(blocks, slots, hours), precision=lax.Precision.HIGH
        )
        return spread.reshape(blocks * width, hours), jnp.sum(total_sq)

    start = observed - forward(first_guess, jnp.zeros((1, LANES), jnp.float32))[0]
    pulled_start, beta_sq = backward(start)
    beta = jnp.sqrt(beta_sq)
    u = start / beta
    pulled = pulled_start / beta
    forward_pulled, alpha_sq = forward(pulled)
    alpha = jnp.sqrt(alpha_sq)
    v = pulled / alpha
    w = v
    estimate = first_guess
    phibar = beta
    rhobar = alpha
    for step in range(ITERS):
        final = step == ITERS - 1
        p = forward_pulled / alpha - alpha * u
        if final:
            beta = jnp.sqrt(global_total(squared_row(p)))
        else:
            pulled_p, beta_sq = backward(p)
            beta = jnp.sqrt(beta_sq)
            pulled = pulled_p / beta - beta * v
            forward_pulled, alpha_next = forward(pulled)
            alpha_next = jnp.sqrt(alpha_next)
            v_next = pulled / alpha_next
        u = p / beta
        rho = jnp.sqrt(rhobar * rhobar + beta * beta)
        cosine = rhobar / rho
        sine = beta / rho
        phi = cosine * phibar
        phibar = sine * phibar
        estimate = estimate + phi / rho * w
        if not final:
            theta = sine * alpha_next
            rhobar = -cosine * alpha_next
            w = v_next - theta / rho * w
            v = v_next
            alpha = alpha_next
    return estimate


def solution(mesh):
    in_specs = (
        P("basin", None, None),
        P("basin"),
        P("basin"),
        P(),
        P("basin", "tm"),
        P("basin", "tm"),
    )
    out_specs = P("basin", "tm")
    return jax.shard_map(shards, mesh=mesh, in_specs=in_specs, out_specs=out_specs, check_vma=False)
```

```python
import functools

import jax
import jax.numpy as jnp
from jax import lax
from jax.experimental import pallas as pl
from jax.experimental.pallas import tpu as pltpu
from jax.sharding import PartitionSpec as P

ITERS = 3
CAP = 32
LANES = 128

HIGH = lax.Precision.HIGH
MESH = pl.DeviceIdType.MESH


def from_behind(x, axis, by):
    devices = lax.axis_size(axis)
    pairs = [(i, i + by) for i in range(devices) if 0 <= i + by < devices]
    return lax.ppermute(x, axis, pairs)


def lag_table(kernels, lag):
    classes, taps = kernels.shape
    rows, hours = lag.shape
    onehot = (lag.T[None, :, :] == jnp.arange(taps)[:, None, None]).astype(jnp.float32)
    picked = jnp.dot(kernels, onehot.reshape(taps, hours * rows), precision=HIGH)
    return picked.reshape(classes, hours, rows)


def class_mix(extended, table, selector):
    spread = lax.dot_general(extended, table, (((1,), (2,)), ((), ())), precision=lax.Precision.HIGH)
    return jnp.sum(spread * selector[:, :, None], axis=1)


def squared(values):
    return jnp.sum(values * values)


def squared_row(values):
    if values.shape[-1] == LANES:
        return jnp.sum(values * values, axis=0, keepdims=True)
    return as_row(squared(values))


def _total_body(x_ref, o_ref, tm_rows, all_rows, own_sem, tsend, trecv, bsend, brecv, *, nb, nt):
    me = lax.axis_index("basin")
    hb = lax.axis_index("tm")
    barrier = pltpu.get_barrier_semaphore()
    for j in range(1, nt):
        pl.semaphore_signal(barrier, inc=1, device_id=(me, lax.rem(hb + j, nt)), device_id_type=MESH)
    order = _peer_order(nb)
    if order is None:
        targets = [lax.rem(me + k, nb) for k in range(1, nb)]
        sources = [lax.rem(me + nb - k, nb) for k in range(1, nb)]
    else:
        targets = [_peer(me, o, 1) for o in order]
        sources = [_peer(me, o, -1) for o in order]
    for target in targets:
        pl.semaphore_signal(barrier, inc=1, device_id=(target, hb), device_id_type=MESH)
    pl.semaphore_wait(barrier, nt - 1 + nb - 1)

    own = pltpu.make_async_copy(x_ref, tm_rows.at[pl.ds(hb, 1)], own_sem.at[0])
    own.start()
    sends = []
    for j in range(1, nt):
        copy = pltpu.make_async_remote_copy(
            src_ref=x_ref, dst_ref=tm_rows.at[pl.ds(hb, 1)], send_sem=tsend.at[j], recv_sem=trecv.at[j],
            device_id=(me, lax.rem(hb + j, nt)), device_id_type=MESH,
        )
        copy.start()
        sends.append(copy)
    own.wait()
    for j in range(1, nt):
        sends[j - 1].wait_send()
        origin = lax.rem(hb + nt - j, nt)
        pltpu.make_async_remote_copy(
            src_ref=x_ref, dst_ref=tm_rows.at[pl.ds(origin, 1)], send_sem=tsend.at[j], recv_sem=trecv.at[j],
            device_id=(me, origin), device_id_type=MESH,
        ).wait_recv()

    own_block = pltpu.make_async_copy(tm_rows, all_rows.at[me], own_sem.at[1])
    own_block.start()
    blocks = []
    for i, target in enumerate(targets):
        copy = pltpu.make_async_remote_copy(
            src_ref=tm_rows, dst_ref=all_rows.at[me], send_sem=bsend.at[i], recv_sem=brecv.at[i],
            device_id=(target, hb), device_id_type=MESH,
        )
        copy.start()
        blocks.append(copy)
    own_block.wait()
    for i, source in enumerate(sources):
        blocks[i].wait_send()
        pltpu.make_async_remote_copy(
            src_ref=tm_rows, dst_ref=all_rows.at[source], send_sem=bsend.at[i], recv_sem=brecv.at[i],
            device_id=(source, hb), device_id_type=MESH,
        ).wait_recv()
    o_ref[...] = jnp.sum(all_rows[...].reshape(nb * nt, LANES), axis=0, keepdims=True)


def global_total(value):
    nb = lax.axis_size("basin")
    nt = lax.axis_size("tm")
    out = pl.pallas_call(
        functools.partial(_total_body, nb=nb, nt=nt),
        out_shape=jax.ShapeDtypeStruct((1, LANES), jnp.float32),
        in_specs=[pl.BlockSpec(memory_space=pltpu.VMEM)],
        out_specs=pl.BlockSpec(memory_space=pltpu.VMEM),
        scratch_shapes=[
            pltpu.VMEM((nt, LANES), jnp.float32),
            pltpu.VMEM((nb, nt, LANES), jnp.float32),
            pltpu.SemaphoreType.DMA((2,)),
            pltpu.SemaphoreType.DMA((nt,)),
            pltpu.SemaphoreType.DMA((nt,)),
            pltpu.SemaphoreType.DMA((nb,)),
            pltpu.SemaphoreType.DMA((nb,)),
        ],
        compiler_params=pltpu.CompilerParams(collective_id=0, has_side_effects=True),
    )(as_row(value))
    return jnp.sum(out)


def _peer_order(nb):
    if nb != 32:
        return None
    offsets = [(dz, dx, dc) for dz in range(4) for dx in range(4) for dc in range(2) if (dz, dx, dc) != (0, 0, 0)]
    return sorted(offsets, key=lambda o: (-(min(o[0], 4 - o[0]) + min(o[1], 4 - o[1])), o))


def _peer(me, offset, sign):
    if len(offset) == 1:
        return lax.rem(me + sign * offset[0] + 32 * 64, 32 * 64) % 32
    dz, dx, dc = offset
    z, x, c = me // 8, (me // 2) % 4, me % 2
    return ((z + sign * dz + 4) % 4) * 8 + ((x + sign * dx + 4) % 4) * 2 + (c + sign * dc + 2) % 2


def _exchange_body(x_ref, c_ref, landed, t_ref, carried, own_sem, send_sem, recv_sem, csend, crecv, *, nb):
    me = lax.axis_index("basin")
    hour_block = lax.axis_index("tm")
    order = _peer_order(nb)
    if order is None:
        order = [(k,) for k in range(1, nb)]
        targets = [lax.rem(me + k, nb) for k in range(1, nb)]
        sources = [lax.rem(me + nb - k, nb) for k in range(1, nb)]
    else:
        targets = [_peer(me, o, 1) for o in order]
        sources = [_peer(me, o, -1) for o in order]
    barrier = pltpu.get_barrier_semaphore()
    for target in targets:
        pl.semaphore_signal(barrier, inc=1, device_id=(target, hour_block), device_id_type=MESH)
    pl.semaphore_wait(barrier, nb - 1)
    own = pltpu.make_async_copy(x_ref.at[me], landed.at[me], own_sem.at[0])
    own.start()
    own_carry = pltpu.make_async_copy(c_ref, carried.at[pl.ds(me, 1)], own_sem.at[1])
    own_carry.start()
    copies = []
    for i, peer in enumerate(targets):
        copy = pltpu.make_async_remote_copy(
            src_ref=x_ref.at[peer],
            dst_ref=landed.at[me],
            send_sem=send_sem.at[i],
            recv_sem=recv_sem.at[i],
            device_id=(peer, hour_block),
            device_id_type=MESH,
        )
        copy.start()
        carry = pltpu.make_async_remote_copy(
            src_ref=c_ref,
            dst_ref=carried.at[pl.ds(me, 1)],
            send_sem=csend.at[i],
            recv_sem=crecv.at[i],
            device_id=(peer, hour_block),
            device_id_type=MESH,
        )
        carry.start()
        copies.append((copy, carry))
    own.wait()
    own_carry.wait()
    for i, source in enumerate(sources):
        copies[i][0].wait_send()
        copies[i][1].wait_send()
        pltpu.make_async_remote_copy(
            src_ref=x_ref.at[source],
            dst_ref=landed.at[source],
            send_sem=send_sem.at[i],
            recv_sem=recv_sem.at[i],
            device_id=(source, hour_block),
            device_id_type=MESH,
        ).wait_recv()
        pltpu.make_async_remote_copy(
            src_ref=c_ref,
            dst_ref=carried.at[pl.ds(source, 1)],
            send_sem=csend.at[i],
            recv_sem=crecv.at[i],
            device_id=(source, hour_block),
            device_id_type=MESH,
        ).wait_recv()
    t_ref[...] = jnp.sum(carried[...], axis=0, keepdims=True)


def as_row(value):
    if value.ndim == 2:
        return value
    return jnp.broadcast_to(value.astype(jnp.float32), (1, LANES))


def basin_exchange(x, carry, ident=1):
    nb = lax.axis_size("basin")
    total, hours = x.shape
    shaped = x.reshape(nb, total // nb, hours)
    out, summed = pl.pallas_call(
        functools.partial(_exchange_body, nb=nb),
        out_shape=(
            jax.ShapeDtypeStruct(shaped.shape, jnp.float32),
            jax.ShapeDtypeStruct((1, LANES), jnp.float32),
        ),
        in_specs=[pl.BlockSpec(memory_space=pltpu.VMEM)] * 2,
        out_specs=(pl.BlockSpec(memory_space=pltpu.VMEM),) * 2,
        scratch_shapes=[
            pltpu.VMEM((nb, LANES), jnp.float32),
            pltpu.SemaphoreType.DMA((2,)),
            pltpu.SemaphoreType.DMA((nb,)),
            pltpu.SemaphoreType.DMA((nb,)),
            pltpu.SemaphoreType.DMA((nb,)),
            pltpu.SemaphoreType.DMA((nb,)),
        ],
        compiler_params=pltpu.CompilerParams(collective_id=ident, has_side_effects=True),
    )(shaped, as_row(carry))
    return out.reshape(total, hours), summed


def _tm_order(nt):
    return sorted(range(1, nt), key=lambda k: (-min(k, nt - k), k))


def _shift_body(x_ref, c_ref, o_ref, t_ref, carried, own_sem, dsend, drecv, csend, crecv, *, nt, by):
    basin = lax.axis_index("basin")
    me = lax.axis_index("tm")
    barrier = pltpu.get_barrier_semaphore()
    for k in _tm_order(nt):
        pl.semaphore_signal(
            barrier, inc=1, device_id=(basin, lax.rem(me + k, nt)), device_id_type=MESH
        )
    pl.semaphore_wait(barrier, nt - 1)

    target = me + by
    source = me - by
    has_target = jnp.logical_and(target >= 0, target < nt)
    has_source = jnp.logical_and(source >= 0, source < nt)
    data = pltpu.make_async_remote_copy(
        src_ref=x_ref,
        dst_ref=o_ref,
        send_sem=dsend,
        recv_sem=drecv,
        device_id=(basin, lax.rem(target + nt, nt)),
        device_id_type=MESH,
    )

    @pl.when(has_target)
    def _():
        data.start()

    own = pltpu.make_async_copy(c_ref, carried.at[pl.ds(me, 1)], own_sem)
    own.start()
    copies = {}
    for k in _tm_order(nt):
        copy = pltpu.make_async_remote_copy(
            src_ref=c_ref,
            dst_ref=carried.at[pl.ds(me, 1)],
            send_sem=csend.at[k],
            recv_sem=crecv.at[k],
            device_id=(basin, lax.rem(me + k, nt)),
            device_id_type=MESH,
        )
        copy.start()
        copies[k] = copy
    own.wait()
    for k in _tm_order(nt):
        copies[k].wait_send()
        origin = lax.rem(me + nt - k, nt)
        pltpu.make_async_remote_copy(
            src_ref=c_ref,
            dst_ref=carried.at[pl.ds(origin, 1)],
            send_sem=csend.at[k],
            recv_sem=crecv.at[k],
            device_id=(basin, origin),
            device_id_type=MESH,
        ).wait_recv()
    t_ref[...] = jnp.sum(carried[...], axis=0, keepdims=True)

    @pl.when(has_target)
    def _():
        data.wait_send()

    @pl.when(has_source)
    def _():
        data.wait_recv()

    @pl.when(jnp.logical_not(has_source))
    def _():
        o_ref[...] = jnp.zeros(o_ref.shape, o_ref.dtype)


def tm_shift(x, carry, by, ident):
    nt = lax.axis_size("tm")
    c = as_row(carry)
    out, summed = pl.pallas_call(
        functools.partial(_shift_body, nt=nt, by=by),
        out_shape=(
            jax.ShapeDtypeStruct(x.shape, jnp.float32),
            jax.ShapeDtypeStruct((1, LANES), jnp.float32),
        ),
        in_specs=[pl.BlockSpec(memory_space=pltpu.VMEM)] * 2,
        out_specs=(pl.BlockSpec(memory_space=pltpu.VMEM),) * 2,
        scratch_shapes=[
            pltpu.VMEM((nt, LANES), jnp.float32),
            pltpu.SemaphoreType.DMA(()),
            pltpu.SemaphoreType.DMA(()),
            pltpu.SemaphoreType.DMA(()),
            pltpu.SemaphoreType.DMA((nt,)),
            pltpu.SemaphoreType.DMA((nt,)),
        ],
        compiler_params=pltpu.CompilerParams(collective_id=ident, has_side_effects=True),
    )(x, c)
    return out, summed


def shards(incidence, row_gauge, gauge_kernel, kernels, observed, first_guess):
    weights = incidence.astype(jnp.float32)
    blocks, slots, width = weights.shape
    gauges_here, hours = observed.shape
    owners = lax.axis_size("basin")
    classes = kernels.shape[0]
    partials = blocks * slots
    outer = jnp.arange(2 * hours)[:, None]
    inner = jnp.arange(hours)[None, :]
    table_fwd = lag_table(kernels, inner + hours - outer)
    table_bwd = lag_table(kernels, outer - inner)
    selector = (gauge_kernel[:, None] == jnp.arange(classes)[None, :]).astype(jnp.float32)

    owner = row_gauge // gauges_here
    local = row_gauge % gauges_here
    hit = owner[:, None] == jnp.arange(owners)[None, :]
    rank = jnp.cumsum(hit.astype(jnp.int32), axis=0) - 1
    dest = owner * CAP + jnp.sum(jnp.where(hit, rank, 0), axis=1)
    entries = owners * CAP
    place = (jnp.arange(entries)[:, None] == dest[None, :]).astype(jnp.float32)
    sent_ids = jnp.full((entries,), -1, jnp.int32).at[dest].set(local)
    id_rows = jnp.zeros((owners, 8, hours), jnp.float32)
    id_rows = id_rows.at[:, 0, :CAP].set(sent_ids.reshape(owners, CAP).astype(jnp.float32))
    routing = {}

    def forward(field, carry=None):
        partial_value = jnp.einsum(
            "bjr,brt->bjt", weights, field.reshape(blocks, width, hours), precision=HIGH
        )
        outgoing = jnp.dot(place, partial_value.reshape(partials, hours), precision=HIGH)
        if "gather" not in routing:
            packed = jnp.concatenate([outgoing.reshape(owners, CAP, hours), id_rows], axis=1)
            landed, basin_sq = basin_exchange(packed.reshape(owners * (CAP + 8), hours), carry, 5)
            landed = landed.reshape(owners, CAP + 8, hours)
            got_ids = landed[:, CAP, :CAP].astype(jnp.int32).reshape(entries)
            routing["gather"] = (jnp.arange(gauges_here)[:, None] == got_ids[None, :]).astype(jnp.float32)
            incoming = landed[:, :CAP, :].reshape(entries, hours)
        else:
            incoming, basin_sq = basin_exchange(outgoing, squared_row(field))
        gather = routing["gather"]
        sums = jnp.dot(gather, incoming, precision=HIGH)
        earlier, total_sq = tm_shift(sums, basin_sq, 1, 2)
        return class_mix(jnp.concatenate([earlier, sums], axis=1), table_fwd, selector), jnp.sum(total_sq)

    def backward(series):
        later, tm_sq = tm_shift(series, squared_row(series), -1, 3)
        upstream = class_mix(jnp.concatenate([series, later], axis=1), table_bwd, selector)
        outgoing = jnp.dot(routing["gather"].T, upstream, precision=lax.Precision.HIGH)
        incoming, total_sq = basin_exchange(outgoing, tm_sq)
        rows = jnp.dot(place.T, incoming, precision=lax.Precision.HIGH)
        spread = jnp.einsum(
            "bjr,bjt->brt", weights, rows.reshape(blocks, slots, hours), precision=lax.Precision.HIGH
        )
        return spread.reshape(blocks * width, hours), jnp.sum(total_sq)

    start = observed - forward(first_guess, jnp.zeros((1, LANES), jnp.float32))[0]
    pulled_start, beta_sq = backward(start)
    beta = jnp.sqrt(beta_sq)
    u = start / beta
    pulled = pulled_start / beta
    forward_pulled, alpha_sq = forward(pulled)
    alpha = jnp.sqrt(alpha_sq)
    v = pulled / alpha
    w = v
    estimate = first_guess
    phibar = beta
    rhobar = alpha
    for step in range(ITERS):
        final = step == ITERS - 1
        p = forward_pulled / alpha - alpha * u
        if final:
            beta = jnp.sqrt(global_total(squared_row(p)))
        else:
            pulled_p, beta_sq = backward(p)
            beta = jnp.sqrt(beta_sq)
            pulled = pulled_p / beta - beta * v
            forward_pulled, alpha_next = forward(pulled)
            alpha_next = jnp.sqrt(alpha_next)
            v_next = pulled / alpha_next
        u = p / beta
        rho = jnp.sqrt(rhobar * rhobar + beta * beta)
        cosine = rhobar / rho
        sine = beta / rho
        phi = cosine * phibar
        phibar = sine * phibar
        estimate = estimate + phi / rho * w
        if not final:
            theta = sine * alpha_next
            rhobar = -cosine * alpha_next
            w = v_next - theta / rho * w
            v = v_next
            alpha = alpha_next
    return estimate


def solution(mesh):
    in_specs = (
        P("basin", None, None),
        P("basin"),
        P("basin"),
        P(),
        P("basin", "tm"),
        P("basin", "tm"),
    )
    out_specs = P("basin", "tm")
    return jax.shard_map(shards, mesh=mesh, in_specs=in_specs, out_specs=out_specs, check_vma=False)
```

```python
import functools

import jax
import jax.numpy as jnp
from jax import lax
from jax.experimental import pallas as pl
from jax.experimental.pallas import tpu as pltpu
from jax.sharding import PartitionSpec as P

ITERS = 3
CAP = 32
LANES = 128

HIGH = lax.Precision.HIGH
MESH = pl.DeviceIdType.MESH


def from_behind(x, axis, by):
    devices = lax.axis_size(axis)
    pairs = [(i, i + by) for i in range(devices) if 0 <= i + by < devices]
    return lax.ppermute(x, axis, pairs)


def lag_table(kernels, lag):
    classes, taps = kernels.shape
    rows, hours = lag.shape
    onehot = (lag.T[None, :, :] == jnp.arange(taps)[:, None, None]).astype(jnp.float32)
    picked = jnp.dot(kernels, onehot.reshape(taps, hours * rows), precision=HIGH)
    return picked.reshape(classes, hours, rows)


def class_mix(extended, table, selector):
    spread = lax.dot_general(extended, table, (((1,), (2,)), ((), ())), precision=lax.Precision.HIGH)
    return jnp.sum(spread * selector[:, :, None], axis=1)


def squared(values):
    return jnp.sum(values * values)


def squared_row(values):
    if values.shape[-1] == LANES:
        return jnp.sum(values * values, axis=0, keepdims=True)
    return as_row(squared(values))


def _total_body(x_ref, o_ref, tm_rows, all_rows, own_sem, tsend, trecv, bsend, brecv, *, nb, nt):
    me = lax.axis_index("basin")
    hb = lax.axis_index("tm")
    barrier = pltpu.get_barrier_semaphore()
    for j in range(1, nt):
        pl.semaphore_signal(barrier, inc=1, device_id=(me, lax.rem(hb + j, nt)), device_id_type=MESH)
    order = _peer_order(nb)
    if order is None:
        targets = [lax.rem(me + k, nb) for k in range(1, nb)]
        sources = [lax.rem(me + nb - k, nb) for k in range(1, nb)]
    else:
        targets = [_peer(me, o, 1) for o in order]
        sources = [_peer(me, o, -1) for o in order]
    for target in targets:
        pl.semaphore_signal(barrier, inc=1, device_id=(target, hb), device_id_type=MESH)
    pl.semaphore_wait(barrier, nt - 1 + nb - 1)

    own = pltpu.make_async_copy(x_ref, tm_rows.at[pl.ds(hb, 1)], own_sem.at[0])
    own.start()
    sends = []
    for j in range(1, nt):
        copy = pltpu.make_async_remote_copy(
            src_ref=x_ref, dst_ref=tm_rows.at[pl.ds(hb, 1)], send_sem=tsend.at[j], recv_sem=trecv.at[j],
            device_id=(me, lax.rem(hb + j, nt)), device_id_type=MESH,
        )
        copy.start()
        sends.append(copy)
    own.wait()
    for j in range(1, nt):
        sends[j - 1].wait_send()
        origin = lax.rem(hb + nt - j, nt)
        pltpu.make_async_remote_copy(
            src_ref=x_ref, dst_ref=tm_rows.at[pl.ds(origin, 1)], send_sem=tsend.at[j], recv_sem=trecv.at[j],
            device_id=(me, origin), device_id_type=MESH,
        ).wait_recv()

    own_block = pltpu.make_async_copy(tm_rows, all_rows.at[me], own_sem.at[1])
    own_block.start()
    blocks = []
    for i, target in enumerate(targets):
        copy = pltpu.make_async_remote_copy(
            src_ref=tm_rows, dst_ref=all_rows.at[me], send_sem=bsend.at[i], recv_sem=brecv.at[i],
            device_id=(target, hb), device_id_type=MESH,
        )
        copy.start()
        blocks.append(copy)
    own_block.wait()
    for i, source in enumerate(sources):
        blocks[i].wait_send()
        pltpu.make_async_remote_copy(
            src_ref=tm_rows, dst_ref=all_rows.at[source], send_sem=bsend.at[i], recv_sem=brecv.at[i],
            device_id=(source, hb), device_id_type=MESH,
        ).wait_recv()
    o_ref[...] = jnp.sum(all_rows[...].reshape(nb * nt, LANES), axis=0, keepdims=True)


def global_total(value):
    nb = lax.axis_size("basin")
    nt = lax.axis_size("tm")
    out = pl.pallas_call(
        functools.partial(_total_body, nb=nb, nt=nt),
        out_shape=jax.ShapeDtypeStruct((1, LANES), jnp.float32),
        in_specs=[pl.BlockSpec(memory_space=pltpu.VMEM)],
        out_specs=pl.BlockSpec(memory_space=pltpu.VMEM),
        scratch_shapes=[
            pltpu.VMEM((nt, LANES), jnp.float32),
            pltpu.VMEM((nb, nt, LANES), jnp.float32),
            pltpu.SemaphoreType.DMA((2,)),
            pltpu.SemaphoreType.DMA((nt,)),
            pltpu.SemaphoreType.DMA((nt,)),
            pltpu.SemaphoreType.DMA((nb,)),
            pltpu.SemaphoreType.DMA((nb,)),
        ],
        compiler_params=pltpu.CompilerParams(collective_id=0, has_side_effects=True),
    )(as_row(value))
    return jnp.sum(out)


def _peer_order(nb):
    if nb != 32:
        return None
    offsets = [(dz, dx, dc) for dz in range(4) for dx in range(4) for dc in range(2) if (dz, dx, dc) != (0, 0, 0)]
    return sorted(offsets, key=lambda o: (-(min(o[0], 4 - o[0]) + min(o[1], 4 - o[1])), o))


def _peer(me, offset, sign):
    if len(offset) == 1:
        return lax.rem(me + sign * offset[0] + 32 * 64, 32 * 64) % 32
    dz, dx, dc = offset
    z, x, c = me // 8, (me // 2) % 4, me % 2
    return ((z + sign * dz + 4) % 4) * 8 + ((x + sign * dx + 4) % 4) * 2 + (c + sign * dc + 2) % 2


def _exchange_body(x_ref, c_ref, landed, t_ref, carried, own_sem, send_sem, recv_sem, csend, crecv, *, nb):
    me = lax.axis_index("basin")
    hour_block = lax.axis_index("tm")
    order = _peer_order(nb)
    if order is None:
        order = [(k,) for k in range(1, nb)]
        targets = [lax.rem(me + k, nb) for k in range(1, nb)]
        sources = [lax.rem(me + nb - k, nb) for k in range(1, nb)]
    else:
        targets = [_peer(me, o, 1) for o in order]
        sources = [_peer(me, o, -1) for o in order]
    barrier = pltpu.get_barrier_semaphore()
    for target in targets:
        pl.semaphore_signal(barrier, inc=1, device_id=(target, hour_block), device_id_type=MESH)
    pl.semaphore_wait(barrier, nb - 1)
    copies = []
    for i, peer in enumerate(targets):
        copy = pltpu.make_async_remote_copy(
            src_ref=x_ref.at[peer],
            dst_ref=landed.at[me],
            send_sem=send_sem.at[i],
            recv_sem=recv_sem.at[i],
            device_id=(peer, hour_block),
            device_id_type=MESH,
        )
        copy.start()
        carry = pltpu.make_async_remote_copy(
            src_ref=c_ref,
            dst_ref=carried.at[pl.ds(me, 1)],
            send_sem=csend.at[i],
            recv_sem=crecv.at[i],
            device_id=(peer, hour_block),
            device_id_type=MESH,
        )
        carry.start()
        copies.append((copy, carry))
    own = pltpu.make_async_copy(x_ref.at[me], landed.at[me], own_sem.at[0])
    own.start()
    own_carry = pltpu.make_async_copy(c_ref, carried.at[pl.ds(me, 1)], own_sem.at[1])
    own_carry.start()
    own.wait()
    own_carry.wait()
    for i, source in enumerate(sources):
        copies[i][0].wait_send()
        copies[i][1].wait_send()
        pltpu.make_async_remote_copy(
            src_ref=x_ref.at[source],
            dst_ref=landed.at[source],
            send_sem=send_sem.at[i],
            recv_sem=recv_sem.at[i],
            device_id=(source, hour_block),
            device_id_type=MESH,
        ).wait_recv()
        pltpu.make_async_remote_copy(
            src_ref=c_ref,
            dst_ref=carried.at[pl.ds(source, 1)],
            send_sem=csend.at[i],
            recv_sem=crecv.at[i],
            device_id=(source, hour_block),
            device_id_type=MESH,
        ).wait_recv()
    t_ref[...] = jnp.sum(carried[...], axis=0, keepdims=True)


def as_row(value):
    if value.ndim == 2:
        return value
    return jnp.broadcast_to(value.astype(jnp.float32), (1, LANES))


def basin_exchange(x, carry, ident=1):
    nb = lax.axis_size("basin")
    total, hours = x.shape
    shaped = x.reshape(nb, total // nb, hours)
    out, summed = pl.pallas_call(
        functools.partial(_exchange_body, nb=nb),
        out_shape=(
            jax.ShapeDtypeStruct(shaped.shape, jnp.float32),
            jax.ShapeDtypeStruct((1, LANES), jnp.float32),
        ),
        in_specs=[pl.BlockSpec(memory_space=pltpu.VMEM)] * 2,
        out_specs=(pl.BlockSpec(memory_space=pltpu.VMEM),) * 2,
        scratch_shapes=[
            pltpu.VMEM((nb, LANES), jnp.float32),
            pltpu.SemaphoreType.DMA((2,)),
            pltpu.SemaphoreType.DMA((nb,)),
            pltpu.SemaphoreType.DMA((nb,)),
            pltpu.SemaphoreType.DMA((nb,)),
            pltpu.SemaphoreType.DMA((nb,)),
        ],
        compiler_params=pltpu.CompilerParams(collective_id=ident, has_side_effects=True),
    )(shaped, as_row(carry))
    return out.reshape(total, hours), summed


def _shift_body(x_ref, c_ref, o_ref, t_ref, carried, own_sem, dsend, drecv, csend, crecv, *, nt, by):
    basin = lax.axis_index("basin")
    me = lax.axis_index("tm")
    barrier = pltpu.get_barrier_semaphore()
    for k in range(1, nt):
        pl.semaphore_signal(
            barrier, inc=1, device_id=(basin, lax.rem(me + k, nt)), device_id_type=MESH
        )
    pl.semaphore_wait(barrier, nt - 1)

    target = me + by
    source = me - by
    has_target = jnp.logical_and(target >= 0, target < nt)
    has_source = jnp.logical_and(source >= 0, source < nt)
    data = pltpu.make_async_remote_copy(
        src_ref=x_ref,
        dst_ref=o_ref,
        send_sem=dsend,
        recv_sem=drecv,
        device_id=(basin, lax.rem(target + nt, nt)),
        device_id_type=MESH,
    )

    @pl.when(has_target)
    def _():
        data.start()

    own = pltpu.make_async_copy(c_ref, carried.at[pl.ds(me, 1)], own_sem)
    own.start()
    copies = []
    for k in range(1, nt):
        copy = pltpu.make_async_remote_copy(
            src_ref=c_ref,
            dst_ref=carried.at[pl.ds(me, 1)],
            send_sem=csend.at[k],
            recv_sem=crecv.at[k],
            device_id=(basin, lax.rem(me + k, nt)),
            device_id_type=MESH,
        )
        copy.start()
        copies.append(copy)
    own.wait()
    for k in range(1, nt):
        copies[k - 1].wait_send()
        origin = lax.rem(me + nt - k, nt)
        pltpu.make_async_remote_copy(
            src_ref=c_ref,
            dst_ref=carried.at[pl.ds(origin, 1)],
            send_sem=csend.at[k],
            recv_sem=crecv.at[k],
            device_id=(basin, origin),
            device_id_type=MESH,
        ).wait_recv()
    t_ref[...] = jnp.sum(carried[...], axis=0, keepdims=True)

    @pl.when(has_target)
    def _():
        data.wait_send()

    @pl.when(has_source)
    def _():
        data.wait_recv()

    @pl.when(jnp.logical_not(has_source))
    def _():
        o_ref[...] = jnp.zeros(o_ref.shape, o_ref.dtype)


def tm_shift(x, carry, by, ident):
    nt = lax.axis_size("tm")
    c = as_row(carry)
    out, summed = pl.pallas_call(
        functools.partial(_shift_body, nt=nt, by=by),
        out_shape=(
            jax.ShapeDtypeStruct(x.shape, jnp.float32),
            jax.ShapeDtypeStruct((1, LANES), jnp.float32),
        ),
        in_specs=[pl.BlockSpec(memory_space=pltpu.VMEM)] * 2,
        out_specs=(pl.BlockSpec(memory_space=pltpu.VMEM),) * 2,
        scratch_shapes=[
            pltpu.VMEM((nt, LANES), jnp.float32),
            pltpu.SemaphoreType.DMA(()),
            pltpu.SemaphoreType.DMA(()),
            pltpu.SemaphoreType.DMA(()),
            pltpu.SemaphoreType.DMA((nt,)),
            pltpu.SemaphoreType.DMA((nt,)),
        ],
        compiler_params=pltpu.CompilerParams(collective_id=ident, has_side_effects=True),
    )(x, c)
    return out, summed


def shards(incidence, row_gauge, gauge_kernel, kernels, observed, first_guess):
    weights = incidence.astype(jnp.float32)
    blocks, slots, width = weights.shape
    gauges_here, hours = observed.shape
    owners = lax.axis_size("basin")
    classes = kernels.shape[0]
    partials = blocks * slots
    outer = jnp.arange(2 * hours)[:, None]
    inner = jnp.arange(hours)[None, :]
    table_fwd = lag_table(kernels, inner + hours - outer)
    table_bwd = lag_table(kernels, outer - inner)
    selector = (gauge_kernel[:, None] == jnp.arange(classes)[None, :]).astype(jnp.float32)

    owner = row_gauge // gauges_here
    local = row_gauge % gauges_here
    hit = owner[:, None] == jnp.arange(owners)[None, :]
    rank = jnp.cumsum(hit.astype(jnp.int32), axis=0) - 1
    dest = owner * CAP + jnp.sum(jnp.where(hit, rank, 0), axis=1)
    entries = owners * CAP
    place = (jnp.arange(entries)[:, None] == dest[None, :]).astype(jnp.float32)
    sent_ids = jnp.full((entries,), -1, jnp.int32).at[dest].set(local)
    id_rows = jnp.zeros((owners, 8, hours), jnp.float32)
    id_rows = id_rows.at[:, 0, :CAP].set(sent_ids.reshape(owners, CAP).astype(jnp.float32))
    routing = {}

    def forward(field, carry=None):
        partial_value = jnp.einsum(
            "bjr,brt->bjt", weights, field.reshape(blocks, width, hours), precision=HIGH
        )
        outgoing = jnp.dot(place, partial_value.reshape(partials, hours), precision=HIGH)
        if "gather" not in routing:
            packed = jnp.concatenate([outgoing.reshape(owners, CAP, hours), id_rows], axis=1)
            landed, basin_sq = basin_exchange(packed.reshape(owners * (CAP + 8), hours), carry, 5)
            landed = landed.reshape(owners, CAP + 8, hours)
            got_ids = landed[:, CAP, :CAP].astype(jnp.int32).reshape(entries)
            routing["gather"] = (jnp.arange(gauges_here)[:, None] == got_ids[None, :]).astype(jnp.float32)
            incoming = landed[:, :CAP, :].reshape(entries, hours)
        else:
            incoming, basin_sq = basin_exchange(outgoing, squared_row(field))
        gather = routing["gather"]
        sums = jnp.dot(gather, incoming, precision=HIGH)
        earlier, total_sq = tm_shift(sums, basin_sq, 1, 2)
        return class_mix(jnp.concatenate([earlier, sums], axis=1), table_fwd, selector), jnp.sum(total_sq)

    def backward(series):
        later, tm_sq = tm_shift(series, squared_row(series), -1, 3)
        upstream = class_mix(jnp.concatenate([series, later], axis=1), table_bwd, selector)
        outgoing = jnp.dot(routing["gather"].T, upstream, precision=lax.Precision.HIGH)
        incoming, total_sq = basin_exchange(outgoing, tm_sq)
        rows = jnp.dot(place.T, incoming, precision=lax.Precision.HIGH)
        spread = jnp.einsum(
            "bjr,bjt->brt", weights, rows.reshape(blocks, slots, hours), precision=lax.Precision.HIGH
        )
        return spread.reshape(blocks * width, hours), jnp.sum(total_sq)

    start = observed - forward(first_guess, jnp.zeros((1, LANES), jnp.float32))[0]
    pulled_start, beta_sq = backward(start)
    beta = jnp.sqrt(beta_sq)
    u = start / beta
    pulled = pulled_start / beta
    forward_pulled, alpha_sq = forward(pulled)
    alpha = jnp.sqrt(alpha_sq)
    v = pulled / alpha
    w = v
    estimate = first_guess
    phibar = beta
    rhobar = alpha
    for step in range(ITERS):
        final = step == ITERS - 1
        p = forward_pulled / alpha - alpha * u
        if final:
            beta = jnp.sqrt(global_total(squared_row(p)))
        else:
            pulled_p, beta_sq = backward(p)
            beta = jnp.sqrt(beta_sq)
            pulled = pulled_p / beta - beta * v
            forward_pulled, alpha_next = forward(pulled)
            alpha_next = jnp.sqrt(alpha_next)
            v_next = pulled / alpha_next
        u = p / beta
        rho = jnp.sqrt(rhobar * rhobar + beta * beta)
        cosine = rhobar / rho
        sine = beta / rho
        phi = cosine * phibar
        phibar = sine * phibar
        estimate = estimate + phi / rho * w
        if not final:
            theta = sine * alpha_next
            rhobar = -cosine * alpha_next
            w = v_next - theta / rho * w
            v = v_next
            alpha = alpha_next
    return estimate


def solution(mesh):
    in_specs = (
        P("basin", None, None),
        P("basin"),
        P("basin"),
        P(),
        P("basin", "tm"),
        P("basin", "tm"),
    )
    out_specs = P("basin", "tm")
    return jax.shard_map(shards, mesh=mesh, in_specs=in_specs, out_specs=out_specs, check_vma=False)
```

```python
import functools

import jax
import jax.numpy as jnp
from jax import lax
from jax.experimental import pallas as pl
from jax.experimental.pallas import tpu as pltpu
from jax.sharding import PartitionSpec as P

ITERS = 3
CAP = 32
LANES = 128

HIGH = lax.Precision.HIGH
MESH = pl.DeviceIdType.MESH


def from_behind(x, axis, by):
    devices = lax.axis_size(axis)
    pairs = [(i, i + by) for i in range(devices) if 0 <= i + by < devices]
    return lax.ppermute(x, axis, pairs)


def lag_table(kernels, lag):
    classes, taps = kernels.shape
    rows, hours = lag.shape
    onehot = (lag.T[None, :, :] == jnp.arange(taps)[:, None, None]).astype(jnp.float32)
    picked = jnp.dot(kernels, onehot.reshape(taps, hours * rows), precision=HIGH)
    return picked.reshape(classes, hours, rows)


def class_mix(extended, table, selector):
    spread = lax.dot_general(extended, table, (((1,), (2,)), ((), ())), precision=lax.Precision.HIGH)
    return jnp.sum(spread * selector[:, :, None], axis=1)


def squared(values):
    return jnp.sum(values * values)


def squared_row(values):
    if values.shape[-1] == LANES:
        return jnp.sum(values * values, axis=0, keepdims=True)
    return as_row(squared(values))


def _total_body(x_ref, o_ref, tm_rows, all_rows, own_sem, tsend, trecv, bsend, brecv, *, nb, nt):
    me = lax.axis_index("basin")
    hb = lax.axis_index("tm")
    barrier = pltpu.get_barrier_semaphore()
    for j in range(1, nt):
        pl.semaphore_signal(barrier, inc=1, device_id=(me, lax.rem(hb + j, nt)), device_id_type=MESH)
    order = _peer_order(nb)
    if order is None:
        targets = [lax.rem(me + k, nb) for k in range(1, nb)]
        sources = [lax.rem(me + nb - k, nb) for k in range(1, nb)]
    else:
        targets = [_peer(me, o, 1) for o in order]
        sources = [_peer(me, o, -1) for o in order]
    for target in targets:
        pl.semaphore_signal(barrier, inc=1, device_id=(target, hb), device_id_type=MESH)
    pl.semaphore_wait(barrier, nt - 1 + nb - 1)

    own = pltpu.make_async_copy(x_ref, tm_rows.at[pl.ds(hb, 1)], own_sem.at[0])
    own.start()
    sends = []
    for j in range(1, nt):
        copy = pltpu.make_async_remote_copy(
            src_ref=x_ref, dst_ref=tm_rows.at[pl.ds(hb, 1)], send_sem=tsend.at[j], recv_sem=trecv.at[j],
            device_id=(me, lax.rem(hb + j, nt)), device_id_type=MESH,
        )
        copy.start()
        sends.append(copy)
    own.wait()
    for j in range(1, nt):
        sends[j - 1].wait_send()
        origin = lax.rem(hb + nt - j, nt)
        pltpu.make_async_remote_copy(
            src_ref=x_ref, dst_ref=tm_rows.at[pl.ds(origin, 1)], send_sem=tsend.at[j], recv_sem=trecv.at[j],
            device_id=(me, origin), device_id_type=MESH,
        ).wait_recv()

    own_block = pltpu.make_async_copy(tm_rows, all_rows.at[me], own_sem.at[1])
    own_block.start()
    blocks = []
    for i, target in enumerate(targets):
        copy = pltpu.make_async_remote_copy(
            src_ref=tm_rows, dst_ref=all_rows.at[me], send_sem=bsend.at[i], recv_sem=brecv.at[i],
            device_id=(target, hb), device_id_type=MESH,
        )
        copy.start()
        blocks.append(copy)
    own_block.wait()
    for i, source in enumerate(sources):
        blocks[i].wait_send()
        pltpu.make_async_remote_copy(
            src_ref=tm_rows, dst_ref=all_rows.at[source], send_sem=bsend.at[i], recv_sem=brecv.at[i],
            device_id=(source, hb), device_id_type=MESH,
        ).wait_recv()
    o_ref[...] = jnp.sum(all_rows[...].reshape(nb * nt, LANES), axis=0, keepdims=True)


def global_total(value):
    nb = lax.axis_size("basin")
    nt = lax.axis_size("tm")
    out = pl.pallas_call(
        functools.partial(_total_body, nb=nb, nt=nt),
        out_shape=jax.ShapeDtypeStruct((1, LANES), jnp.float32),
        in_specs=[pl.BlockSpec(memory_space=pltpu.VMEM)],
        out_specs=pl.BlockSpec(memory_space=pltpu.VMEM),
        scratch_shapes=[
            pltpu.VMEM((nt, LANES), jnp.float32),
            pltpu.VMEM((nb, nt, LANES), jnp.float32),
            pltpu.SemaphoreType.DMA((2,)),
            pltpu.SemaphoreType.DMA((nt,)),
            pltpu.SemaphoreType.DMA((nt,)),
            pltpu.SemaphoreType.DMA((nb,)),
            pltpu.SemaphoreType.DMA((nb,)),
        ],
        compiler_params=pltpu.CompilerParams(collective_id=0, has_side_effects=True),
    )(as_row(value))
    return jnp.sum(out)


def _peer_order(nb):
    if nb != 32:
        return None
    offsets = [(dz, dx, dc) for dz in range(4) for dx in range(4) for dc in range(2) if (dz, dx, dc) != (0, 0, 0)]
    return sorted(offsets, key=lambda o: (-(min(o[0], 4 - o[0]) + min(o[1], 4 - o[1])), o))


def _peer(me, offset, sign):
    if len(offset) == 1:
        return lax.rem(me + sign * offset[0] + 32 * 64, 32 * 64) % 32
    dz, dx, dc = offset
    z, x, c = me // 8, (me // 2) % 4, me % 2
    return ((z + sign * dz + 4) % 4) * 8 + ((x + sign * dx + 4) % 4) * 2 + (c + sign * dc + 2) % 2


def _exchange_body(x_ref, c_ref, landed, t_ref, carried, own_sem, send_sem, recv_sem, csend, crecv, *, nb):
    me = lax.axis_index("basin")
    hour_block = lax.axis_index("tm")
    order = _peer_order(nb)
    if order is None:
        order = [(k,) for k in range(1, nb)]
        targets = [lax.rem(me + k, nb) for k in range(1, nb)]
        sources = [lax.rem(me + nb - k, nb) for k in range(1, nb)]
    else:
        targets = [_peer(me, o, 1) for o in order]
        sources = [_peer(me, o, -1) for o in order]
    barrier = pltpu.get_barrier_semaphore()
    for target in targets:
        pl.semaphore_signal(barrier, inc=1, device_id=(target, hour_block), device_id_type=MESH)
    pl.semaphore_wait(barrier, nb - 1)
    own = pltpu.make_async_copy(x_ref.at[me], landed.at[me], own_sem.at[0])
    own.start()
    own_carry = pltpu.make_async_copy(c_ref, carried.at[pl.ds(me, 1)], own_sem.at[1])
    own_carry.start()
    copies = []
    for i, peer in enumerate(targets):
        copy = pltpu.make_async_remote_copy(
            src_ref=x_ref.at[peer],
            dst_ref=landed.at[me],
            send_sem=send_sem.at[i],
            recv_sem=recv_sem.at[i],
            device_id=(peer, hour_block),
            device_id_type=MESH,
        )
        copy.start()
        copies.append([copy])
    for i, peer in enumerate(targets):
        carry = pltpu.make_async_remote_copy(
            src_ref=c_ref,
            dst_ref=carried.at[pl.ds(me, 1)],
            send_sem=csend.at[i],
            recv_sem=crecv.at[i],
            device_id=(peer, hour_block),
            device_id_type=MESH,
        )
        carry.start()
        copies[i].append(carry)
    own.wait()
    own_carry.wait()
    for i, source in enumerate(sources):
        copies[i][0].wait_send()
        copies[i][1].wait_send()
        pltpu.make_async_remote_copy(
            src_ref=x_ref.at[source],
            dst_ref=landed.at[source],
            send_sem=send_sem.at[i],
            recv_sem=recv_sem.at[i],
            device_id=(source, hour_block),
            device_id_type=MESH,
        ).wait_recv()
        pltpu.make_async_remote_copy(
            src_ref=c_ref,
            dst_ref=carried.at[pl.ds(source, 1)],
            send_sem=csend.at[i],
            recv_sem=crecv.at[i],
            device_id=(source, hour_block),
            device_id_type=MESH,
        ).wait_recv()
    t_ref[...] = jnp.sum(carried[...], axis=0, keepdims=True)


def as_row(value):
    if value.ndim == 2:
        return value
    return jnp.broadcast_to(value.astype(jnp.float32), (1, LANES))


def basin_exchange(x, carry, ident=1):
    nb = lax.axis_size("basin")
    total, hours = x.shape
    shaped = x.reshape(nb, total // nb, hours)
    out, summed = pl.pallas_call(
        functools.partial(_exchange_body, nb=nb),
        out_shape=(
            jax.ShapeDtypeStruct(shaped.shape, jnp.float32),
            jax.ShapeDtypeStruct((1, LANES), jnp.float32),
        ),
        in_specs=[pl.BlockSpec(memory_space=pltpu.VMEM)] * 2,
        out_specs=(pl.BlockSpec(memory_space=pltpu.VMEM),) * 2,
        scratch_shapes=[
            pltpu.VMEM((nb, LANES), jnp.float32),
            pltpu.SemaphoreType.DMA((2,)),
            pltpu.SemaphoreType.DMA((nb,)),
            pltpu.SemaphoreType.DMA((nb,)),
            pltpu.SemaphoreType.DMA((nb,)),
            pltpu.SemaphoreType.DMA((nb,)),
        ],
        compiler_params=pltpu.CompilerParams(collective_id=ident, has_side_effects=True),
    )(shaped, as_row(carry))
    return out.reshape(total, hours), summed


def _shift_body(x_ref, c_ref, o_ref, t_ref, carried, own_sem, dsend, drecv, csend, crecv, *, nt, by):
    basin = lax.axis_index("basin")
    me = lax.axis_index("tm")
    barrier = pltpu.get_barrier_semaphore()
    for k in range(1, nt):
        pl.semaphore_signal(
            barrier, inc=1, device_id=(basin, lax.rem(me + k, nt)), device_id_type=MESH
        )
    pl.semaphore_wait(barrier, nt - 1)

    target = me + by
    source = me - by
    has_target = jnp.logical_and(target >= 0, target < nt)
    has_source = jnp.logical_and(source >= 0, source < nt)
    data = pltpu.make_async_remote_copy(
        src_ref=x_ref,
        dst_ref=o_ref,
        send_sem=dsend,
        recv_sem=drecv,
        device_id=(basin, lax.rem(target + nt, nt)),
        device_id_type=MESH,
    )

    @pl.when(has_target)
    def _():
        data.start()

    own = pltpu.make_async_copy(c_ref, carried.at[pl.ds(me, 1)], own_sem)
    own.start()
    copies = []
    for k in range(1, nt):
        copy = pltpu.make_async_remote_copy(
            src_ref=c_ref,
            dst_ref=carried.at[pl.ds(me, 1)],
            send_sem=csend.at[k],
            recv_sem=crecv.at[k],
            device_id=(basin, lax.rem(me + k, nt)),
            device_id_type=MESH,
        )
        copy.start()
        copies.append(copy)
    own.wait()
    for k in range(1, nt):
        copies[k - 1].wait_send()
        origin = lax.rem(me + nt - k, nt)
        pltpu.make_async_remote_copy(
            src_ref=c_ref,
            dst_ref=carried.at[pl.ds(origin, 1)],
            send_sem=csend.at[k],
            recv_sem=crecv.at[k],
            device_id=(basin, origin),
            device_id_type=MESH,
        ).wait_recv()
    t_ref[...] = jnp.sum(carried[...], axis=0, keepdims=True)

    @pl.when(has_target)
    def _():
        data.wait_send()

    @pl.when(has_source)
    def _():
        data.wait_recv()

    @pl.when(jnp.logical_not(has_source))
    def _():
        o_ref[...] = jnp.zeros(o_ref.shape, o_ref.dtype)


def tm_shift(x, carry, by, ident):
    nt = lax.axis_size("tm")
    c = as_row(carry)
    out, summed = pl.pallas_call(
        functools.partial(_shift_body, nt=nt, by=by),
        out_shape=(
            jax.ShapeDtypeStruct(x.shape, jnp.float32),
            jax.ShapeDtypeStruct((1, LANES), jnp.float32),
        ),
        in_specs=[pl.BlockSpec(memory_space=pltpu.VMEM)] * 2,
        out_specs=(pl.BlockSpec(memory_space=pltpu.VMEM),) * 2,
        scratch_shapes=[
            pltpu.VMEM((nt, LANES), jnp.float32),
            pltpu.SemaphoreType.DMA(()),
            pltpu.SemaphoreType.DMA(()),
            pltpu.SemaphoreType.DMA(()),
            pltpu.SemaphoreType.DMA((nt,)),
            pltpu.SemaphoreType.DMA((nt,)),
        ],
        compiler_params=pltpu.CompilerParams(collective_id=ident, has_side_effects=True),
    )(x, c)
    return out, summed


def shards(incidence, row_gauge, gauge_kernel, kernels, observed, first_guess):
    weights = incidence.astype(jnp.float32)
    blocks, slots, width = weights.shape
    gauges_here, hours = observed.shape
    owners = lax.axis_size("basin")
    classes = kernels.shape[0]
    partials = blocks * slots
    outer = jnp.arange(2 * hours)[:, None]
    inner = jnp.arange(hours)[None, :]
    table_fwd = lag_table(kernels, inner + hours - outer)
    table_bwd = lag_table(kernels, outer - inner)
    selector = (gauge_kernel[:, None] == jnp.arange(classes)[None, :]).astype(jnp.float32)

    owner = row_gauge // gauges_here
    local = row_gauge % gauges_here
    hit = owner[:, None] == jnp.arange(owners)[None, :]
    rank = jnp.cumsum(hit.astype(jnp.int32), axis=0) - 1
    dest = owner * CAP + jnp.sum(jnp.where(hit, rank, 0), axis=1)
    entries = owners * CAP
    place = (jnp.arange(entries)[:, None] == dest[None, :]).astype(jnp.float32)
    sent_ids = jnp.full((entries,), -1, jnp.int32).at[dest].set(local)
    id_rows = jnp.zeros((owners, 8, hours), jnp.float32)
    id_rows = id_rows.at[:, 0, :CAP].set(sent_ids.reshape(owners, CAP).astype(jnp.float32))
    routing = {}

    def forward(field, carry=None):
        partial_value = jnp.einsum(
            "bjr,brt->bjt", weights, field.reshape(blocks, width, hours), precision=HIGH
        )
        outgoing = jnp.dot(place, partial_value.reshape(partials, hours), precision=HIGH)
        if "gather" not in routing:
            packed = jnp.concatenate([outgoing.reshape(owners, CAP, hours), id_rows], axis=1)
            landed, basin_sq = basin_exchange(packed.reshape(owners * (CAP + 8), hours), carry, 5)
            landed = landed.reshape(owners, CAP + 8, hours)
            got_ids = landed[:, CAP, :CAP].astype(jnp.int32).reshape(entries)
            routing["gather"] = (jnp.arange(gauges_here)[:, None] == got_ids[None, :]).astype(jnp.float32)
            incoming = landed[:, :CAP, :].reshape(entries, hours)
        else:
            incoming, basin_sq = basin_exchange(outgoing, squared_row(field))
        gather = routing["gather"]
        sums = jnp.dot(gather, incoming, precision=HIGH)
        earlier, total_sq = tm_shift(sums, basin_sq, 1, 2)
        return class_mix(jnp.concatenate([earlier, sums], axis=1), table_fwd, selector), jnp.sum(total_sq)

    def backward(series):
        later, tm_sq = tm_shift(series, squared_row(series), -1, 3)
        upstream = class_mix(jnp.concatenate([series, later], axis=1), table_bwd, selector)
        outgoing = jnp.dot(routing["gather"].T, upstream, precision=lax.Precision.HIGH)
        incoming, total_sq = basin_exchange(outgoing, tm_sq)
        rows = jnp.dot(place.T, incoming, precision=lax.Precision.HIGH)
        spread = jnp.einsum(
            "bjr,bjt->brt", weights, rows.reshape(blocks, slots, hours), precision=lax.Precision.HIGH
        )
        return spread.reshape(blocks * width, hours), jnp.sum(total_sq)

    start = observed - forward(first_guess, jnp.zeros((1, LANES), jnp.float32))[0]
    pulled_start, beta_sq = backward(start)
    beta = jnp.sqrt(beta_sq)
    u = start / beta
    pulled = pulled_start / beta
    forward_pulled, alpha_sq = forward(pulled)
    alpha = jnp.sqrt(alpha_sq)
    v = pulled / alpha
    w = v
    estimate = first_guess
    phibar = beta
    rhobar = alpha
    for step in range(ITERS):
        final = step == ITERS - 1
        p = forward_pulled / alpha - alpha * u
        if final:
            beta = jnp.sqrt(global_total(squared_row(p)))
        else:
            pulled_p, beta_sq = backward(p)
            beta = jnp.sqrt(beta_sq)
            pulled = pulled_p / beta - beta * v
            forward_pulled, alpha_next = forward(pulled)
            alpha_next = jnp.sqrt(alpha_next)
            v_next = pulled / alpha_next
        u = p / beta
        rho = jnp.sqrt(rhobar * rhobar + beta * beta)
        cosine = rhobar / rho
        sine = beta / rho
        phi = cosine * phibar
        phibar = sine * phibar
        estimate = estimate + phi / rho * w
        if not final:
            theta = sine * alpha_next
            rhobar = -cosine * alpha_next
            w = v_next - theta / rho * w
            v = v_next
            alpha = alpha_next
    return estimate


def solution(mesh):
    in_specs = (
        P("basin", None, None),
        P("basin"),
        P("basin"),
        P(),
        P("basin", "tm"),
        P("basin", "tm"),
    )
    out_specs = P("basin", "tm")
    return jax.shard_map(shards, mesh=mesh, in_specs=in_specs, out_specs=out_specs, check_vma=False)
```
